32 devices in a mesh: sec: 4 (over y, x), blk: 4 (over z), case: 2 (over core).
Axes of the slice: x: 2, y: 2, z: 4, core: 2. Of those that a mesh axis runs over, the one named last changes fastest.
Arguments:
- vertex_costate: float32 [512, 128, 128], P(('sec', 'blk'), 'case'), may hold values from -6 to 6
- inverter_costate: float32 [512, 128, 128], P(('sec', 'blk'), 'case'), may hold values from -6 to 6
- highvoltage_costate: float32 [128, 4096], P('case', ('sec', 'blk')), may hold values from -6 to 6
- derivative_tiles: bfloat16 [3072, 128, 128], P(('sec', 'blk', 'case')), may hold values from -0.25 to 0.25
- tile_source_index: int32 [3072], P(('sec', 'blk', 'case')), may hold values from 0 to 31
- tile_target_index: int32 [3072], P(('sec', 'blk', 'case')), may hold values from 0 to 47
- inverter_decay_factor: float32 [512, 128], P(('sec', 'blk')), may hold values from 0.05 to 0.95
- costate_to_inverter_factor: float32 [512, 128], P(('sec', 'blk')), may hold values from 0.2 to 1
- inverter_to_costate_factor: float32 [512, 128], P(('sec', 'blk')), may hold values from -1 to 1
- distribution_entry_vertex: int32 [2048], P(('sec', 'blk')), may hold values from 0 to 4095
- distribution_entry_holder: int32 [2048, 1], P(('sec', 'blk')), may hold values from 0 to 15; in each aligned block of 128 rows (0 to 127, 128 to 255, ...) at most 16 rows name the same one
- distribution_entry_substation: int32 [2048], P(('sec', 'blk')), may hold values from 0 to 255
- highvoltage_derivative_matrix: bfloat16 [4096, 256], P(('sec', 'blk')), may hold values from -0.375 to 0.375
Outputs:
- adjoint_out: float32 [512, 128, 128], P(('sec', 'blk'), 'case')
- droop_out: float32 [512, 128, 128], P(('sec', 'blk'), 'case')
- trans_out: float32 [128, 4096], P('case', ('sec', 'blk'))
The draws below stay inside these ranges and needn't reach their ends.
Inputs may be any that keep to these rules, and one draw needn't show every extreme that they name: `distribution_entry_holder`: in each aligned block of 128 rows (the feeder heads of one network device) no owner is named by more than 16 rows, a bound that some block reaches.
All inputs are finite; a program needn't handle non-finite values.
Results may differ from the reference program's by a relative error of at most 0.0047.
Values may be sent and summed in bfloat16 or wider, within the bound.
No kernel may reach another device: no remote copies, remote signals or barrier semaphores. Data moves between devices by JAX's collectives and lax.ppermute only.
A program may use at most 64 MiB of HBM per device.

```python
import math
import jax
import jax.numpy as jnp
import numpy as np
from jax import lax

NB_DEV = 32
SUBGRID_VERTICES = 128
S_DEV = 128
TBUS = 256
STEPS = 3
RIM = 16
E_DEV = 192
CAP = 16
SCENARIO_COUNT = 128
GRID_PARTITIONS = 512
NBUS = 4096
N_SEC = 4
N_BLK = 4


def place_ends(values, rng, low, top_value):
    longest = values.shape.index(max(values.shape))
    spots = []
    for shift in (0, 1):
        where = [jax.random.randint(jax.random.fold_in(rng, axis), (), 0, length) for axis, length in enumerate(values.shape)]
        where[longest] = (where[longest] + shift) % values.shape[longest]
        spots.append(tuple(where))
    return values.at[spots[0]].set(low).at[spots[1]].set(top_value)


def levels(own_key, dims, split, low, high):
    def one(position, shards_of):
        heights = jax.random.uniform(jax.random.fold_in(jax.random.fold_in(own_key, 6), position), (shards_of,), jnp.float32, low / len(split), high / len(split))
        return jnp.repeat(jnp.exp(heights), dims[position] // shards_of).reshape((-1,) + (1,) * (len(dims) - position - 1))

    factor_of = one(*split[0])
    for cut in split[1:]:
        factor_of = factor_of * one(*cut)
    return factor_of


def assign_block(own_key, own, number, rows, amount, top, most, lean):
    ranking = jax.random.permutation(own_key, amount)
    crowded, ordinary = shares(amount, rows * top, most, lean, True), shares(amount, rows * top, most, lean, False)
    places = jnp.arange(amount)

    def named(sizes, turn):
        used = int((sizes > 0).sum())
        fixed = max(1, used // 4)
        shifted = fixed + (places - fixed + turn * (used - fixed)) % max(1, amount - fixed)
        return jnp.zeros((amount,), jnp.int32).at[ranking[jnp.where(places < fixed, places, shifted)]].set(jnp.asarray(sizes, jnp.int32))

    sizes = jnp.where(number % 4 == 0, named(crowded, number // 4), named(ordinary, number - number // 4 - 1))
    mixed = jax.random.permutation(jax.random.fold_in(own, 3), amount)
    giver, taker = mixed[0:amount // 2 * 2:2], mixed[1:amount // 2 * 2:2]
    room = jnp.minimum(sizes[giver] - 1, most - sizes[taker]) // 2
    room = jnp.where((giver == ranking[0]) | (taker == ranking[0]) | (sizes[taker] == 0), 0, jnp.maximum(room, 0))
    shifted = jax.random.randint(jax.random.fold_in(own, 4), (amount // 2,), 0, 1 << 20) % (room + 1)
    sizes = sizes.at[giver].add(-shifted).at[taker].add(shifted)
    members = jnp.searchsorted(jnp.cumsum(sizes), jnp.arange(rows * top), side="right").astype(jnp.int32)
    listing = members.reshape(top, rows).T
    listing = listing[jax.random.permutation(jax.random.fold_in(own, 1), rows)]
    turn = jax.random.randint(jax.random.fold_in(own, 2), (rows, 1), 0, top)
    return jnp.take_along_axis(listing, (jnp.arange(top)[None, :] + turn) % top, axis=1)


def shares(amount, total, reach, lean, full):
    weights = [(1 << 20) // math.isqrt(standing ** lean) + 1 for standing in range(1, amount + 1)]
    largest = reach if full else min(reach, max(-(-total // amount), total * weights[0] // sum(weights)))
    least = 1 if total - largest >= amount - 1 else 0
    given, rest = [largest] + [least] * (amount - 1), total - largest - least * (amount - 1)
    while rest > 0:
        movable = [i for i in range(1, amount) if given[i] < largest] or [i for i in range(1, amount) if given[i] < reach]
        whole, left = sum([weights[i] for i in movable]), rest
        for i in movable:
            addition = min(reach - given[i], max(1, left * weights[i] // whole), rest)
            given[i] = given[i] + addition
            rest = rest - addition
    return np.array(given)


def gaussian(key, extent, deviation, bound, shards=(), held_as=jnp.bfloat16):
    entries = deviation * jax.random.normal(key, extent, jnp.float32)
    if shards:
        entries = entries * levels(key, extent, shards, -0.22, 0.18)
    return jnp.clip(entries, -bound, bound).astype(held_as)


def setup_inputs(seed: int = 0) -> dict:
    seeds = jax.random.split(jax.random.key(seed), 14)
    vertex_costate = gaussian(seeds[0], (GRID_PARTITIONS, SCENARIO_COUNT, SUBGRID_VERTICES), 1.0, 6.0, ((0, 16), (1, 2)), jnp.float32)
    inverter_costate = gaussian(seeds[1], (GRID_PARTITIONS, SCENARIO_COUNT, SUBGRID_VERTICES), 1.0, 6.0, ((0, 16), (1, 2)), jnp.float32)
    highvoltage_costate = gaussian(seeds[2], (SCENARIO_COUNT, NBUS), 1.0, 6.0, ((0, 2), (1, 16)), jnp.float32)
    derivative_tiles = gaussian(seeds[3], (E_DEV * N_SEC * N_BLK, SUBGRID_VERTICES, SUBGRID_VERTICES), (SUBGRID_VERTICES * E_DEV // (NB_DEV + RIM)) ** -0.5, 0.25, ((0, 32),))
    tile_source_index = place_ends(jax.random.randint(seeds[4], (E_DEV * N_SEC * N_BLK,), 0, NB_DEV), jax.random.fold_in(seeds[4], 1), 0, NB_DEV - 1).astype(jnp.int32)
    tile_target_index = place_ends(jax.random.randint(seeds[5], (E_DEV * N_SEC * N_BLK,), 0, NB_DEV + RIM), jax.random.fold_in(seeds[5], 1), 0, (NB_DEV + RIM) - 1).astype(jnp.int32)
    inverter_decay_factor = jnp.clip(jnp.exp(math.log(0.95) - 2.944439 * jax.random.uniform(seeds[6], (GRID_PARTITIONS, SUBGRID_VERTICES), jnp.float32) ** levels(seeds[6], (GRID_PARTITIONS, SUBGRID_VERTICES), ((0, 16),), -0.2, 0.2)), 0.05, 0.95)
    costate_to_inverter_factor = jnp.clip(0.2 + 0.8 * jax.random.uniform(seeds[7], (GRID_PARTITIONS, SUBGRID_VERTICES), jnp.float32) ** levels(seeds[7], (GRID_PARTITIONS, SUBGRID_VERTICES), ((0, 16),), -0.2, 0.2), 0.2, 1.0)
    inverter_to_costate_factor = jnp.clip(jax.random.uniform(seeds[8], (GRID_PARTITIONS, SUBGRID_VERTICES), jnp.float32, -1.0, 1.0) * levels(seeds[8], (GRID_PARTITIONS, SUBGRID_VERTICES), ((0, 16),), -0.4, 0.0), -1.0, 1.0)
    distribution_entry_vertex = place_ends(jax.random.randint(seeds[9], (S_DEV * N_SEC * N_BLK,), 0, NB_DEV * SUBGRID_VERTICES), jax.random.fold_in(seeds[9], 1), 0, (NB_DEV * SUBGRID_VERTICES) - 1).astype(jnp.int32)
    distribution_entry_holder_keys = jax.random.split(jax.random.fold_in(seeds[10], 1), (S_DEV * N_SEC * N_BLK) // S_DEV)
    distribution_entry_holder_turns = jax.random.permutation(jax.random.fold_in(seeds[10], 3), (S_DEV * N_SEC * N_BLK) // S_DEV)
    distribution_entry_holder = jax.vmap(lambda own, number: assign_block(jax.random.fold_in(seeds[10], 2), own, number, S_DEV, N_SEC * N_BLK, 1, CAP, 2))(distribution_entry_holder_keys, distribution_entry_holder_turns).reshape((S_DEV * N_SEC * N_BLK, 1))
    distribution_entry_substation = place_ends(jax.random.randint(seeds[11], (S_DEV * N_SEC * N_BLK,), 0, TBUS), jax.random.fold_in(seeds[11], 1), 0, TBUS - 1).astype(jnp.int32)
    highvoltage_derivative_matrix = gaussian(seeds[12], (NBUS, TBUS), TBUS ** -0.5, 0.375, ((0, 16),))
    return dict(vertex_costate=vertex_costate, inverter_costate=inverter_costate, highvoltage_costate=highvoltage_costate, derivative_tiles=derivative_tiles, tile_source_index=tile_source_index, tile_target_index=tile_target_index, inverter_decay_factor=inverter_decay_factor, costate_to_inverter_factor=costate_to_inverter_factor, inverter_to_costate_factor=inverter_to_costate_factor, distribution_entry_vertex=distribution_entry_vertex, distribution_entry_holder=distribution_entry_holder, distribution_entry_substation=distribution_entry_substation, highvoltage_derivative_matrix=highvoltage_derivative_matrix)


def reference(vertex_costate, inverter_costate, highvoltage_costate, derivative_tiles, tile_source_index, tile_target_index, inverter_decay_factor, costate_to_inverter_factor, inverter_to_costate_factor, distribution_entry_vertex, distribution_entry_holder, distribution_entry_substation, highvoltage_derivative_matrix):
    network = N_SEC * N_BLK
    lam = vertex_costate
    iteration_carry = inverter_costate
    trans = highvoltage_costate
    decay_triple = inverter_decay_factor[:, None, :]
    inflow_factor = costate_to_inverter_factor[:, None, :]
    outflow_factor = inverter_to_costate_factor[:, None, :]
    head_dev = jnp.arange(network * S_DEV, dtype=jnp.int32) // S_DEV
    head_block = head_dev * NB_DEV + distribution_entry_vertex // SUBGRID_VERTICES
    head_pos = distribution_entry_vertex % SUBGRID_VERTICES
    target = distribution_entry_holder[:, 0] * TBUS + distribution_entry_substation
    tj_whole = highvoltage_derivative_matrix.astype(jnp.float32).reshape(network, TBUS, TBUS)
    for step in range(STEPS):
        lam_bf = lam.astype(jnp.bfloat16)

        def device_term(carry, device):
            first = device * E_DEV
            row_ids = lax.dynamic_slice_in_dim(tile_source_index, first, E_DEV) + device * NB_DEV
            col_ids = lax.dynamic_slice_in_dim(tile_target_index, first, E_DEV)
            mats = lax.dynamic_slice_in_dim(derivative_tiles, first, E_DEV, 0).astype(jnp.float32)
            picked = jnp.take(lam_bf, row_ids, axis=0).astype(jnp.float32)
            prods = jnp.einsum('ecn,enm->ecm', picked, mats, precision=lax.Precision.HIGHEST)
            partial_sum = jax.ops.segment_sum(prods, col_ids, num_segments=NB_DEV + RIM)
            start = (device * NB_DEV).astype(jnp.int32)
            current = lax.dynamic_slice_in_dim(carry, start, NB_DEV, 0)
            carry = lax.dynamic_update_slice_in_dim(carry, current + partial_sum[:NB_DEV], start, 0)
            keep = ((device % N_BLK) < N_BLK - 1).astype(jnp.float32)
            following = (jnp.minimum(device + 1, network - 1) * NB_DEV).astype(jnp.int32)
            ahead = lax.dynamic_slice_in_dim(carry, following, RIM, 0)
            carry = lax.dynamic_update_slice_in_dim(carry, ahead + keep * partial_sum[NB_DEV:], following, 0)
            return carry, None

        summed, unused = lax.scan(device_term, jnp.zeros(lam.shape, jnp.float32), jnp.arange(network, dtype=jnp.int32))
        head_vals = lam[head_block, :, head_pos]
        inj = jax.ops.segment_sum(head_vals, target, num_segments=network * TBUS).T
        tlam_bf = trans.astype(jnp.bfloat16).astype(jnp.float32).reshape(SCENARIO_COUNT, network, TBUS)
        trans_next = jnp.einsum('cdt,dts->cds', tlam_bf, tj_whole, precision=lax.Precision.HIGHEST).reshape(SCENARIO_COUNT, network * TBUS) + inj
        state_next = decay_triple * iteration_carry + inflow_factor * lam
        lam_next = summed + outflow_factor * iteration_carry
        lam, iteration_carry, trans = lam_next, state_next, trans_next
    return (lam, iteration_carry, trans)
```

```python
import jax
import jax.numpy as jnp
from jax import lax
from jax.experimental import pallas as pl
from jax.experimental.pallas import tpu as pltpu
from jax.sharding import PartitionSpec as P

STEPS = 3
UNROLL = 16
CLASSES = 4
VMEM_LIMIT = 24 << 20

F32 = jnp.float32
BF16 = jnp.bfloat16
VM = pl.BlockSpec(memory_space=pltpu.VMEM)
SM = pl.BlockSpec(memory_space=pltpu.SMEM)


def kernel(body, outs, ins, name, scratch=(), out_specs=None):
    return pl.pallas_call(
        body,
        out_shape=outs,
        in_specs=[spec for _, spec in ins],
        out_specs=out_specs or tuple(VM for _ in outs),
        scratch_shapes=list(scratch),
        compiler_params=pltpu.CompilerParams(vmem_limit_bytes=VMEM_LIMIT),
        name=name,
    )(*[array for array, _ in ins])


def array(shape, dtype):
    return jax.ShapeDtypeStruct(shape, dtype)


def heads_of(lam, vertex, heads, cases, nodes):
    lane = lax.broadcasted_iota(jnp.int32, (cases, nodes), 1)

    def pick(s, kept):
        where = vertex[s]
        row = lam[where // nodes]
        turned = pltpu.roll(row, lax.rem(s - lax.rem(where, nodes) + nodes, nodes), 1)
        return jnp.where(lane == s, turned, kept)

    return lax.fori_loop(0, heads, pick, jnp.zeros((cases, nodes), F32), unroll=8)


def local(
    vertex_costate,
    inverter_costate,
    highvoltage_costate,
    derivative_tiles,
    tile_source_index,
    tile_target_index,
    inverter_decay_factor,
    costate_to_inverter_factor,
    inverter_to_costate_factor,
    distribution_entry_vertex,
    distribution_entry_holder,
    distribution_entry_substation,
    highvoltage_derivative_matrix,
):
    blocks, cases, nodes = vertex_costate.shape
    rim = blocks // 2
    low = blocks // 2
    targets = blocks + rim
    stored = derivative_tiles.shape[0]
    sections = lax.axis_size("sec")
    owners = lax.axis_size("blk")
    network = sections * owners
    heads = distribution_entry_vertex.shape[0]
    slots = max(2, 2 * heads // network)
    buses = highvoltage_derivative_matrix.shape[1]
    span = stored + UNROLL
    rows_sent = network * 2 * slots

    state = (blocks, cases, nodes)
    half = (low, cases, nodes)
    padded = (low + 1, cases, nodes)
    swap = [(0, 1), (1, 0)]
    onward = [(i, (i + 1) % owners) for i in range(owners)]

    own_codes = tile_source_index | (tile_target_index << 8)
    other_codes = lax.ppermute(own_codes, "case", swap)
    own = derivative_tiles
    other = lax.ppermute(own, "case", swap)
    follows = (lax.axis_index("blk") > 0).astype(jnp.int32).reshape(1)

    def run(lists, counts, segment, lam, tiles, acc):
        start = segment * span

        def some(i, carry):
            codes = [lists[start + i * UNROLL + u] for u in range(UNROLL)]
            prods = [
                jnp.dot(lam[(c >> 8) & 255], tiles[c & 255], preferred_element_type=F32)
                for c in codes
            ]
            for c, prod in zip(codes, prods):
                acc[c >> 16] += prod
            return carry

        lax.fori_loop(0, (counts[segment] + UNROLL - 1) // UNROLL, some, 0)

    def first_body(
        codes, vertex, lam, icar, tiles, decay, inflow, outflow, acc, lo, hi, icar_next, head, lam_bf
    ):
        zero = jnp.zeros((cases, nodes), BF16)
        for b in range(blocks):
            row = lam[b]
            rounded = row.astype(BF16)
            lam_bf[b] = rounded
            if b < low:
                lo[b] = rounded
            else:
                hi[b - low] = rounded
            kept = icar[b]
            acc[b] = outflow[b : b + 1, :] * kept
            icar_next[b] = decay[b : b + 1, :] * kept + inflow[b : b + 1, :] * row
        lo[low] = zero
        hi[blocks - low] = zero
        for b in range(rim):
            acc[blocks + b] = jnp.zeros((cases, nodes), F32)

        def some(i, carry):
            codes_here = [codes[i * UNROLL + u] for u in range(UNROLL)]
            prods = [
                jnp.dot(lam_bf[c & 255], tiles[i * UNROLL + u], preferred_element_type=F32)
                for u, c in enumerate(codes_here)
            ]
            for c, prod in zip(codes_here, prods):
                acc[c >> 8] += prod
            return carry

        lax.fori_loop(0, stored // UNROLL, some, 0)
        head[...] = heads_of(lam, vertex, heads, cases, nodes).astype(BF16)

    acc, lo, hi, icar, head0 = kernel(
        first_body,
        (
            array((targets, cases, nodes), F32),
            array(padded, BF16),
            array(padded, BF16),
            array(state, F32),
            array((cases, heads), BF16),
        ),
        [
            (own_codes, SM),
            (distribution_entry_vertex, SM),
            (vertex_costate, VM),
            (inverter_costate, VM),
            (own, VM),
            (inverter_decay_factor, VM),
            (costate_to_inverter_factor, VM),
            (inverter_to_costate_factor, VM),
        ],
        "first",
        scratch=[pltpu.VMEM(state, BF16)],
    )

    def sort_body(own_code, other_code, lists, counts):
        for side, code in enumerate((own_code, other_code)):

            def place(e, used, code=code, side=side):
                c = code[e]
                row = c & 255
                target = c >> 8
                is_low = (row < low).astype(jnp.int32)
                is_own = (target < blocks).astype(jnp.int32)
                kind = 2 * is_own + is_low
                at = (used >> (8 * kind)) & 255
                lists[(side * CLASSES + kind) * span + at] = (
                    e | ((row - low * (1 - is_low)) << 8) | ((target - blocks * (1 - is_own)) << 16)
                )
                return used + (1 << (8 * kind))

            used = lax.fori_loop(0, stored, place, jnp.int32(0), unroll=8)
            for kind in range(CLASSES):
                at = (used >> (8 * kind)) & 255
                counts[side * CLASSES + kind] = at
                for u in range(UNROLL):
                    lists[(side * CLASSES + kind) * span + at + u] = low << 8

    lists, counts = kernel(
        sort_body,
        (array((2 * CLASSES * span,), jnp.int32), array((2 * CLASSES,), jnp.int32)),
        [(own_codes, SM), (other_codes, SM)],
        "sort",
        out_specs=(SM, SM),
    )

    def rim_first_body(lists, counts, acc, lo, hi, other, out, sums):
        sums[...] = acc[blocks:]
        run(lists, counts, CLASSES + 0, hi, other, sums)
        run(lists, counts, CLASSES + 1, lo, other, sums)
        out[...] = sums[...].astype(BF16)

    (leaving,) = kernel(
        rim_first_body,
        (array((rim, cases, nodes), BF16),),
        [(lists, SM), (counts, SM), (acc, VM), (lo, VM), (hi, VM), (other, VM)],
        "rim_first",
        scratch=[pltpu.VMEM((rim, cases, nodes), F32)],
    )

    def begin_next(lists, counts, lam, icar, outflow, own, other, acc, hi):
        for b in range(blocks):
            acc[b] = outflow[b : b + 1, :] * icar[b]
        for b in range(rim):
            acc[blocks + b] = jnp.zeros((cases, nodes), F32)
        for b in range(low, blocks):
            hi[b - low] = lam[b].astype(BF16)
        hi[blocks - low] = jnp.zeros((cases, nodes), BF16)
        for side, tiles in enumerate((own, other)):
            run(lists, counts, side * CLASSES + 0, hi, tiles, acc.at[pl.ds(blocks, rim)])
            run(lists, counts, side * CLASSES + 2, hi, tiles, acc)

    def main_first_body(
        lists, counts, acc, lo, hi, icar, own, other, outflow, lam_next, acc_next, hi_next
    ):
        lam_next[...] = acc[:blocks]
        run(lists, counts, CLASSES + 2, hi, other, lam_next)
        run(lists, counts, CLASSES + 3, lo, other, lam_next)
        begin_next(lists, counts, lam_next, icar, outflow, own, other, acc_next, hi_next)

    def rim_body(lists, counts, follows, arrived, lam, acc, own, other, out, full, lo, sums):
        keep = follows[0] > 0
        for b in range(low):
            came = jnp.where(keep, arrived[b].astype(F32), 0.0)
            row = lam[b] + came
            full[b] = row
            lo[b] = row.astype(BF16)
        lo[low] = jnp.zeros((cases, nodes), BF16)
        sums[...] = acc[blocks:]
        run(lists, counts, 1, lo, own, sums)
        run(lists, counts, CLASSES + 1, lo, other, sums)
        out[...] = sums[...].astype(BF16)
        full[low:] = lam[low:]

    def finish_step(lists, counts, lam, lo, acc, icar, decay, inflow, own, other, lam_next, icar_next):
        lam_next[...] = acc[:blocks]
        run(lists, counts, 3, lo, own, lam_next)
        run(lists, counts, CLASSES + 3, lo, other, lam_next)
        for b in range(blocks):
            icar_next[b] = decay[b : b + 1, :] * icar[b] + inflow[b : b + 1, :] * lam[b]

    def main_body(
        lists, counts, vertex, lam, lo, acc, icar, own, other, decay, inflow, outflow,
        lam_next, acc_next, hi_next, icar_next, head,
    ):
        finish_step(
            lists, counts, lam, lo, acc, icar, decay, inflow, own, other, lam_next, icar_next
        )
        begin_next(lists, counts, lam_next, icar_next, outflow, own, other, acc_next, hi_next)
        head[...] = heads_of(lam, vertex, heads, cases, nodes).astype(BF16)

    def main_last_body(
        lists, counts, lam, lo, acc, icar, own, other, decay, inflow, lam_next, icar_next
    ):
        finish_step(
            lists, counts, lam, lo, acc, icar, decay, inflow, own, other, lam_next, icar_next
        )

    def pack_body(vertex, owner_col, owner_row, bus_row, lam, head0, head1, out):
        head2 = heads_of(lam, vertex, heads, cases, nodes)
        before = lax.broadcasted_iota(jnp.int32, (heads, heads), 0)
        after = lax.broadcasted_iota(jnp.int32, (heads, heads), 1)
        same = jnp.logical_and(owner_col[...] == owner_row[...], before < after)
        slot = jnp.sum(same.astype(jnp.int32), axis=0, keepdims=True)
        dest = owner_row[...] * (2 * slots) + slot
        row = lax.broadcasted_iota(jnp.int32, (rows_sent, heads), 0)
        place_a = (row == dest).astype(F32).astype(BF16)
        place_b = (row == dest + slots).astype(F32).astype(BF16)
        bus = jnp.broadcast_to((bus_row[...] + 1).astype(F32), (nodes - cases, heads))
        pair_a = jnp.concatenate([head0[...], head1[...]], axis=0)
        pair_b = jnp.concatenate([head2, bus], axis=0).astype(BF16)
        dims = (((1,), (1,)), ((), ()))
        sent = lax.dot_general(place_a, pair_a, dims, preferred_element_type=F32)
        sent += lax.dot_general(place_b, pair_b, dims, preferred_element_type=F32)
        out[...] = sent.astype(BF16)

    def trans_body(received, trans, matrix, out):
        got = received[...].astype(F32)
        row = lax.broadcasted_iota(jnp.int32, (rows_sent, buses), 0)
        second = lax.rem(row, 2 * slots) >= slots
        column = lax.broadcasted_iota(jnp.int32, (rows_sent, buses), 1)
        label = got[:, cases : cases + 1].astype(jnp.int32) - 1
        hot_b = jnp.where(jnp.logical_and(label == column, second), 1.0, 0.0)
        hot_a = pltpu.roll(hot_b, rows_sent - slots, 0)
        dims = (((0,), (0,)), ((), ()))
        first = lax.dot_general(received[...], hot_a.astype(BF16), dims, preferred_element_type=F32)
        last = lax.dot_general(received[...], hot_b.astype(BF16), dims, preferred_element_type=F32)
        value = trans[...]
        for inj in (first[:cases], first[cases:], last[:cases]):
            value = jnp.dot(value.astype(BF16), matrix[...], preferred_element_type=F32) + inj
        out[...] = value

    def last_body(follows, arrived, lam, out):
        keep = follows[0] > 0
        for b in range(low):
            out[b] = lam[b] + jnp.where(keep, arrived[b].astype(F32), 0.0)

    listed = [(lists, SM), (counts, SM)]
    tiles = [(own, VM), (other, VM)]
    factors = [(inverter_decay_factor, VM), (costate_to_inverter_factor, VM)]
    outflow = (inverter_to_costate_factor, VM)
    acc_type = array((targets, cases, nodes), F32)

    arriving = lax.ppermute(leaving, "blk", onward)
    lam, acc, hi = kernel(
        main_first_body,
        (array(state, F32), acc_type, array(padded, BF16)),
        listed + [(acc, VM), (lo, VM), (hi, VM), (icar, VM)] + tiles + [outflow],
        "main_first",
    )
    for step in range(1, STEPS):
        leaving, full, lo = kernel(
            rim_body,
            (array((rim, cases, nodes), BF16), array(state, F32), array(padded, BF16)),
            listed + [(follows, SM), (arriving, VM), (lam, VM), (acc, VM)] + tiles,
            "rim",
            scratch=[pltpu.VMEM((rim, cases, nodes), F32)],
        )
        arriving = lax.ppermute(leaving, "blk", onward)
        if step < STEPS - 1:
            lam, acc, hi, icar, head1 = kernel(
                main_body,
                (
                    array(state, F32),
                    acc_type,
                    array(padded, BF16),
                    array(state, F32),
                    array((cases, heads), BF16),
                ),
                listed
                + [(distribution_entry_vertex, SM), (full, VM), (lo, VM), (acc, VM), (icar, VM)]
                + tiles
                + factors
                + [outflow],
                "main",
            )
        else:
            (sent,) = kernel(
                pack_body,
                (array((rows_sent, nodes), BF16),),
                [
                    (distribution_entry_vertex, SM),
                    (distribution_entry_holder, VM),
                    (distribution_entry_holder.reshape(1, heads), VM),
                    (distribution_entry_substation.reshape(1, heads), VM),
                    (full, VM),
                    (head0, VM),
                    (head1, VM),
                ],
                "pack",
            )
            received = lax.all_to_all(
                sent.reshape(network, 2 * slots, nodes),
                ("sec", "blk"),
                split_axis=0,
                concat_axis=0,
                tiled=True,
            ).reshape(rows_sent, nodes)
            lam, icar = kernel(
                main_last_body,
                (array(state, F32), array(state, F32)),
                listed + [(full, VM), (lo, VM), (acc, VM), (icar, VM)] + tiles + factors,
                "main_last",
            )
    (trans,) = kernel(
        trans_body,
        (array(highvoltage_costate.shape, F32),),
        [(received, VM), (highvoltage_costate, VM), (highvoltage_derivative_matrix, VM)],
        "trans",
    )
    lower = pl.BlockSpec(half, lambda i: (0, 0, 0))
    lam = pl.pallas_call(
        last_body,
        grid=(1,),
        out_shape=array(state, F32),
        in_specs=[SM, lower, lower],
        out_specs=lower,
        input_output_aliases={2: 0},
        name="last",
    )(follows, arriving, lam)
    return (lam, icar, trans)


def solution(mesh):
    placed = (
        P(("sec", "blk"), "case", None),
        P(("sec", "blk"), "case", None),
        P("case", ("sec", "blk")),
        P(("sec", "blk", "case"), None, None),
        P(("sec", "blk", "case")),
        P(("sec", "blk", "case")),
        P(("sec", "blk"), None),
        P(("sec", "blk"), None),
        P(("sec", "blk"), None),
        P(("sec", "blk")),
        P(("sec", "blk"), None),
        P(("sec", "blk")),
        P(("sec", "blk"), None),
    )
    return jax.shard_map(
        local,
        mesh=mesh,
        in_specs=placed,
        out_specs=(
            P(("sec", "blk"), "case", None),
            P(("sec", "blk"), "case", None),
            P("case", ("sec", "blk")),
        ),
        check_vma=False,
    )
```

```python
import jax
import jax.numpy as jnp
from jax import lax
from jax.experimental import pallas as pl
from jax.experimental.pallas import tpu as pltpu
from jax.sharding import PartitionSpec as P

STEPS = 3
UNROLL = 16
CLASSES = 4
VMEM_LIMIT = 24 << 20

F32 = jnp.float32
BF16 = jnp.bfloat16
VM = pl.BlockSpec(memory_space=pltpu.VMEM)
SM = pl.BlockSpec(memory_space=pltpu.SMEM)
HB = pl.BlockSpec(memory_space=pltpu.HBM)
STRIDE = 128


def kernel(body, outs, ins, name, scratch=(), out_specs=None, aliases=None):
    return pl.pallas_call(
        body,
        out_shape=outs,
        in_specs=[spec for _, spec in ins],
        out_specs=out_specs or tuple(VM for _ in outs),
        scratch_shapes=list(scratch),
        input_output_aliases=aliases or {},
        compiler_params=pltpu.CompilerParams(vmem_limit_bytes=VMEM_LIMIT),
        name=name,
    )(*[in_hbm(array) if spec is HB else array for array, spec in ins])


def in_hbm(array):
    return pltpu.with_memory_space_constraint(array, pltpu.HBM)


def array(shape, dtype):
    return jax.ShapeDtypeStruct(shape, dtype)


def local(
    vertex_costate,
    inverter_costate,
    highvoltage_costate,
    derivative_tiles,
    tile_source_index,
    tile_target_index,
    inverter_decay_factor,
    costate_to_inverter_factor,
    inverter_to_costate_factor,
    distribution_entry_vertex,
    distribution_entry_holder,
    distribution_entry_substation,
    highvoltage_derivative_matrix,
):
    blocks, cases, nodes = vertex_costate.shape
    rim = blocks // 2
    low = blocks // 2
    targets = blocks + rim
    stored = derivative_tiles.shape[0]
    sections = lax.axis_size("sec")
    owners = lax.axis_size("blk")
    network = sections * owners
    heads = distribution_entry_vertex.shape[0]
    slots = max(2, 2 * heads // network)
    buses = highvoltage_derivative_matrix.shape[1]
    rows_sent = network * 2 * slots
    assert stored + UNROLL <= STRIDE and blocks <= 64

    state = (blocks, cases, nodes)
    half = (low, cases, nodes)
    padded = (low + 1, cases, nodes)
    acc_shape = (targets, cases, nodes)
    hot_shape = (blocks, nodes, heads)
    factor_shape = inverter_decay_factor.shape
    swap = [(0, 1), (1, 0)]
    onward = [(i, (i + 1) % owners) for i in range(owners)]

    own = derivative_tiles
    other = lax.ppermute(own, "case", swap)
    is_low = (tile_source_index < low).astype(jnp.int32)
    is_own = (tile_target_index < blocks).astype(jnp.int32)
    own_codes = (
        lax.iota(jnp.int32, stored)
        | ((tile_source_index - low * (1 - is_low)) << 8)
        | ((tile_target_index - blocks * (1 - is_own)) << 16)
        | ((16 * is_own + 8 * is_low) << 24)
    )
    other_codes = lax.ppermute(own_codes, "case", swap)

    def group(codes, lam, tiles, acc):
        prods = [
            jnp.dot(lam[(c >> 8) & 255], tiles[c & 255], preferred_element_type=F32) for c in codes
        ]
        for c, prod in zip(codes, prods):
            acc[(c >> 16) & 255] += prod

    def run(lists, counts, segment, lam, tiles, acc):
        def some(i, carry):
            start = segment * STRIDE + i * UNROLL
            group([lists[start + u] for u in range(UNROLL)], lam, tiles, acc)
            return carry

        lax.fori_loop(0, (counts[segment] + UNROLL - 1) // UNROLL, some, 0)

    def first_body(codes, lam_in, own_in, acc, lo, hi, own_kept, lam, lam_bf, sems):
        lam_copy = pltpu.make_async_copy(lam_in, lam, sems.at[0])
        lam_copy.start()
        copies = [
            pltpu.make_async_copy(
                own_in.at[pl.ds(i, UNROLL)], own_kept.at[pl.ds(i, UNROLL)], sems.at[1 + i // UNROLL]
            )
            for i in range(0, stored, UNROLL)
        ]
        for copy in copies:
            copy.start()
        for b in range(targets):
            acc[b] = jnp.zeros((cases, nodes), F32)
        zero = jnp.zeros((cases, nodes), BF16)
        lo[low] = zero
        hi[blocks - low] = zero
        lam_copy.wait()
        for b in range(blocks):
            rounded = lam[b].astype(BF16)
            lam_bf[b] = rounded
            if b < low:
                lo[b] = rounded
            else:
                hi[b - low] = rounded
        for i, copy in enumerate(copies):
            copy.wait()
            prods = []
            for u in range(UNROLL):
                c = codes[i * UNROLL + u]
                k = c >> 24
                row = ((c >> 8) & 255) + jnp.where((k & 8) > 0, 0, low)
                target = ((c >> 16) & 255) + jnp.where((k & 16) > 0, 0, blocks)
                prod = jnp.dot(
                    lam_bf[row], own_kept[i * UNROLL + u], preferred_element_type=F32
                )
                prods.append((target, prod))
            for target, prod in prods:
                acc[target] += prod

    acc, lo, hi, own = kernel(
        first_body,
        (
            array(acc_shape, F32),
            array(padded, BF16),
            array(padded, BF16),
            array(own.shape, BF16),
        ),
        [(own_codes, SM), (vertex_costate, HB), (own, HB)],
        "first",
        scratch=[
            pltpu.VMEM(state, F32),
            pltpu.VMEM(state, BF16),
            pltpu.SemaphoreType.DMA((1 + stored // UNROLL,)),
        ],
    )

    def sort_body(own_code, other_code, lists, counts):
        for side, code in enumerate((own_code, other_code)):
            base = side * CLASSES * STRIDE

            def place(e, used, code=code, base=base):
                c = code[e]
                shift = c >> 24
                lists[base + shift * (STRIDE // 8) + ((used >> shift) & 255)] = c
                return used + (1 << shift)

            used = lax.fori_loop(0, stored, place, jnp.int32(0), unroll=8)
            for kind in range(CLASSES):
                at = (used >> (8 * kind)) & 255
                counts[side * CLASSES + kind] = at
                for u in range(UNROLL):
                    lists[base + kind * STRIDE + at + u] = low << 8

    lists, counts = kernel(
        sort_body,
        (array((2 * CLASSES * STRIDE,), jnp.int32), array((2 * CLASSES,), jnp.int32)),
        [(own_codes, SM), (other_codes, SM)],
        "sort",
        out_specs=(SM, SM),
    )
    listed = [(lists, SM), (counts, SM)]

    def rim_first_body(lists, counts, acc, lo, hi, other, out, sums):
        sums[...] = acc[blocks:]
        run(lists, counts, CLASSES + 0, hi, other, sums)
        run(lists, counts, CLASSES + 1, lo, other, sums)
        out[...] = sums[...].astype(BF16)

    (leaving,) = kernel(
        rim_first_body,
        (array((rim, cases, nodes), BF16),),
        listed + [(acc, VM), (lo, VM), (hi, VM), (other, VM)],
        "rim_first",
        scratch=[pltpu.VMEM((rim, cases, nodes), F32)],
    )
    arriving = lax.ppermute(leaving, "blk", onward)

    def begin_next(lists, counts, lam, icar, outflow, own, other, acc, acc_rim, hi):
        for b in range(blocks):
            acc[b] = outflow[b : b + 1, :] * icar[b]
        for b in range(rim):
            acc_rim[b] = jnp.zeros((cases, nodes), F32)
        for b in range(low, blocks):
            hi[b - low] = lam[b].astype(BF16)
        hi[blocks - low] = jnp.zeros((cases, nodes), BF16)
        for side, tiles in enumerate((own, other)):
            run(lists, counts, side * CLASSES + 0, hi, tiles, acc_rim)
            run(lists, counts, side * CLASSES + 2, hi, tiles, acc)

    def head_values(lo, hi, hot):
        total = jnp.dot(lo[0], hot[0], preferred_element_type=F32)
        for b in range(1, blocks):
            row = lo[b] if b < low else hi[b - low]
            total += jnp.dot(row, hot[b], preferred_element_type=F32)
        return total.astype(BF16)

    def main_first_body(
        lists, counts, acc, lo, hi, own, other, vertex, lam_in, icar_in, decay_in, inflow_in, outflow_in,
        lam_next, acc_next, acc_rim, hi_next, icar_next, head, hot, decay, inflow, outflow, other_kept,
        lam, icar, sems,
    ):
        kept = pltpu.make_async_copy(other, other_kept, sems.at[5])
        kept.start()
        pairs = [
            (icar_in, icar), (outflow_in, outflow), (lam_in, lam), (decay_in, decay), (inflow_in, inflow)
        ]
        copies = [pltpu.make_async_copy(a, b, sems.at[i]) for i, (a, b) in enumerate(pairs)]
        for copy in copies:
            copy.start()
        for copy in copies:
            copy.wait()
        for b in range(blocks):
            lam_next[b] = acc[b] + outflow[b : b + 1, :] * icar[b]
            icar_next[b] = decay[b : b + 1, :] * icar[b] + inflow[b : b + 1, :] * lam[b]
        run(lists, counts, CLASSES + 2, hi, other, lam_next)
        run(lists, counts, CLASSES + 3, lo, other, lam_next)
        begin_next(
            lists, counts, lam_next, icar_next, outflow, own, other, acc_next, acc_rim, hi_next
        )
        node = lax.broadcasted_iota(jnp.int32, (nodes, heads), 0)
        for b in range(blocks):
            hot[b] = jnp.where(node + b * nodes == vertex[...], 1.0, 0.0).astype(BF16)
        head[...] = head_values(lo, hi, hot)
        kept.wait()

    factor = array(factor_shape, F32)
    lam, acc, acc_rim, hi_next, icar, head0, hot, decay, inflow, outflow, other_kept = kernel(
        main_first_body,
        (
            array(state, F32),
            array(state, F32),
            array((rim, cases, nodes), F32),
            array(padded, BF16),
            array(state, F32),
            array((cases, heads), BF16),
            array(hot_shape, BF16),
            factor,
            factor,
            factor,
            array(other.shape, BF16),
        ),
        listed
        + [(acc, VM), (lo, VM), (hi, VM), (own, VM), (other, VM)]
        + [(distribution_entry_vertex.reshape(1, heads), VM)]
        + [(vertex_costate, HB), (inverter_costate, HB), (inverter_decay_factor, HB)]
        + [(costate_to_inverter_factor, HB), (inverter_to_costate_factor, HB)],
        "main_first",
        scratch=[pltpu.VMEM(state, F32), pltpu.VMEM(state, F32), pltpu.SemaphoreType.DMA((6,))],
        out_specs=(VM,) * 10 + (HB,),
    )

    def take_arrived(arrived, lam, low_rows, lo):
        keep = lax.axis_index("blk") > 0
        for b in range(low):
            row = lam[b] + jnp.where(keep, arrived[b].astype(F32), 0.0)
            low_rows[b] = row
            lo[b] = row.astype(BF16)
        lo[low] = jnp.zeros((cases, nodes), BF16)

    def rim_sums(lists, counts, acc_rim, lo, own, other, out, sums):
        sums[...] = acc_rim[...]
        run(lists, counts, 1, lo, own, sums)
        run(lists, counts, CLASSES + 1, lo, other, sums)
        out[...] = sums[...].astype(BF16)

    def rim_body(lists, counts, arrived, lam, acc_rim, own, other, out, low_rows, lo, sums):
        take_arrived(arrived, lam, low_rows, lo)
        rim_sums(lists, counts, acc_rim, lo, own, other, out, sums)

    def rim_last_body(
        lists, counts, arrived, lam, acc_rim, hi, own, other, hot, begun, place,
        out, low_rows, lo, sent, sums,
    ):
        take_arrived(arrived, lam, low_rows, lo)
        rim_sums(lists, counts, acc_rim, lo, own, other, out, sums)
        head = jnp.concatenate(
            [head_values(lo, hi, hot), jnp.zeros((nodes - cases, heads), BF16)], axis=0
        )
        dims = (((1,), (1,)), ((), ()))
        sent[...] = (
            begun[...] + lax.dot_general(place[...], head, dims, preferred_element_type=F32)
        ).astype(BF16)

    def main_body(
        lists, counts, owner, bus, low_rows, lam, lo, hi, acc, icar, own, other, hot, head0,
        decay, inflow, outflow,
        lam_low, acc_next, acc_rim, hi_next, icar_low, begun, place, icar_out,
        lam_next, icar_next, sem,
    ):
        for b in range(blocks):
            row = low_rows[b] if b < low else lam[b]
            icar_next[b] = decay[b : b + 1, :] * icar[b] + inflow[b : b + 1, :] * row
        lam_next[...] = acc[...]
        run(lists, counts, 3, lo, own, lam_next)
        run(lists, counts, CLASSES + 3, lo, other, lam_next)
        begin_next(
            lists, counts, lam_next, icar_next, outflow, own, other, acc_next, acc_rim, hi_next
        )
        for b in range(low):
            lam_low[b] = lam_next[b]
            icar_low[b] = icar_next[b]
        for b in range(low, blocks):
            icar_next[b] = decay[b : b + 1, :] * icar_next[b] + inflow[b : b + 1, :] * lam_next[b]
        upper = pl.ds(low, blocks - low)
        copy = pltpu.make_async_copy(icar_next.at[upper], icar_out.at[upper], sem)
        copy.start()
        mine = jnp.broadcast_to(owner[...].astype(F32), (heads, heads))
        before = lax.broadcasted_iota(jnp.int32, (heads, heads), 0)
        after = lax.broadcasted_iota(jnp.int32, (heads, heads), 1)
        same = jnp.logical_and(mine.T == mine, before < after)
        slot = jnp.sum(jnp.where(same, 1.0, 0.0), axis=0, keepdims=True).astype(jnp.int32)
        dest = owner[...] * (2 * slots) + slot
        row = lax.broadcasted_iota(jnp.int32, (rows_sent, heads), 0)
        place_a = jnp.where(row == dest, 1.0, 0.0).astype(BF16)
        place_b = jnp.where(row == dest + slots, 1.0, 0.0).astype(BF16)
        place[...] = place_b
        label = jnp.broadcast_to((bus[...] + 1).astype(F32), (nodes - cases, heads)).astype(BF16)
        pair_a = jnp.concatenate([head0[...], head_values(lo, hi, hot)], axis=0)
        pair_b = jnp.concatenate([jnp.zeros((cases, heads), BF16), label], axis=0)
        dims = (((1,), (1,)), ((), ()))
        begun[...] = lax.dot_general(
            place_a, pair_a, dims, preferred_element_type=F32
        ) + lax.dot_general(place_b, pair_b, dims, preferred_element_type=F32)
        copy.wait()

    tiles = [(own, VM), (other, VM)]
    rim_type = array((rim, cases, nodes), BF16)
    low_type = array(half, F32)
    sums = pltpu.VMEM((rim, cases, nodes), F32)
    assert STEPS == 3
    hi = hi_next
    leaving, low_rows, lo = kernel(
        rim_body,
        (rim_type, low_type, array(padded, BF16)),
        listed + [(arriving, VM), (lam, VM), (acc_rim, VM)] + tiles,
        "rim",
        scratch=[sums],
    )
    arriving = lax.ppermute(leaving, "blk", onward)
    lam, acc, acc_rim, hi_next, icar_low, begun, place, icar = kernel(
        main_body,
        (
            low_type,
            array(state, F32),
            array((rim, cases, nodes), F32),
            array(padded, BF16),
            low_type,
            array((rows_sent, nodes), F32),
            array((rows_sent, heads), BF16),
            array(state, F32),
        ),
        listed
        + [(distribution_entry_holder.reshape(1, heads), VM)]
        + [(distribution_entry_substation.reshape(1, heads), VM)]
        + [(low_rows, VM), (lam, VM), (lo, VM), (hi, VM), (acc, VM), (icar, VM)]
        + tiles
        + [(hot, VM), (head0, VM), (decay, VM), (inflow, VM), (outflow, VM)],
        "main",
        scratch=[pltpu.VMEM(state, F32), pltpu.VMEM(state, F32), pltpu.SemaphoreType.DMA],
        out_specs=(VM,) * 7 + (HB,),
    )

    leaving, low_rows, lo, sent = kernel(
        rim_last_body,
        (rim_type, low_type, array(padded, BF16), array((rows_sent, nodes), BF16)),
        listed
        + [(arriving, VM), (lam, VM), (acc_rim, VM), (hi_next, VM)]
        + tiles
        + [(hot, VM), (begun, VM), (place, VM)],
        "rim_last",
        scratch=[sums],
    )
    arriving = lax.ppermute(leaving, "blk", onward)
    received = lax.all_to_all(
        sent.reshape(network, 2 * slots, nodes),
        ("sec", "blk"),
        split_axis=0,
        concat_axis=0,
        tiled=True,
    ).reshape(rows_sent, nodes)

    def main_last_body(
        lists, counts, low_rows, lo, acc, icar_low, decay, inflow, own_in, other_in, icar_in,
        lam_out, low_next, icar_out, lam_next, icar_next, fetched, sems,
    ):
        del icar_in

        def fetch(side, source):
            segment = side * CLASSES + 3

            def one(i, carry):
                c = lists[segment * STRIDE + i]
                pltpu.make_async_copy(
                    source.at[c & 255], fetched.at[side * stored + i], sems.at[side]
                ).start()
                return carry

            lax.fori_loop(0, counts[segment], one, 0)

        def fetched_all(side, source):
            def one(i, carry):
                pltpu.make_async_copy(source.at[0], fetched.at[side * stored], sems.at[side]).wait()
                return carry

            lax.fori_loop(0, counts[side * CLASSES + 3], one, 0)

        fetch(0, own_in)
        fetch(1, other_in)
        for b in range(low):
            icar_next[b] = decay[b : b + 1, :] * icar_low[b] + inflow[b : b + 1, :] * low_rows[b]
        lower = pl.ds(0, low)
        icar_copy = pltpu.make_async_copy(icar_next, icar_out.at[lower], sems.at[2])
        icar_copy.start()
        lam_next[...] = acc[...]
        for side, source in enumerate((own_in, other_in)):
            fetched_all(side, source)
            segment = side * CLASSES + 3

            def some(i, carry, side=side, segment=segment):
                start = i * UNROLL
                words = []
                for u in range(UNROLL):
                    at = jnp.minimum(start + u, counts[segment] - 1)
                    words.append((lists[segment * STRIDE + start + u], side * stored + at))
                prods = [
                    jnp.dot(lo[(c >> 8) & 255], fetched[at], preferred_element_type=F32)
                    for c, at in words
                ]
                for (c, _), prod in zip(words, prods):
                    lam_next[(c >> 16) & 255] += prod
                return carry

            lax.fori_loop(0, (counts[segment] + UNROLL - 1) // UNROLL, some, 0)
        upper = pl.ds(low, blocks - low)
        lam_copy = pltpu.make_async_copy(lam_next.at[upper], lam_out.at[upper], sems.at[3])
        lam_copy.start()
        low_next[...] = lam_next[:low]
        icar_copy.wait()
        lam_copy.wait()

    lam, low_next, icar = kernel(
        main_last_body,
        (array(state, F32), low_type, array(state, F32)),
        listed
        + [(low_rows, VM), (lo, VM), (acc, VM), (icar_low, VM), (decay, VM), (inflow, VM)]
        + [(derivative_tiles, HB), (other_kept, HB), (icar, HB)],
        "main_last",
        scratch=[
            pltpu.VMEM(state, F32),
            pltpu.VMEM(half, F32),
            pltpu.VMEM((2 * stored, nodes, nodes), BF16),
            pltpu.SemaphoreType.DMA((4,)),
        ],
        out_specs=(HB, VM, HB),
        aliases={10: 2},
    )

    def trans_body(received, trans_in, matrix_in, out, trans, matrix, sems):
        copies = [
            pltpu.make_async_copy(trans_in, trans, sems.at[0]),
            pltpu.make_async_copy(matrix_in, matrix, sems.at[1]),
        ]
        for copy in copies:
            copy.start()
        got = received[...].astype(F32)
        row = lax.broadcasted_iota(jnp.int32, (rows_sent, buses), 0)
        second = lax.rem(row, 2 * slots) >= slots
        column = lax.broadcasted_iota(jnp.int32, (rows_sent, buses), 1)
        label = got[:, cases : cases + 1].astype(jnp.int32) - 1
        hot_b = jnp.where(jnp.logical_and(label == column, second), 1.0, 0.0)
        hot_a = pltpu.roll(hot_b, rows_sent - slots, 0)
        dims = (((0,), (0,)), ((), ()))
        first = lax.dot_general(received[...], hot_a.astype(BF16), dims, preferred_element_type=F32)
        last = lax.dot_general(received[...], hot_b.astype(BF16), dims, preferred_element_type=F32)
        for copy in copies:
            copy.wait()
        value = trans[...]
        for inj in (first[:cases], first[cases:], last[:cases]):
            value = jnp.dot(value.astype(BF16), matrix[...], preferred_element_type=F32) + inj
        out[...] = value

    (trans,) = kernel(
        trans_body,
        (array(highvoltage_costate.shape, F32),),
        [(received, VM), (highvoltage_costate, HB), (highvoltage_derivative_matrix, HB)],
        "trans",
        scratch=[
            pltpu.VMEM(highvoltage_costate.shape, F32),
            pltpu.VMEM(highvoltage_derivative_matrix.shape, BF16),
            pltpu.SemaphoreType.DMA((2,)),
        ],
    )

    def last_body(arrived, low_next, lam_in, lam_out, rows, sems):
        del lam_in
        keep = lax.axis_index("blk") > 0
        copies = []
        part = low // 4
        for i in range(4):
            for b in range(i * part, (i + 1) * part):
                rows[b] = low_next[b] + jnp.where(keep, arrived[b].astype(F32), 0.0)
            here = pl.ds(i * part, part)
            copies.append(pltpu.make_async_copy(rows.at[here], lam_out.at[here], sems.at[i]))
            copies[-1].start()
        for copy in copies:
            copy.wait()

    (lam,) = kernel(
        last_body,
        (array(state, F32),),
        [(arriving, VM), (low_next, VM), (lam, HB)],
        "last",
        scratch=[pltpu.VMEM(half, F32), pltpu.SemaphoreType.DMA((4,))],
        out_specs=(HB,),
        aliases={2: 0},
    )
    return (lam, icar, trans)


def solution(mesh):
    placed = (
        P(("sec", "blk"), "case", None),
        P(("sec", "blk"), "case", None),
        P("case", ("sec", "blk")),
        P(("sec", "blk", "case"), None, None),
        P(("sec", "blk", "case")),
        P(("sec", "blk", "case")),
        P(("sec", "blk"), None),
        P(("sec", "blk"), None),
        P(("sec", "blk"), None),
        P(("sec", "blk")),
        P(("sec", "blk"), None),
        P(("sec", "blk")),
        P(("sec", "blk"), None),
    )
    return jax.shard_map(
        local,
        mesh=mesh,
        in_specs=placed,
        out_specs=(
            P(("sec", "blk"), "case", None),
            P(("sec", "blk"), "case", None),
            P("case", ("sec", "blk")),
        ),
        check_vma=False,
    )
```

```python
import jax
import jax.numpy as jnp
from jax import lax
from jax.experimental import pallas as pl
from jax.experimental.pallas import tpu as pltpu
from jax.sharding import PartitionSpec as P


STEPS = 3
UNROLL = 16
FEW = 24
MANY = 40
CLASSES = 4
VMEM_LIMIT = 24 << 20

F32 = jnp.float32
BF16 = jnp.bfloat16
VM = pl.BlockSpec(memory_space=pltpu.VMEM)
SM = pl.BlockSpec(memory_space=pltpu.SMEM)
HB = pl.BlockSpec(memory_space=pltpu.HBM)
STRIDE = 128


def kernel(body, outs, ins, scratch=(), out_specs=None, aliases=None):
    return pl.pallas_call(
        body,
        out_shape=outs,
        in_specs=[spec for _, spec in ins],
        out_specs=out_specs or tuple(VM for _ in outs),
        scratch_shapes=list(scratch),
        input_output_aliases=aliases or {},
        compiler_params=pltpu.CompilerParams(vmem_limit_bytes=VMEM_LIMIT),
    )(*[in_hbm(array) if spec is HB else array for array, spec in ins])


def with_lists(body):
    def whole(own_list, own_count, other_list, other_count, *refs):
        return body((own_list, other_list), (own_count, other_count), *refs)

    return whole


def in_hbm(array):
    return pltpu.with_memory_space_constraint(array, pltpu.HBM)


def array(shape, dtype):
    return jax.ShapeDtypeStruct(shape, dtype)


def local(
    vertex_costate,
    inverter_costate,
    highvoltage_costate,
    derivative_tiles,
    tile_source_index,
    tile_target_index,
    inverter_decay_factor,
    costate_to_inverter_factor,
    inverter_to_costate_factor,
    distribution_entry_vertex,
    distribution_entry_holder,
    distribution_entry_substation,
    highvoltage_derivative_matrix,
):
    blocks, cases, nodes = vertex_costate.shape
    rim = blocks // 2
    low = blocks // 2
    targets = blocks + rim
    stored = derivative_tiles.shape[0]
    sections = lax.axis_size("sec")
    owners = lax.axis_size("blk")
    network = sections * owners
    heads = distribution_entry_vertex.shape[0]
    slots = max(2, 2 * heads // network)
    buses = highvoltage_derivative_matrix.shape[1]
    rows_sent = network * 2 * slots
    assert -(-stored // MANY) * MANY <= STRIDE and -(-stored // FEW) * FEW <= STRIDE

    state = (blocks, cases, nodes)
    half = (low, cases, nodes)
    padded = (low + 1, cases, nodes)
    acc_shape = (targets, cases, nodes)
    hot_shape = (blocks, nodes, heads)
    factor_shape = inverter_decay_factor.shape
    swap = [(0, 1), (1, 0)]
    onward = [(i, (i + 1) % owners) for i in range(owners)]

    is_low = (tile_source_index < low).astype(jnp.int32)
    is_own = (tile_target_index < blocks).astype(jnp.int32)
    own_codes = (
        lax.iota(jnp.int32, stored)
        | ((tile_source_index - low * (1 - is_low)) << 8)
        | ((tile_target_index - blocks * (1 - is_own)) << 16)
        | ((16 * is_own + 8 * is_low) << 24)
    )
    own = derivative_tiles
    other_codes = lax.ppermute(own_codes, "case", swap)
    other = lax.ppermute(own, "case", swap)

    def run(lists, counts, parts, width):
        def some(i, carry):
            words = [
                (lists[side][kind * STRIDE + i * width + u], lam, tiles, acc)
                for (side, kind), lam, tiles, acc in parts
                for u in range(width)
            ]
            prods = [
                jnp.dot(lam[(c >> 8) & 255], tiles[c & 255], preferred_element_type=F32)
                for c, lam, tiles, _ in words
            ]
            for (c, _, _, acc), prod in zip(words, prods):
                acc[(c >> 16) & 255] += prod
            return carry

        longest = 0
        for (side, kind), _, _, _ in parts:
            longest = jnp.maximum(longest, counts[side][kind])
        lax.fori_loop(0, (longest + width - 1) // width, some, 0)

    def sort(codes, lists, counts):
        def place(e, used):
            c = codes[e]
            shift = c >> 24
            lists[shift * (STRIDE // 8) + ((used >> shift) & 255)] = c
            return used + (1 << shift)

        used = lax.fori_loop(0, stored, place, jnp.int32(0), unroll=8)
        for kind in range(CLASSES):
            counts[kind] = (used >> (8 * kind)) & 255

    list_shape = (CLASSES * STRIDE,)
    list_types = (array(list_shape, jnp.int32), array((CLASSES,), jnp.int32))

    def fill_idle(idle, lists, sem):
        idle[...] = jnp.full(idle.shape, low << 8, jnp.int32)
        fill = pltpu.make_async_copy(idle, lists, sem)
        fill.start()
        return fill

    def first_body(
        codes, lam_in, own_in, acc, lo, hi, own_kept, lists, counts, lam, lam_bf, idle, sems
    ):
        lam_copy = pltpu.make_async_copy(lam_in, lam, sems.at[0])
        lam_copy.start()
        copies = [
            pltpu.make_async_copy(
                own_in.at[pl.ds(i, UNROLL)], own_kept.at[pl.ds(i, UNROLL)], sems.at[1 + i // UNROLL]
            )
            for i in range(0, stored, UNROLL)
        ]
        for copy in copies:
            copy.start()
        fill = fill_idle(idle, lists, sems.at[1 + stored // UNROLL])
        for b in range(targets):
            acc[b] = jnp.zeros((cases, nodes), F32)
        zero = jnp.zeros((cases, nodes), BF16)
        lo[low] = zero
        hi[blocks - low] = zero
        fill.wait()
        sort(codes, lists, counts)
        lam_copy.wait()
        for b in range(blocks):
            rounded = lam[b].astype(BF16)
            lam_bf[b] = rounded
            if b < low:
                lo[b] = rounded
            else:
                hi[b - low] = rounded
        for i, copy in enumerate(copies):
            copy.wait()
            prods = []
            for u in range(UNROLL):
                c = codes[i * UNROLL + u]
                k = c >> 24
                row = ((c >> 8) & 255) + jnp.where((k & 8) > 0, 0, low)
                target = ((c >> 16) & 255) + jnp.where((k & 16) > 0, 0, blocks)
                prod = jnp.dot(
                    lam_bf[row], own_kept[i * UNROLL + u], preferred_element_type=F32
                )
                prods.append((target, prod))
            for target, prod in prods:
                acc[target] += prod

    acc, lo, hi, own, own_lists, own_counts = kernel(
        first_body,
        (
            array(acc_shape, F32),
            array(padded, BF16),
            array(padded, BF16),
            array(own.shape, BF16),
        )
        + list_types,
        [(own_codes, SM), (vertex_costate, HB), (own, HB)],
        scratch=[
            pltpu.VMEM(state, F32),
            pltpu.VMEM(state, BF16),
            pltpu.VMEM(list_shape, jnp.int32),
            pltpu.SemaphoreType.DMA((2 + stored // UNROLL,)),
        ],
        out_specs=(VM,) * 4 + (SM, SM),
    )

    def sort_body(codes, lists, counts, idle, sem):
        fill_idle(idle, lists, sem).wait()
        sort(codes, lists, counts)

    other_lists, other_counts = kernel(
        sort_body,
        list_types,
        [(other_codes, SM)],
        scratch=[pltpu.VMEM(list_shape, jnp.int32), pltpu.SemaphoreType.DMA],
        out_specs=(SM, SM),
    )
    listed = [(own_lists, SM), (own_counts, SM), (other_lists, SM), (other_counts, SM)]

    def rim_first_body(lists, counts, acc, lo, hi, other, out, sums):
        sums[...] = acc[blocks:]
        run(
            lists,
            counts,
            [((1, 0), hi, other, sums), ((1, 1), lo, other, sums)],
            FEW,
        )
        out[...] = sums[...].astype(BF16)

    (leaving,) = kernel(
        with_lists(rim_first_body),
        (array((rim, cases, nodes), BF16),),
        listed + [(acc, VM), (lo, VM), (hi, VM), (other, VM)],
        scratch=[pltpu.VMEM((rim, cases, nodes), F32)],
    )
    arriving = lax.ppermute(leaving, "blk", onward)

    def begin_next(lists, counts, lam, icar, outflow, own, other, acc, acc_rim, hi):
        for b in range(blocks):
            acc[b] = outflow[b : b + 1, :] * icar[b]
        for b in range(rim):
            acc_rim[b] = jnp.zeros((cases, nodes), F32)
        for b in range(low, blocks):
            hi[b - low] = lam[b].astype(BF16)
        hi[blocks - low] = jnp.zeros((cases, nodes), BF16)
        run(lists, counts, [((0, 0), hi, own, acc_rim), ((1, 0), hi, other, acc_rim)], FEW)
        run(lists, counts, [((0, 2), hi, own, acc), ((1, 2), hi, other, acc)], MANY)

    def head_values(lo, hi, hot):
        total = jnp.dot(lo[0], hot[0], preferred_element_type=F32)
        for b in range(1, blocks):
            row = lo[b] if b < low else hi[b - low]
            total += jnp.dot(row, hot[b], preferred_element_type=F32)
        return total.astype(BF16)

    def main_first_body(
        lists, counts, acc, lo, hi, own, other, vertex, lam_in, icar_in, decay_in, inflow_in, outflow_in,
        lam_next, acc_next, acc_rim, hi_next, icar_next, head, hot, decay, inflow, outflow, other_kept,
        lam, icar, sems,
    ):
        kept = pltpu.make_async_copy(other, other_kept, sems.at[5])
        kept.start()
        pairs = [
            (icar_in, icar), (outflow_in, outflow), (lam_in, lam), (decay_in, decay), (inflow_in, inflow)
        ]
        copies = [pltpu.make_async_copy(a, b, sems.at[i]) for i, (a, b) in enumerate(pairs)]
        for copy in copies:
            copy.start()
        lam_next[...] = acc[:blocks]
        run(
            lists,
            counts,
            [((1, 2), hi, other, lam_next), ((1, 3), lo, other, lam_next)],
            MANY,
        )
        for copy in copies:
            copy.wait()
        for b in range(blocks):
            lam_next[b] += outflow[b : b + 1, :] * icar[b]
            icar_next[b] = decay[b : b + 1, :] * icar[b] + inflow[b : b + 1, :] * lam[b]
        begin_next(
            lists, counts, lam_next, icar_next, outflow, own, other, acc_next, acc_rim, hi_next
        )
        node = lax.broadcasted_iota(jnp.int32, (nodes, heads), 0)
        for b in range(blocks):
            hot[b] = jnp.where(node + b * nodes == vertex[...], 1.0, 0.0).astype(BF16)
        head[...] = head_values(lo, hi, hot)
        kept.wait()

    factor = array(factor_shape, F32)
    lam, acc, acc_rim, hi_next, icar, head0, hot, decay, inflow, outflow, other_kept = kernel(
        with_lists(main_first_body),
        (
            array(state, F32),
            array(state, F32),
            array((rim, cases, nodes), F32),
            array(padded, BF16),
            array(state, F32),
            array((cases, heads), BF16),
            array(hot_shape, BF16),
            factor,
            factor,
            factor,
            array(other.shape, BF16),
        ),
        listed
        + [(acc, VM), (lo, VM), (hi, VM), (own, VM), (other, VM)]
        + [(distribution_entry_vertex.reshape(1, heads), VM)]
        + [(vertex_costate, HB), (inverter_costate, HB), (inverter_decay_factor, HB)]
        + [(costate_to_inverter_factor, HB), (inverter_to_costate_factor, HB)],
        scratch=[pltpu.VMEM(state, F32), pltpu.VMEM(state, F32), pltpu.SemaphoreType.DMA((6,))],
        out_specs=(VM,) * 10 + (HB,),
    )

    def take_arrived(arrived, lam, low_rows, lo):
        keep = lax.axis_index("blk") > 0
        for b in range(low):
            row = lam[b] + jnp.where(keep, arrived[b].astype(F32), 0.0)
            low_rows[b] = row
            lo[b] = row.astype(BF16)
        lo[low] = jnp.zeros((cases, nodes), BF16)

    def rim_sums(lists, counts, acc_rim, lo, own, other, out, sums):
        sums[...] = acc_rim[...]
        run(lists, counts, [((0, 1), lo, own, sums), ((1, 1), lo, other, sums)], FEW)
        out[...] = sums[...].astype(BF16)

    def rim_body(lists, counts, arrived, lam, acc_rim, own, other, out, low_rows, lo, sums):
        take_arrived(arrived, lam, low_rows, lo)
        rim_sums(lists, counts, acc_rim, lo, own, other, out, sums)

    def rim_last_body(
        lists, counts, arrived, lam, acc_rim, hi, own, other, hot, begun, place,
        out, low_rows, lo, sent, sums,
    ):
        take_arrived(arrived, lam, low_rows, lo)
        rim_sums(lists, counts, acc_rim, lo, own, other, out, sums)
        head = jnp.concatenate(
            [head_values(lo, hi, hot), jnp.zeros((nodes - cases, heads), BF16)], axis=0
        )
        dims = (((1,), (1,)), ((), ()))
        sent[...] = (
            begun[...] + lax.dot_general(place[...], head, dims, preferred_element_type=F32)
        ).astype(BF16)

    def main_body(
        lists, counts, owner, bus, low_rows, lam, lo, hi, acc, icar, own, other, hot, head0,
        decay, inflow, outflow,
        lam_low, acc_next, acc_rim, hi_next, icar_low, begun, place, icar_out,
        lam_next, icar_next, sem,
    ):
        for b in range(blocks):
            row = low_rows[b] if b < low else lam[b]
            icar_next[b] = decay[b : b + 1, :] * icar[b] + inflow[b : b + 1, :] * row
        lam_next[...] = acc[...]
        run(lists, counts, [((0, 3), lo, own, lam_next), ((1, 3), lo, other, lam_next)], MANY)
        begin_next(
            lists, counts, lam_next, icar_next, outflow, own, other, acc_next, acc_rim, hi_next
        )
        for b in range(low):
            lam_low[b] = lam_next[b]
            icar_low[b] = icar_next[b]
        for b in range(low, blocks):
            icar_next[b] = decay[b : b + 1, :] * icar_next[b] + inflow[b : b + 1, :] * lam_next[b]
        upper = pl.ds(low, blocks - low)
        copy = pltpu.make_async_copy(icar_next.at[upper], icar_out.at[upper], sem)
        copy.start()
        mine = jnp.broadcast_to(owner[...].astype(F32), (heads, heads))
        before = lax.broadcasted_iota(jnp.int32, (heads, heads), 0)
        after = lax.broadcasted_iota(jnp.int32, (heads, heads), 1)
        same = jnp.logical_and(mine.T == mine, before < after)
        slot = jnp.sum(jnp.where(same, 1.0, 0.0), axis=0, keepdims=True).astype(jnp.int32)
        dest = owner[...] * (2 * slots) + slot
        row = lax.broadcasted_iota(jnp.int32, (rows_sent, heads), 0)
        place_a = jnp.where(row == dest, 1.0, 0.0).astype(BF16)
        place_b = jnp.where(row == dest + slots, 1.0, 0.0).astype(BF16)
        place[...] = place_b
        label = jnp.broadcast_to((bus[...] + 1).astype(F32), (nodes - cases, heads)).astype(BF16)
        pair_a = jnp.concatenate([head0[...], head_values(lo, hi, hot)], axis=0)
        pair_b = jnp.concatenate([jnp.zeros((cases, heads), BF16), label], axis=0)
        dims = (((1,), (1,)), ((), ()))
        begun[...] = lax.dot_general(
            place_a, pair_a, dims, preferred_element_type=F32
        ) + lax.dot_general(place_b, pair_b, dims, preferred_element_type=F32)
        copy.wait()

    tiles = [(own, VM), (other, VM)]
    rim_type = array((rim, cases, nodes), BF16)
    low_type = array(half, F32)
    sums = pltpu.VMEM((rim, cases, nodes), F32)
    assert STEPS == 3
    hi = hi_next
    leaving, low_rows, lo = kernel(
        with_lists(rim_body),
        (rim_type, low_type, array(padded, BF16)),
        listed + [(arriving, VM), (lam, VM), (acc_rim, VM)] + tiles,
        scratch=[sums],
    )
    arriving = lax.ppermute(leaving, "blk", onward)
    lam, acc, acc_rim, hi_next, icar_low, begun, place, icar = kernel(
        with_lists(main_body),
        (
            low_type,
            array(state, F32),
            array((rim, cases, nodes), F32),
            array(padded, BF16),
            low_type,
            array((rows_sent, nodes), F32),
            array((rows_sent, heads), BF16),
            array(state, F32),
        ),
        listed
        + [(distribution_entry_holder.reshape(1, heads), VM)]
        + [(distribution_entry_substation.reshape(1, heads), VM)]
        + [(low_rows, VM), (lam, VM), (lo, VM), (hi, VM), (acc, VM), (icar, VM)]
        + tiles
        + [(hot, VM), (head0, VM), (decay, VM), (inflow, VM), (outflow, VM)],
        scratch=[pltpu.VMEM(state, F32), pltpu.VMEM(state, F32), pltpu.SemaphoreType.DMA],
        out_specs=(VM,) * 7 + (HB,),
    )

    leaving, low_rows, lo, sent = kernel(
        with_lists(rim_last_body),
        (rim_type, low_type, array(padded, BF16), array((rows_sent, nodes), BF16)),
        listed
        + [(arriving, VM), (lam, VM), (acc_rim, VM), (hi_next, VM)]
        + tiles
        + [(hot, VM), (begun, VM), (place, VM)],
        scratch=[sums],
    )
    arriving = lax.ppermute(leaving, "blk", onward)
    received = lax.all_to_all(
        sent.reshape(network, 2 * slots, nodes),
        ("sec", "blk"),
        split_axis=0,
        concat_axis=0,
        tiled=True,
    ).reshape(rows_sent, nodes)

    def main_last_body(
        lists, counts, low_rows, lo, acc, icar_low, decay, inflow, own_in, other_in, icar_in,
        lam_out, low_next, icar_out, lam_next, icar_next, fetched, sems,
    ):
        del icar_in

        def fetch(side, source):
            def one(i, carry):
                c = lists[side][3 * STRIDE + i]
                pltpu.make_async_copy(
                    source.at[c & 255], fetched.at[side * stored + i], sems.at[side]
                ).start()
                return carry

            lax.fori_loop(0, counts[side][3], one, 0)

        def fetched_all(side, source):
            def one(i, carry):
                pltpu.make_async_copy(source.at[0], fetched.at[side * stored], sems.at[side]).wait()
                return carry

            lax.fori_loop(0, counts[side][3], one, 0)

        fetch(0, own_in)
        fetch(1, other_in)
        for b in range(low):
            icar_next[b] = decay[b : b + 1, :] * icar_low[b] + inflow[b : b + 1, :] * low_rows[b]
        lower = pl.ds(0, low)
        icar_copy = pltpu.make_async_copy(icar_next, icar_out.at[lower], sems.at[2])
        icar_copy.start()
        lam_next[...] = acc[...]
        for side, source in enumerate((own_in, other_in)):
            fetched_all(side, source)

            def some(i, carry, side=side):
                start = i * MANY
                words = []
                for u in range(MANY):
                    at = jnp.minimum(start + u, counts[side][3] - 1)
                    words.append((lists[side][3 * STRIDE + start + u], side * stored + at))
                prods = [
                    jnp.dot(lo[(c >> 8) & 255], fetched[at], preferred_element_type=F32)
                    for c, at in words
                ]
                for (c, _), prod in zip(words, prods):
                    lam_next[(c >> 16) & 255] += prod
                return carry

            lax.fori_loop(0, (counts[side][3] + MANY - 1) // MANY, some, 0)
        upper = pl.ds(low, blocks - low)
        lam_copy = pltpu.make_async_copy(lam_next.at[upper], lam_out.at[upper], sems.at[3])
        lam_copy.start()
        low_next[...] = lam_next[:low]
        icar_copy.wait()
        lam_copy.wait()

    lam, low_next, icar = kernel(
        with_lists(main_last_body),
        (array(state, F32), low_type, array(state, F32)),
        listed
        + [(low_rows, VM), (lo, VM), (acc, VM), (icar_low, VM), (decay, VM), (inflow, VM)]
        + [(derivative_tiles, HB), (other_kept, HB), (icar, HB)],
        scratch=[
            pltpu.VMEM(state, F32),
            pltpu.VMEM(half, F32),
            pltpu.VMEM((2 * stored, nodes, nodes), BF16),
            pltpu.SemaphoreType.DMA((4,)),
        ],
        out_specs=(HB, VM, HB),
        aliases={12: 2},
    )

    def trans_body(received, trans_in, matrix_in, out, trans, matrix, sems):
        copies = [
            pltpu.make_async_copy(trans_in, trans, sems.at[0]),
            pltpu.make_async_copy(matrix_in, matrix, sems.at[1]),
        ]
        for copy in copies:
            copy.start()
        dims = (((0,), (0,)), ((), ()))
        if slots % 16 == 0:
            parts = received[...].reshape(network, 2, slots, nodes)
            part_a = parts[:, 0].reshape(network * slots, nodes)
            part_b = parts[:, 1].reshape(network * slots, nodes)
            column = lax.broadcasted_iota(jnp.int32, (network * slots, buses), 1)
            label = part_b[:, cases : cases + 1].astype(F32).astype(jnp.int32) - 1
            hot = jnp.where(label == column, 1.0, 0.0).astype(BF16)
            first = lax.dot_general(part_a, hot, dims, preferred_element_type=F32)
            last = lax.dot_general(part_b, hot, dims, preferred_element_type=F32)
        else:
            got = received[...].astype(F32)
            row = lax.broadcasted_iota(jnp.int32, (rows_sent, buses), 0)
            second = lax.rem(row, 2 * slots) >= slots
            column = lax.broadcasted_iota(jnp.int32, (rows_sent, buses), 1)
            label = got[:, cases : cases + 1].astype(jnp.int32) - 1
            hot_b = jnp.where(jnp.logical_and(label == column, second), 1.0, 0.0)
            hot_a = pltpu.roll(hot_b, rows_sent - slots, 0).astype(BF16)
            hot_b = hot_b.astype(BF16)
            first = lax.dot_general(received[...], hot_a, dims, preferred_element_type=F32)
            last = lax.dot_general(received[...], hot_b, dims, preferred_element_type=F32)
        for copy in copies:
            copy.wait()
        value = trans[...]
        for inj in (first[:cases], first[cases:], last[:cases]):
            value = jnp.dot(value.astype(BF16), matrix[...], preferred_element_type=F32) + inj
        out[...] = value

    (trans,) = kernel(
        trans_body,
        (array(highvoltage_costate.shape, F32),),
        [(received, VM), (highvoltage_costate, HB), (highvoltage_derivative_matrix, HB)],
        scratch=[
            pltpu.VMEM(highvoltage_costate.shape, F32),
            pltpu.VMEM(highvoltage_derivative_matrix.shape, BF16),
            pltpu.SemaphoreType.DMA((2,)),
        ],
    )

    def last_body(arrived, low_next, lam_in, lam_out, rows, sems):
        del lam_in
        keep = lax.axis_index("blk") > 0
        copies = []
        part = low // 4
        for i in range(4):
            for b in range(i * part, (i + 1) * part):
                rows[b] = low_next[b] + jnp.where(keep, arrived[b].astype(F32), 0.0)
            here = pl.ds(i * part, part)
            copies.append(pltpu.make_async_copy(rows.at[here], lam_out.at[here], sems.at[i]))
            copies[-1].start()
        for copy in copies:
            copy.wait()

    (lam,) = kernel(
        last_body,
        (array(state, F32),),
        [(arriving, VM), (low_next, VM), (lam, HB)],
        scratch=[pltpu.VMEM(half, F32), pltpu.SemaphoreType.DMA((4,))],
        out_specs=(HB,),
        aliases={2: 0},
    )
    return (lam, icar, trans)


def solution(mesh):
    placed = (
        P(("sec", "blk"), "case", None),
        P(("sec", "blk"), "case", None),
        P("case", ("sec", "blk")),
        P(("sec", "blk", "case"), None, None),
        P(("sec", "blk", "case")),
        P(("sec", "blk", "case")),
        P(("sec", "blk"), None),
        P(("sec", "blk"), None),
        P(("sec", "blk"), None),
        P(("sec", "blk")),
        P(("sec", "blk"), None),
        P(("sec", "blk")),
        P(("sec", "blk"), None),
    )

    return jax.shard_map(
        local,
        mesh=mesh,
        in_specs=placed,
        out_specs=(
            P(("sec", "blk"), "case", None),
            P(("sec", "blk"), "case", None),
            P("case", ("sec", "blk")),
        ),
        check_vma=False,
    )
```

```python
import jax
import jax.numpy as jnp
from jax import lax
from jax.experimental import pallas as pl
from jax.experimental.pallas import tpu as pltpu
from jax.sharding import PartitionSpec as P


STEPS = 3
UNROLL = 16
FEW = 24
MANY = 40
CLASSES = 4
VMEM_LIMIT = 24 << 20

F32 = jnp.float32
BF16 = jnp.bfloat16
VM = pl.BlockSpec(memory_space=pltpu.VMEM)
SM = pl.BlockSpec(memory_space=pltpu.SMEM)
HB = pl.BlockSpec(memory_space=pltpu.HBM)
STRIDE = 128


def kernel(body, outs, ins, scratch=(), out_specs=None, aliases=None):
    return pl.pallas_call(
        body,
        out_shape=outs,
        in_specs=[spec for _, spec in ins],
        out_specs=out_specs or tuple(VM for _ in outs),
        scratch_shapes=list(scratch),
        input_output_aliases=aliases or {},
        compiler_params=pltpu.CompilerParams(vmem_limit_bytes=VMEM_LIMIT),
    )(*[in_hbm(array) if spec is HB else array for array, spec in ins])


def with_lists(body):
    def whole(own_list, own_count, other_list, other_count, *refs):
        return body((own_list, other_list), (own_count, other_count), *refs)

    return whole


def in_hbm(array):
    return pltpu.with_memory_space_constraint(array, pltpu.HBM)


def array(shape, dtype):
    return jax.ShapeDtypeStruct(shape, dtype)


def local(
    vertex_costate,
    inverter_costate,
    highvoltage_costate,
    derivative_tiles,
    tile_source_index,
    tile_target_index,
    inverter_decay_factor,
    costate_to_inverter_factor,
    inverter_to_costate_factor,
    distribution_entry_vertex,
    distribution_entry_holder,
    distribution_entry_substation,
    highvoltage_derivative_matrix,
):
    blocks, cases, nodes = vertex_costate.shape
    rim = blocks // 2
    low = blocks // 2
    targets = blocks + rim
    stored = derivative_tiles.shape[0]
    sections = lax.axis_size("sec")
    owners = lax.axis_size("blk")
    network = sections * owners
    heads = distribution_entry_vertex.shape[0]
    slots = max(2, 2 * heads // network)
    buses = highvoltage_derivative_matrix.shape[1]
    rows_sent = network * 3 * slots
    assert -(-stored // MANY) * MANY <= STRIDE and -(-stored // FEW) * FEW <= STRIDE

    state = (blocks, cases, nodes)
    half = (low, cases, nodes)
    padded = (low + 1, cases, nodes)
    acc_shape = (targets, cases, nodes)
    hot_shape = (blocks, nodes, heads)
    factor_shape = inverter_decay_factor.shape
    swap = [(0, 1), (1, 0)]
    onward = [(i, (i + 1) % owners) for i in range(owners)]
    backward = [(j, i) for i, j in onward]

    is_low = (tile_source_index < low).astype(jnp.int32)
    is_own = (tile_target_index < blocks).astype(jnp.int32)
    own_codes = (
        lax.iota(jnp.int32, stored)
        | ((tile_source_index - low * (1 - is_low)) << 8)
        | ((tile_target_index - blocks * (1 - is_own)) << 16)
        | ((16 * is_own + 8 * is_low) << 24)
    )
    own = derivative_tiles
    other_codes = lax.ppermute(own_codes, "case", swap)
    other = lax.ppermute(own, "case", swap)

    def run(lists, counts, parts, width):
        def some(i, carry):
            words = [
                (lists[side][kind * STRIDE + i * width + u], lam, tiles, acc)
                for (side, kind), lam, tiles, acc in parts
                for u in range(width)
            ]
            prods = [
                jnp.dot(lam[(c >> 8) & 255], tiles[c & 255], preferred_element_type=F32)
                for c, lam, tiles, _ in words
            ]
            for (c, _, _, acc), prod in zip(words, prods):
                acc[(c >> 16) & 255] += prod
            return carry

        longest = 0
        for (side, kind), _, _, _ in parts:
            longest = jnp.maximum(longest, counts[side][kind])
        lax.fori_loop(0, (longest + width - 1) // width, some, 0)

    def sort(codes, lists, counts):
        def place(e, used):
            c = codes[e]
            shift = c >> 24
            lists[shift * (STRIDE // 8) + ((used >> shift) & 255)] = c
            return used + (1 << shift)

        used = lax.fori_loop(0, stored, place, jnp.int32(0), unroll=8)
        for kind in range(CLASSES):
            counts[kind] = (used >> (8 * kind)) & 255

    list_shape = (CLASSES * STRIDE,)
    list_types = (array(list_shape, jnp.int32), array((CLASSES,), jnp.int32))

    def fill_idle(idle, lists, sem):
        idle[...] = jnp.full(idle.shape, low << 8, jnp.int32)
        fill = pltpu.make_async_copy(idle, lists, sem)
        fill.start()
        return fill

    def first_body(
        codes, lam_in, own_in, acc, lo, hi, own_kept, lists, counts, lam, lam_bf, idle, sems
    ):
        lam_copy = pltpu.make_async_copy(lam_in, lam, sems.at[0])
        lam_copy.start()
        copies = [
            pltpu.make_async_copy(
                own_in.at[pl.ds(i, UNROLL)], own_kept.at[pl.ds(i, UNROLL)], sems.at[1 + i // UNROLL]
            )
            for i in range(0, stored, UNROLL)
        ]
        for copy in copies:
            copy.start()
        fill = fill_idle(idle, lists, sems.at[1 + stored // UNROLL])
        for b in range(targets):
            acc[b] = jnp.zeros((cases, nodes), F32)
        zero = jnp.zeros((cases, nodes), BF16)
        lo[low] = zero
        hi[blocks - low] = zero
        fill.wait()
        sort(codes, lists, counts)
        lam_copy.wait()
        for b in range(blocks):
            rounded = lam[b].astype(BF16)
            lam_bf[b] = rounded
            if b < low:
                lo[b] = rounded
            else:
                hi[b - low] = rounded
        for i, copy in enumerate(copies):
            copy.wait()
            prods = []
            for u in range(UNROLL):
                c = codes[i * UNROLL + u]
                k = c >> 24
                row = ((c >> 8) & 255) + jnp.where((k & 8) > 0, 0, low)
                target = ((c >> 16) & 255) + jnp.where((k & 16) > 0, 0, blocks)
                prod = jnp.dot(
                    lam_bf[row], own_kept[i * UNROLL + u], preferred_element_type=F32
                )
                prods.append((target, prod))
            for target, prod in prods:
                acc[target] += prod

    acc, lo, hi, own, own_lists, own_counts = kernel(
        first_body,
        (
            array(acc_shape, F32),
            array(padded, BF16),
            array(padded, BF16),
            array(own.shape, BF16),
        )
        + list_types,
        [(own_codes, SM), (vertex_costate, HB), (own, HB)],
        scratch=[
            pltpu.VMEM(state, F32),
            pltpu.VMEM(state, BF16),
            pltpu.VMEM(list_shape, jnp.int32),
            pltpu.SemaphoreType.DMA((2 + stored // UNROLL,)),
        ],
        out_specs=(VM,) * 4 + (SM, SM),
    )

    def sort_body(codes, lists, counts, idle, sem):
        fill_idle(idle, lists, sem).wait()
        sort(codes, lists, counts)

    other_lists, other_counts = kernel(
        sort_body,
        list_types,
        [(other_codes, SM)],
        scratch=[pltpu.VMEM(list_shape, jnp.int32), pltpu.SemaphoreType.DMA],
        out_specs=(SM, SM),
    )
    listed = [(own_lists, SM), (own_counts, SM), (other_lists, SM), (other_counts, SM)]

    def rim_first_body(lists, counts, acc, lo, hi, other, out, sums):
        sums[...] = acc[blocks:]
        run(
            lists,
            counts,
            [((1, 0), hi, other, sums), ((1, 1), lo, other, sums)],
            FEW,
        )
        out[...] = sums[...].astype(BF16)

    (leaving,) = kernel(
        with_lists(rim_first_body),
        (array((rim, cases, nodes), BF16),),
        listed + [(acc, VM), (lo, VM), (hi, VM), (other, VM)],
        scratch=[pltpu.VMEM((rim, cases, nodes), F32)],
    )
    arriving = lax.ppermute(leaving, "blk", onward)

    mine = jnp.concatenate(
        [distribution_entry_vertex, distribution_entry_holder[:, 0], distribution_entry_substation]
    )
    theirs = lax.ppermute(mine, "blk", backward)

    def begin_next(lists, counts, lam, icar, outflow, own, other, acc, acc_rim, hi):
        for b in range(blocks):
            acc[b] = outflow[b : b + 1, :] * icar[b]
        for b in range(rim):
            acc_rim[b] = jnp.zeros((cases, nodes), F32)
        for b in range(low, blocks):
            hi[b - low] = lam[b].astype(BF16)
        hi[blocks - low] = jnp.zeros((cases, nodes), BF16)
        run(lists, counts, [((0, 0), hi, own, acc_rim), ((1, 0), hi, other, acc_rim)], FEW)
        run(lists, counts, [((0, 2), hi, own, acc), ((1, 2), hi, other, acc)], MANY)

    def head_values(lo, hi, hot):
        total = jnp.dot(lo[0], hot[0], preferred_element_type=F32)
        for b in range(1, blocks):
            row = lo[b] if b < low else hi[b - low]
            total += jnp.dot(row, hot[b], preferred_element_type=F32)
        return total.astype(BF16)

    def main_first_body(
        lists, counts, acc, lo, hi, own, other, vertex, lam_in, icar_in, decay_in, inflow_in, outflow_in,
        lam_next, acc_next, acc_rim, hi_next, icar_next, head, hot, decay, inflow, outflow, other_kept,
        lam, icar, sems,
    ):
        kept = pltpu.make_async_copy(other, other_kept, sems.at[5])
        kept.start()
        pairs = [
            (icar_in, icar), (outflow_in, outflow), (lam_in, lam), (decay_in, decay), (inflow_in, inflow)
        ]
        copies = [pltpu.make_async_copy(a, b, sems.at[i]) for i, (a, b) in enumerate(pairs)]
        for copy in copies:
            copy.start()
        lam_next[...] = acc[:blocks]
        run(
            lists,
            counts,
            [((1, 2), hi, other, lam_next), ((1, 3), lo, other, lam_next)],
            MANY,
        )
        for copy in copies:
            copy.wait()
        for b in range(blocks):
            lam_next[b] += outflow[b : b + 1, :] * icar[b]
            icar_next[b] = decay[b : b + 1, :] * icar[b] + inflow[b : b + 1, :] * lam[b]
        begin_next(
            lists, counts, lam_next, icar_next, outflow, own, other, acc_next, acc_rim, hi_next
        )
        node = lax.broadcasted_iota(jnp.int32, (nodes, heads), 0)
        for b in range(blocks):
            hot[b] = jnp.where(node + b * nodes == vertex[...], 1.0, 0.0).astype(BF16)
        head[...] = head_values(lo, hi, hot)
        kept.wait()

    factor = array(factor_shape, F32)
    lam, acc, acc_rim, hi_next, icar, head0, hot, decay, inflow, outflow, other_kept = kernel(
        with_lists(main_first_body),
        (
            array(state, F32),
            array(state, F32),
            array((rim, cases, nodes), F32),
            array(padded, BF16),
            array(state, F32),
            array((cases, heads), BF16),
            array(hot_shape, BF16),
            factor,
            factor,
            factor,
            array(other.shape, BF16),
        ),
        listed
        + [(acc, VM), (lo, VM), (hi, VM), (own, VM), (other, VM)]
        + [(distribution_entry_vertex.reshape(1, heads), VM)]
        + [(vertex_costate, HB), (inverter_costate, HB), (inverter_decay_factor, HB)]
        + [(costate_to_inverter_factor, HB), (inverter_to_costate_factor, HB)],
        scratch=[pltpu.VMEM(state, F32), pltpu.VMEM(state, F32), pltpu.SemaphoreType.DMA((6,))],
        out_specs=(VM,) * 10 + (HB,),
    )

    def take_arrived(arrived, lam, low_rows, lo):
        keep = lax.axis_index("blk") > 0
        for b in range(low):
            row = lam[b] + jnp.where(keep, arrived[b].astype(F32), 0.0)
            low_rows[b] = row
            lo[b] = row.astype(BF16)
        lo[low] = jnp.zeros((cases, nodes), BF16)

    def rim_sums(lists, counts, acc_rim, lo, own, other, out, sums):
        sums[...] = acc_rim[...]
        run(lists, counts, [((0, 1), lo, own, sums), ((1, 1), lo, other, sums)], FEW)
        out[...] = sums[...].astype(BF16)

    def rim_body(lists, counts, arrived, lam, acc_rim, own, other, out, low_rows, lo, sums):
        take_arrived(arrived, lam, low_rows, lo)
        rim_sums(lists, counts, acc_rim, lo, own, other, out, sums)

    def rim_last_body(lists, counts, arrived, lam, acc_rim, kept, out, low_rows, lo, sums):
        take_arrived(arrived, lam, low_rows, lo)
        sums[...] = acc_rim[...]
        for side in (0, 1):
            run_fetched(lists, counts, side, 1, lo, kept, side * stored, sums, FEW)
        out[...] = sums[...].astype(BF16)

    def rows_of(owner):
        names = jnp.broadcast_to(owner.astype(F32), (heads, heads))
        before = lax.broadcasted_iota(jnp.int32, (heads, heads), 0)
        after = lax.broadcasted_iota(jnp.int32, (heads, heads), 1)
        same = jnp.logical_and(names.T == names, before < after)
        slot = jnp.sum(jnp.where(same, 1.0, 0.0), axis=0, keepdims=True).astype(jnp.int32)
        return owner * (3 * slots) + slot

    def main_body(
        lists, counts, owner, bus, theirs, left,
        low_rows, lam, lo, hi, acc, icar, own, other, hot, head0, decay, inflow, outflow,
        lam_low, acc_next, hi_next, icar_low, sent, icar_out, lam_next, icar_next, lo_base, sem,
    ):
        for b in range(blocks):
            row = low_rows[b] if b < low else lam[b]
            icar_next[b] = decay[b : b + 1, :] * icar[b] + inflow[b : b + 1, :] * row
            acc_next[b] = outflow[b : b + 1, :] * icar_next[b]
        lam_next[...] = acc[...]
        run(lists, counts, [((0, 3), lo, own, lam_next), ((1, 3), lo, other, lam_next)], MANY)
        for b in range(low):
            lam_low[b] = lam_next[b]
            lo_base[b] = lam_next[b].astype(BF16)
            icar_low[b] = icar_next[b]
        for b in range(low, blocks):
            hi_next[b - low] = lam_next[b].astype(BF16)
            icar_next[b] = decay[b : b + 1, :] * icar_next[b] + inflow[b : b + 1, :] * lam_next[b]
        hi_next[blocks - low] = jnp.zeros((cases, nodes), BF16)
        upper = pl.ds(low, blocks - low)
        copy = pltpu.make_async_copy(icar_next.at[upper], icar_out.at[upper], sem)
        copy.start()
        node = lax.broadcasted_iota(jnp.int32, (nodes, heads), 0)
        vertex_next, owner_next, bus_next = (theirs[:, i * heads : (i + 1) * heads] for i in range(3))
        head_next = jnp.zeros((cases, heads), F32)
        for b in range(low):
            hot_next = jnp.where(node + b * nodes == vertex_next, 1.0, 0.0).astype(BF16)
            head_next += jnp.dot(left[b], hot_next, preferred_element_type=F32)
        row = lax.broadcasted_iota(jnp.int32, (rows_sent, heads), 0)
        dest = rows_of(owner[...])
        followed = lax.axis_index("blk") < owners - 1
        dest_next = jnp.where(followed, rows_of(owner_next) + 2 * slots, -1)
        width = (nodes - cases, heads)
        pairs = [
            (dest, head0[...], head_values(lo, hi, hot)),
            (
                dest + slots,
                head_values(lo_base, hi_next, hot),
                jnp.broadcast_to((bus[...] + 1).astype(F32), width).astype(BF16),
            ),
            (
                dest_next,
                head_next.astype(BF16),
                jnp.broadcast_to((bus_next + 1).astype(F32), width).astype(BF16),
            ),
        ]
        total = jnp.zeros((rows_sent, nodes), F32)
        for where, upper_half, lower_half in pairs:
            place = jnp.where(row == where, 1.0, 0.0).astype(BF16)
            total += lax.dot_general(
                place,
                jnp.concatenate([upper_half, lower_half], axis=0),
                (((1,), (1,)), ((), ())),
                preferred_element_type=F32,
            )
        sent[...] = total.astype(BF16)
        copy.wait()

    def fetch(lists, counts, side, kind, source, dest, first, sem):
        def one(i, carry):
            c = lists[side][kind * STRIDE + i]
            pltpu.make_async_copy(source.at[c & 255], dest.at[first + i], sem).start()
            return carry

        lax.fori_loop(0, counts[side][kind], one, 0)

    def fetched(counts, side, kind, source, dest, sem):
        def one(i, carry):
            pltpu.make_async_copy(source.at[0], dest.at[0], sem).wait()
            return carry

        lax.fori_loop(0, counts[side][kind], one, 0)

    def run_fetched(lists, counts, side, kind, lam, source, first, acc, width):
        def some(i, carry):
            words = []
            for u in range(width):
                at = jnp.minimum(i * width + u, counts[side][kind] - 1)
                words.append((lists[side][kind * STRIDE + i * width + u], first + at))
            prods = [
                jnp.dot(lam[(c >> 8) & 255], source[at], preferred_element_type=F32)
                for c, at in words
            ]
            for (c, _), prod in zip(words, prods):
                acc[(c >> 16) & 255] += prod
            return carry

        lax.fori_loop(0, (counts[side][kind] + width - 1) // width, some, 0)

    def begin_last_body(
        lists, counts, begun, hi, own_in, other_in, acc, acc_rim, kept, ready, sems
    ):
        sources = (own_in, other_in)
        for side in (0, 1):
            first = side * stored
            fetch(lists, counts, side, 0, sources[side], ready, first, sems.at[side, 0])
            fetch(
                lists, counts, side, 2, sources[side], ready, first + counts[side][0], sems.at[side, 2]
            )
        for side in (0, 1):
            fetch(lists, counts, side, 1, sources[side], kept, side * stored, sems.at[side, 1])
        acc[...] = begun[...]
        acc_rim[...] = jnp.zeros(acc_rim.shape, F32)
        for side in (0, 1):
            first = side * stored
            fetched(counts, side, 0, sources[side], ready, sems.at[side, 0])
            run_fetched(lists, counts, side, 0, hi, ready, first, acc_rim, FEW)
            fetched(counts, side, 2, sources[side], ready, sems.at[side, 2])
            run_fetched(lists, counts, side, 2, hi, ready, first + counts[side][0], acc, MANY)
        for side in (0, 1):
            fetched(counts, side, 1, sources[side], kept, sems.at[side, 1])

    tiles = [(own, VM), (other, VM)]
    rim_type = array((rim, cases, nodes), BF16)
    low_type = array(half, F32)
    sums = pltpu.VMEM((rim, cases, nodes), F32)
    assert STEPS == 3
    hi = hi_next
    leaving, low_rows, lo = kernel(
        with_lists(rim_body),
        (rim_type, low_type, array(padded, BF16)),
        listed + [(arriving, VM), (lam, VM), (acc_rim, VM)] + tiles,
        scratch=[sums],
    )
    arriving = lax.ppermute(leaving, "blk", onward)
    lam, acc, hi_next, icar_low, sent, icar = kernel(
        with_lists(main_body),
        (
            low_type,
            array(state, F32),
            array(padded, BF16),
            low_type,
            array((rows_sent, nodes), BF16),
            array(state, F32),
        ),
        listed
        + [
            (distribution_entry_holder.reshape(1, heads), VM),
            (distribution_entry_substation.reshape(1, heads), VM),
            (theirs.reshape(1, 3 * heads), VM),
            (leaving, VM),
        ]
        + [(low_rows, VM), (lam, VM), (lo, VM), (hi, VM), (acc, VM), (icar, VM)]
        + tiles
        + [(hot, VM), (head0, VM), (decay, VM), (inflow, VM), (outflow, VM)],
        scratch=[
            pltpu.VMEM(state, F32),
            pltpu.VMEM(state, F32),
            pltpu.VMEM(half, BF16),
            pltpu.SemaphoreType.DMA,
        ],
        out_specs=(VM,) * 5 + (HB,),
    )
    received = lax.all_to_all(
        sent.reshape(network, 3 * slots, nodes),
        ("sec", "blk"),
        split_axis=0,
        concat_axis=0,
        tiled=True,
    )
    received = received.reshape(rows_sent, nodes)
    stored_in = [(derivative_tiles, HB), (other_kept, HB)]
    fetched_shape = (2 * stored, nodes, nodes)
    acc, acc_rim, kept = kernel(
        with_lists(begin_last_body),
        (array(state, F32), array((rim, cases, nodes), F32), array(fetched_shape, BF16)),
        listed + [(acc, VM), (hi_next, VM)] + stored_in,
        scratch=[pltpu.VMEM(fetched_shape, BF16), pltpu.SemaphoreType.DMA((2, 3))],
    )

    leaving, low_rows, lo = kernel(
        with_lists(rim_last_body),
        (rim_type, low_type, array(padded, BF16)),
        listed + [(arriving, VM), (lam, VM), (acc_rim, VM), (kept, VM)],
        scratch=[sums],
    )
    arriving = lax.ppermute(leaving, "blk", onward)

    def main_last_body(
        lists, counts, low_rows, lo, acc, icar_low, decay, inflow, own_in, other_in, icar_in,
        lam_out, low_next, icar_out, lam_next, icar_next, ready, sems,
    ):
        del icar_in
        sources = (own_in, other_in)
        for side in (0, 1):
            fetch(lists, counts, side, 3, sources[side], ready, side * stored, sems.at[side])
        for b in range(low):
            icar_next[b] = decay[b : b + 1, :] * icar_low[b] + inflow[b : b + 1, :] * low_rows[b]
        lower = pl.ds(0, low)
        icar_copy = pltpu.make_async_copy(icar_next, icar_out.at[lower], sems.at[2])
        icar_copy.start()
        lam_next[...] = acc[...]
        for side in (0, 1):
            fetched(counts, side, 3, sources[side], ready, sems.at[side])
            run_fetched(lists, counts, side, 3, lo, ready, side * stored, lam_next, MANY)
        upper = pl.ds(low, blocks - low)
        lam_copy = pltpu.make_async_copy(lam_next.at[upper], lam_out.at[upper], sems.at[3])
        lam_copy.start()
        low_next[...] = lam_next[:low]
        icar_copy.wait()
        lam_copy.wait()

    lam, low_next, icar = kernel(
        with_lists(main_last_body),
        (array(state, F32), low_type, array(state, F32)),
        listed
        + [(low_rows, VM), (lo, VM), (acc, VM), (icar_low, VM), (decay, VM), (inflow, VM)]
        + stored_in
        + [(icar, HB)],
        scratch=[
            pltpu.VMEM(state, F32),
            pltpu.VMEM(half, F32),
            pltpu.VMEM(fetched_shape, BF16),
            pltpu.SemaphoreType.DMA((4,)),
        ],
        out_specs=(HB, VM, HB),
        aliases={12: 2},
    )

    def trans_body(received, trans_in, matrix_in, out, trans, matrix, sems):
        copies = [
            pltpu.make_async_copy(trans_in, trans, sems.at[0]),
            pltpu.make_async_copy(matrix_in, matrix, sems.at[1]),
        ]
        for copy in copies:
            copy.start()
        dims = (((0,), (0,)), ((), ()))
        if slots % 16 == 0:
            parts = received[...].reshape(network, 3, slots, nodes)
            part = [parts[:, i].reshape(network * slots, nodes) for i in range(3)]
            column = lax.broadcasted_iota(jnp.int32, (network * slots, buses), 1)

            def hot_of(rows):
                label = rows[:, cases : cases + 1].astype(F32).astype(jnp.int32) - 1
                return jnp.where(label == column, 1.0, 0.0).astype(BF16)

            hot = hot_of(part[1])
            first = lax.dot_general(part[0], hot, dims, preferred_element_type=F32)
            last = lax.dot_general(part[1], hot, dims, preferred_element_type=F32)
            last += lax.dot_general(part[2], hot_of(part[2]), dims, preferred_element_type=F32)
        else:
            got = received[...].astype(F32)
            row = lax.broadcasted_iota(jnp.int32, (rows_sent, buses), 0)
            place = lax.rem(row, 3 * slots)
            column = lax.broadcasted_iota(jnp.int32, (rows_sent, buses), 1)
            label = got[:, cases : cases + 1].astype(jnp.int32) - 1
            hot = jnp.where(jnp.logical_and(label == column, place >= slots), 1.0, 0.0)
            own_hot = jnp.where(place < 2 * slots, hot, 0.0)
            hot_a = pltpu.roll(own_hot, rows_sent - slots, 0).astype(BF16)
            first = lax.dot_general(received[...], hot_a, dims, preferred_element_type=F32)
            last = lax.dot_general(
                received[...], hot.astype(BF16), dims, preferred_element_type=F32
            )
        for copy in copies:
            copy.wait()
        value = trans[...]
        for inj in (first[:cases], first[cases:], last[:cases]):
            value = jnp.dot(value.astype(BF16), matrix[...], preferred_element_type=F32) + inj
        out[...] = value

    (trans,) = kernel(
        trans_body,
        (array(highvoltage_costate.shape, F32),),
        [(received, VM), (highvoltage_costate, HB), (highvoltage_derivative_matrix, HB)],
        scratch=[
            pltpu.VMEM(highvoltage_costate.shape, F32),
            pltpu.VMEM(highvoltage_derivative_matrix.shape, BF16),
            pltpu.SemaphoreType.DMA((2,)),
        ],
    )

    def last_body(arrived, low_next, lam_in, lam_out, rows, sems):
        del lam_in
        keep = lax.axis_index("blk") > 0
        copies = []
        part = low // 4
        for i in range(4):
            for b in range(i * part, (i + 1) * part):
                rows[b] = low_next[b] + jnp.where(keep, arrived[b].astype(F32), 0.0)
            here = pl.ds(i * part, part)
            copies.append(pltpu.make_async_copy(rows.at[here], lam_out.at[here], sems.at[i]))
            copies[-1].start()
        for copy in copies:
            copy.wait()

    (lam,) = kernel(
        last_body,
        (array(state, F32),),
        [(arriving, VM), (low_next, VM), (lam, HB)],
        scratch=[pltpu.VMEM(half, F32), pltpu.SemaphoreType.DMA((4,))],
        out_specs=(HB,),
        aliases={2: 0},
    )
    return (lam, icar, trans)


def solution(mesh):
    placed = (
        P(("sec", "blk"), "case", None),
        P(("sec", "blk"), "case", None),
        P("case", ("sec", "blk")),
        P(("sec", "blk", "case"), None, None),
        P(("sec", "blk", "case")),
        P(("sec", "blk", "case")),
        P(("sec", "blk"), None),
        P(("sec", "blk"), None),
        P(("sec", "blk"), None),
        P(("sec", "blk")),
        P(("sec", "blk"), None),
        P(("sec", "blk")),
        P(("sec", "blk"), None),
    )

    return jax.shard_map(
        local,
        mesh=mesh,
        in_specs=placed,
        out_specs=(
            P(("sec", "blk"), "case", None),
            P(("sec", "blk"), "case", None),
            P("case", ("sec", "blk")),
        ),
        check_vma=False,
    )
```

```python
import jax
import jax.numpy as jnp
from jax import lax
from jax.experimental import pallas as pl
from jax.experimental.pallas import tpu as pltpu
from jax.sharding import PartitionSpec as P


STEPS = 3
UNROLL = 16
FEW = 24
MANY = 40
CLASSES = 4
VMEM_LIMIT = 24 << 20

F32 = jnp.float32
BF16 = jnp.bfloat16
VM = pl.BlockSpec(memory_space=pltpu.VMEM)
SM = pl.BlockSpec(memory_space=pltpu.SMEM)
HB = pl.BlockSpec(memory_space=pltpu.HBM)
STRIDE = 128


def kernel(body, outs, ins, scratch=(), out_specs=None, aliases=None):
    return pl.pallas_call(
        body,
        out_shape=outs,
        in_specs=[spec for _, spec in ins],
        out_specs=out_specs or tuple(VM for _ in outs),
        scratch_shapes=list(scratch),
        input_output_aliases=aliases or {},
        compiler_params=pltpu.CompilerParams(vmem_limit_bytes=VMEM_LIMIT),
    )(*[in_hbm(array) if spec is HB else array for array, spec in ins])


def with_lists(body):
    def whole(own_list, own_count, other_list, other_count, *refs):
        return body((own_list, other_list), (own_count, other_count), *refs)

    return whole


def in_hbm(array):
    return pltpu.with_memory_space_constraint(array, pltpu.HBM)


def array(shape, dtype):
    return jax.ShapeDtypeStruct(shape, dtype)


def hbm_array(shape, dtype):
    return pltpu.HBM(shape, dtype)


def local(
    vertex_costate,
    inverter_costate,
    highvoltage_costate,
    derivative_tiles,
    tile_source_index,
    tile_target_index,
    inverter_decay_factor,
    costate_to_inverter_factor,
    inverter_to_costate_factor,
    distribution_entry_vertex,
    distribution_entry_holder,
    distribution_entry_substation,
    highvoltage_derivative_matrix,
):
    blocks, cases, nodes = vertex_costate.shape
    rim = blocks // 2
    low = blocks // 2
    targets = blocks + rim
    stored = derivative_tiles.shape[0]
    sections = lax.axis_size("sec")
    owners = lax.axis_size("blk")
    network = sections * owners
    heads = distribution_entry_vertex.shape[0]
    slots = max(2, 2 * heads // network)
    buses = highvoltage_derivative_matrix.shape[1]
    rows_sent = network * 3 * slots
    assert -(-stored // MANY) * MANY <= STRIDE and -(-stored // FEW) * FEW <= STRIDE

    state = (blocks, cases, nodes)
    half = (low, cases, nodes)
    padded = (low + 1, cases, nodes)
    acc_shape = (targets, cases, nodes)
    hot_shape = (blocks, nodes, heads)
    factor_shape = inverter_decay_factor.shape
    swap = [(0, 1), (1, 0)]
    onward = [(i, (i + 1) % owners) for i in range(owners)]
    backward = [(j, i) for i, j in onward]

    is_low = (tile_source_index < low).astype(jnp.int32)
    is_own = (tile_target_index < blocks).astype(jnp.int32)
    own_codes = (
        lax.iota(jnp.int32, stored)
        | ((tile_source_index - low * (1 - is_low)) << 8)
        | ((tile_target_index - blocks * (1 - is_own)) << 16)
        | ((16 * is_own + 8 * is_low) << 24)
    )
    own = derivative_tiles
    other_codes = lax.ppermute(own_codes, "case", swap)
    other = lax.ppermute(own, "case", swap)

    def run(lists, counts, parts, width):
        def some(i, carry):
            words = [
                (lists[side][kind * STRIDE + i * width + u], lam, tiles, acc)
                for (side, kind), lam, tiles, acc in parts
                for u in range(width)
            ]
            prods = [
                jnp.dot(lam[(c >> 8) & 255], tiles[c & 255], preferred_element_type=F32)
                for c, lam, tiles, _ in words
            ]
            for (c, _, _, acc), prod in zip(words, prods):
                acc[(c >> 16) & 255] += prod
            return carry

        longest = 0
        for (side, kind), _, _, _ in parts:
            longest = jnp.maximum(longest, counts[side][kind])
        lax.fori_loop(0, (longest + width - 1) // width, some, 0)

    def sort(codes, lists, counts):
        def place(e, used):
            c = codes[e]
            shift = c >> 24
            lists[shift * (STRIDE // 8) + ((used >> shift) & 255)] = c
            return used + (1 << shift)

        used = lax.fori_loop(0, stored, place, jnp.int32(0), unroll=8)
        for kind in range(CLASSES):
            counts[kind] = (used >> (8 * kind)) & 255

    list_shape = (CLASSES * STRIDE,)
    list_types = (array(list_shape, jnp.int32), array((CLASSES,), jnp.int32))

    def fill_idle(idle, lists, sem):
        idle[...] = jnp.full(idle.shape, low << 8, jnp.int32)
        fill = pltpu.make_async_copy(idle, lists, sem)
        fill.start()
        return fill

    def first_body(
        codes, lam_in, own_in, acc, lo, hi, own_kept, lists, counts, lam, lam_bf, idle, sems
    ):
        lam_copy = pltpu.make_async_copy(lam_in, lam, sems.at[0])
        lam_copy.start()
        copies = [
            pltpu.make_async_copy(
                own_in.at[pl.ds(i, UNROLL)], own_kept.at[pl.ds(i, UNROLL)], sems.at[1 + i // UNROLL]
            )
            for i in range(0, stored, UNROLL)
        ]
        for copy in copies:
            copy.start()
        fill = fill_idle(idle, lists, sems.at[1 + stored // UNROLL])
        for b in range(targets):
            acc[b] = jnp.zeros((cases, nodes), F32)
        zero = jnp.zeros((cases, nodes), BF16)
        lo[low] = zero
        hi[blocks - low] = zero
        fill.wait()
        sort(codes, lists, counts)
        lam_copy.wait()
        for b in range(blocks):
            rounded = lam[b].astype(BF16)
            lam_bf[b] = rounded
            if b < low:
                lo[b] = rounded
            else:
                hi[b - low] = rounded
        for i, copy in enumerate(copies):
            copy.wait()
            prods = []
            for u in range(UNROLL):
                c = codes[i * UNROLL + u]
                k = c >> 24
                row = ((c >> 8) & 255) + jnp.where((k & 8) > 0, 0, low)
                target = ((c >> 16) & 255) + jnp.where((k & 16) > 0, 0, blocks)
                prod = jnp.dot(
                    lam_bf[row], own_kept[i * UNROLL + u], preferred_element_type=F32
                )
                prods.append((target, prod))
            for target, prod in prods:
                acc[target] += prod

    acc, lo, hi, own, own_lists, own_counts = kernel(
        first_body,
        (
            array(acc_shape, F32),
            array(padded, BF16),
            array(padded, BF16),
            array(own.shape, BF16),
        )
        + list_types,
        [(own_codes, SM), (vertex_costate, HB), (own, HB)],
        scratch=[
            pltpu.VMEM(state, F32),
            pltpu.VMEM(state, BF16),
            pltpu.VMEM(list_shape, jnp.int32),
            pltpu.SemaphoreType.DMA((2 + stored // UNROLL,)),
        ],
        out_specs=(VM,) * 4 + (SM, SM),
    )

    def sort_body(codes, lists, counts, idle, sem):
        fill_idle(idle, lists, sem).wait()
        sort(codes, lists, counts)

    other_lists, other_counts = kernel(
        sort_body,
        list_types,
        [(other_codes, SM)],
        scratch=[pltpu.VMEM(list_shape, jnp.int32), pltpu.SemaphoreType.DMA],
        out_specs=(SM, SM),
    )
    listed = [(own_lists, SM), (own_counts, SM), (other_lists, SM), (other_counts, SM)]

    def rim_first_body(lists, counts, acc, lo, hi, other, out, sums):
        sums[...] = acc[blocks:]
        run(
            lists,
            counts,
            [((1, 0), hi, other, sums), ((1, 1), lo, other, sums)],
            FEW,
        )
        out[...] = sums[...].astype(BF16)

    (leaving,) = kernel(
        with_lists(rim_first_body),
        (array((rim, cases, nodes), BF16),),
        listed + [(acc, VM), (lo, VM), (hi, VM), (other, VM)],
        scratch=[pltpu.VMEM((rim, cases, nodes), F32)],
    )
    arriving = lax.ppermute(leaving, "blk", onward)

    mine = jnp.concatenate(
        [
            distribution_entry_vertex.reshape(1, heads),
            distribution_entry_holder.reshape(1, heads),
            distribution_entry_substation.reshape(1, heads),
        ],
        axis=1,
    )
    theirs = lax.ppermute(mine, "blk", backward)

    def begin_next(lists, counts, lam, icar, outflow, own, other, acc, acc_rim, hi):
        for b in range(blocks):
            acc[b] = outflow[b : b + 1, :] * icar[b]
        for b in range(rim):
            acc_rim[b] = jnp.zeros((cases, nodes), F32)
        for b in range(low, blocks):
            hi[b - low] = lam[b].astype(BF16)
        hi[blocks - low] = jnp.zeros((cases, nodes), BF16)
        run(lists, counts, [((0, 0), hi, own, acc_rim), ((1, 0), hi, other, acc_rim)], FEW)
        run(lists, counts, [((0, 2), hi, own, acc), ((1, 2), hi, other, acc)], MANY)

    def head_values(lo, hi, hot):
        total = jnp.dot(lo[0], hot[0], preferred_element_type=F32)
        for b in range(1, blocks):
            row = lo[b] if b < low else hi[b - low]
            total += jnp.dot(row, hot[b], preferred_element_type=F32)
        return total.astype(BF16)

    def main_first_body(
        lists, counts, acc, lo, hi, own, other, vertex, lam_in, icar_in, decay_in, inflow_in, outflow_in,
        lam_next, acc_next, acc_rim, hi_next, icar_next, head, hot, decay, inflow, outflow, other_kept,
        lam, icar, sems,
    ):
        kept = pltpu.make_async_copy(other, other_kept, sems.at[5])
        kept.start()
        pairs = [
            (icar_in, icar), (outflow_in, outflow), (lam_in, lam), (decay_in, decay), (inflow_in, inflow)
        ]
        copies = [pltpu.make_async_copy(a, b, sems.at[i]) for i, (a, b) in enumerate(pairs)]
        for copy in copies:
            copy.start()
        lam_next[...] = acc[:blocks]
        run(
            lists,
            counts,
            [((1, 2), hi, other, lam_next), ((1, 3), lo, other, lam_next)],
            MANY,
        )
        for copy in copies:
            copy.wait()
        for b in range(blocks):
            lam_next[b] += outflow[b : b + 1, :] * icar[b]
            icar_next[b] = decay[b : b + 1, :] * icar[b] + inflow[b : b + 1, :] * lam[b]
        begin_next(
            lists, counts, lam_next, icar_next, outflow, own, other, acc_next, acc_rim, hi_next
        )
        node = lax.broadcasted_iota(jnp.int32, (nodes, heads), 0)
        for b in range(blocks):
            hot[b] = jnp.where(node + b * nodes == vertex[...], 1.0, 0.0).astype(BF16)
        head[...] = head_values(lo, hi, hot)
        kept.wait()

    factor = array(factor_shape, F32)
    lam, acc, acc_rim, hi_next, icar, head0, hot, decay, inflow, outflow, other_kept = kernel(
        with_lists(main_first_body),
        (
            array(state, F32),
            array(state, F32),
            array((rim, cases, nodes), F32),
            array(padded, BF16),
            array(state, F32),
            array((cases, heads), BF16),
            array(hot_shape, BF16),
            factor,
            factor,
            factor,
            hbm_array(other.shape, BF16),
        ),
        listed
        + [(acc, VM), (lo, VM), (hi, VM), (own, VM), (other, VM)]
        + [(distribution_entry_vertex.reshape(1, heads), VM)]
        + [(vertex_costate, HB), (inverter_costate, HB), (inverter_decay_factor, HB)]
        + [(costate_to_inverter_factor, HB), (inverter_to_costate_factor, HB)],
        scratch=[pltpu.VMEM(state, F32), pltpu.VMEM(state, F32), pltpu.SemaphoreType.DMA((6,))],
        out_specs=(VM,) * 10 + (HB,),
    )

    def take_arrived(arrived, lam, low_rows, lo):
        keep = lax.axis_index("blk") > 0
        for b in range(low):
            row = lam[b] + jnp.where(keep, arrived[b].astype(F32), 0.0)
            low_rows[b] = row
            lo[b] = row.astype(BF16)
        lo[low] = jnp.zeros((cases, nodes), BF16)

    def rim_sums(lists, counts, acc_rim, lo, own, other, out, sums):
        sums[...] = acc_rim[...]
        run(lists, counts, [((0, 1), lo, own, sums), ((1, 1), lo, other, sums)], FEW)
        out[...] = sums[...].astype(BF16)

    def rim_body(lists, counts, arrived, lam, acc_rim, own, other, out, low_rows, lo, sums):
        take_arrived(arrived, lam, low_rows, lo)
        rim_sums(lists, counts, acc_rim, lo, own, other, out, sums)

    def rim_last_body(
        lists, counts, arrived, lam, acc_rim, own_in, other_in, out, low_rows, lo, sums, ready, sems
    ):
        sources = (own_in, other_in)
        for side in (0, 1):
            fetch(lists, counts, side, 1, sources[side], ready, side * stored, sems.at[side])
        take_arrived(arrived, lam, low_rows, lo)
        sums[...] = acc_rim[...]
        for side in (0, 1):
            fetched(counts, side, 1, sources[side], ready, sems.at[side])
            run_fetched(lists, counts, side, 1, lo, ready, side * stored, sums, FEW)
        out[...] = sums[...].astype(BF16)

    def rows_of(owner):
        names = jnp.broadcast_to(owner.astype(F32), (heads, heads))
        before = lax.broadcasted_iota(jnp.int32, (heads, heads), 0)
        after = lax.broadcasted_iota(jnp.int32, (heads, heads), 1)
        same = jnp.logical_and(names.T == names, before < after)
        slot = jnp.sum(jnp.where(same, 1.0, 0.0), axis=0, keepdims=True).astype(jnp.int32)
        return owner * (3 * slots) + slot

    def main_body(
        lists, counts, owner, bus, theirs, left,
        low_rows, lam, lo, hi, acc, icar, own, other, hot, head0, decay, inflow,
        lam_next, acc_rim, hi_next, sent, icar_out, icar_next, lo_base, sem,
    ):
        for b in range(blocks):
            row = low_rows[b] if b < low else lam[b]
            icar_next[b] = decay[b : b + 1, :] * icar[b] + inflow[b : b + 1, :] * row
        copy = pltpu.make_async_copy(icar_next, icar_out, sem)
        copy.start()
        lam_next[...] = acc[...]
        run(lists, counts, [((0, 3), lo, own, lam_next), ((1, 3), lo, other, lam_next)], MANY)
        for b in range(low):
            lo_base[b] = lam_next[b].astype(BF16)
        for b in range(low, blocks):
            hi_next[b - low] = lam_next[b].astype(BF16)
        hi_next[blocks - low] = jnp.zeros((cases, nodes), BF16)
        acc_rim[...] = jnp.zeros(acc_rim.shape, F32)
        run(lists, counts, [((0, 0), hi_next, own, acc_rim), ((1, 0), hi_next, other, acc_rim)], FEW)
        node = lax.broadcasted_iota(jnp.int32, (nodes, heads), 0)
        vertex_next, owner_next, bus_next = (theirs[:, i * heads : (i + 1) * heads] for i in range(3))
        head_next = jnp.zeros((cases, heads), F32)
        for b in range(low):
            hot_next = jnp.where(node + b * nodes == vertex_next, 1.0, 0.0).astype(BF16)
            head_next += jnp.dot(left[b], hot_next, preferred_element_type=F32)
        row = lax.broadcasted_iota(jnp.int32, (rows_sent, heads), 0)
        dest = rows_of(owner[...])
        followed = lax.axis_index("blk") < owners - 1
        dest_next = jnp.where(followed, rows_of(owner_next) + 2 * slots, -1)
        width = (nodes - cases, heads)
        pairs = [
            (dest, head0[...], head_values(lo, hi, hot)),
            (
                dest + slots,
                head_values(lo_base, hi_next, hot),
                jnp.broadcast_to((bus[...] + 1).astype(F32), width).astype(BF16),
            ),
            (
                dest_next,
                head_next.astype(BF16),
                jnp.broadcast_to((bus_next + 1).astype(F32), width).astype(BF16),
            ),
        ]
        total = jnp.zeros((rows_sent, nodes), F32)
        for where, upper_half, lower_half in pairs:
            place = jnp.where(row == where, 1.0, 0.0).astype(BF16)
            total += lax.dot_general(
                place,
                jnp.concatenate([upper_half, lower_half], axis=0),
                (((1,), (1,)), ((), ())),
                preferred_element_type=F32,
            )
        sent[...] = total.astype(BF16)
        copy.wait()

    def fetch(lists, counts, side, kind, source, dest, first, sem):
        def one(i, carry):
            c = lists[side][kind * STRIDE + i]
            pltpu.make_async_copy(source.at[c & 255], dest.at[first + i], sem).start()
            return carry

        lax.fori_loop(0, counts[side][kind], one, 0)

    def fetched(counts, side, kind, source, dest, sem):
        def one(i, carry):
            pltpu.make_async_copy(source.at[0], dest.at[0], sem).wait()
            return carry

        lax.fori_loop(0, counts[side][kind], one, 0)

    def run_fetched(lists, counts, side, kind, lam, source, first, acc, width):
        def some(i, carry):
            words = []
            for u in range(width):
                at = jnp.minimum(i * width + u, counts[side][kind] - 1)
                words.append((lists[side][kind * STRIDE + i * width + u], first + at))
            prods = [
                jnp.dot(lam[(c >> 8) & 255], source[at], preferred_element_type=F32)
                for c, at in words
            ]
            for (c, _), prod in zip(words, prods):
                acc[(c >> 16) & 255] += prod
            return carry

        lax.fori_loop(0, (counts[side][kind] + width - 1) // width, some, 0)

    tiles = [(own, VM), (other, VM)]
    rim_type = array((rim, cases, nodes), BF16)
    low_type = array(half, F32)
    sums = pltpu.VMEM((rim, cases, nodes), F32)
    assert STEPS == 3
    hi = hi_next
    leaving, low_rows, lo = kernel(
        with_lists(rim_body),
        (rim_type, low_type, array(padded, BF16)),
        listed + [(arriving, VM), (lam, VM), (acc_rim, VM)] + tiles,
        scratch=[sums],
    )
    arriving = lax.ppermute(leaving, "blk", onward)
    lam, acc_rim, hi_next, sent, icar = kernel(
        with_lists(main_body),
        (
            array(state, F32),
            array((rim, cases, nodes), F32),
            array(padded, BF16),
            array((rows_sent, nodes), BF16),
            hbm_array(state, F32),
        ),
        listed
        + [
            (distribution_entry_holder.reshape(1, heads), VM),
            (distribution_entry_substation.reshape(1, heads), VM),
            (theirs, VM),
            (leaving, VM),
        ]
        + [(low_rows, VM), (lam, VM), (lo, VM), (hi, VM), (acc, VM), (icar, VM)]
        + tiles
        + [(hot, VM), (head0, VM), (decay, VM), (inflow, VM)],
        scratch=[
            pltpu.VMEM(state, F32),
            pltpu.VMEM(half, BF16),
            pltpu.SemaphoreType.DMA,
        ],
        out_specs=(VM,) * 4 + (HB,),
    )
    received = lax.all_to_all(
        sent.reshape(network, 3 * slots, nodes),
        ("sec", "blk"),
        split_axis=0,
        concat_axis=0,
        tiled=True,
    )
    received = received.reshape(rows_sent, nodes)
    stored_in = [(derivative_tiles, HB), (other_kept, HB)]
    fetched_shape = (2 * stored, nodes, nodes)
    leaving, low_rows, lo = kernel(
        with_lists(rim_last_body),
        (rim_type, low_type, array(padded, BF16)),
        listed + [(arriving, VM), (lam, VM), (acc_rim, VM)] + stored_in,
        scratch=[sums, pltpu.VMEM(fetched_shape, BF16), pltpu.SemaphoreType.DMA((2,))],
    )
    arriving = lax.ppermute(leaving, "blk", onward)

    def main_last_body(
        lists, counts, low_rows, lam, lo, hi, decay, inflow, outflow, own_in, other_in, icar_in,
        lam_out, low_next, icar_out, lam_next, icar, own, other, sems,
    ):
        copies = [
            pltpu.make_async_copy(icar_in, icar, sems.at[0]),
            pltpu.make_async_copy(own_in, own, sems.at[1]),
            pltpu.make_async_copy(other_in, other, sems.at[2]),
        ]
        for copy in copies:
            copy.start()
        copies[0].wait()
        for b in range(blocks):
            row = low_rows[b] if b < low else lam[b]
            before = icar[b]
            lam_next[b] = outflow[b : b + 1, :] * before
            icar[b] = decay[b : b + 1, :] * before + inflow[b : b + 1, :] * row
        icar_copy = pltpu.make_async_copy(icar, icar_out, sems.at[0])
        icar_copy.start()
        copies[1].wait()
        copies[2].wait()
        run(lists, counts, [((0, 2), hi, own, lam_next), ((1, 2), hi, other, lam_next)], MANY)
        run(lists, counts, [((0, 3), lo, own, lam_next), ((1, 3), lo, other, lam_next)], MANY)
        upper = pl.ds(low, blocks - low)
        lam_copy = pltpu.make_async_copy(lam_next.at[upper], lam_out.at[upper], sems.at[1])
        lam_copy.start()
        low_next[...] = lam_next[:low]
        icar_copy.wait()
        lam_copy.wait()

    lam, low_next, icar = kernel(
        with_lists(main_last_body),
        (hbm_array(state, F32), low_type, hbm_array(state, F32)),
        listed
        + [(low_rows, VM), (lam, VM), (lo, VM), (hi_next, VM)]
        + [(decay, VM), (inflow, VM), (outflow, VM)]
        + stored_in
        + [(icar, HB)],
        scratch=[
            pltpu.VMEM(state, F32),
            pltpu.VMEM(state, F32),
            pltpu.VMEM(own.shape, BF16),
            pltpu.VMEM(own.shape, BF16),
            pltpu.SemaphoreType.DMA((3,)),
        ],
        out_specs=(HB, VM, HB),
    )

    def trans_body(received, trans_in, matrix_in, out, trans, matrix, sems):
        copies = [
            pltpu.make_async_copy(trans_in, trans, sems.at[0]),
            pltpu.make_async_copy(matrix_in, matrix, sems.at[1]),
        ]
        for copy in copies:
            copy.start()
        dims = (((0,), (0,)), ((), ()))
        if slots % 16 == 0:
            parts = received[...].reshape(network, 3, slots, nodes)
            part = [parts[:, i].reshape(network * slots, nodes) for i in range(3)]
            column = lax.broadcasted_iota(jnp.int32, (network * slots, buses), 1)

            def hot_of(rows):
                label = rows[:, cases : cases + 1].astype(F32).astype(jnp.int32) - 1
                return jnp.where(label == column, 1.0, 0.0).astype(BF16)

            hot = hot_of(part[1])
            first = lax.dot_general(part[0], hot, dims, preferred_element_type=F32)
            last = lax.dot_general(part[1], hot, dims, preferred_element_type=F32)
            last += lax.dot_general(part[2], hot_of(part[2]), dims, preferred_element_type=F32)
        else:
            got = received[...].astype(F32)
            row = lax.broadcasted_iota(jnp.int32, (rows_sent, buses), 0)
            place = lax.rem(row, 3 * slots)
            column = lax.broadcasted_iota(jnp.int32, (rows_sent, buses), 1)
            label = got[:, cases : cases + 1].astype(jnp.int32) - 1
            hot = jnp.where(jnp.logical_and(label == column, place >= slots), 1.0, 0.0)
            own_hot = jnp.where(place < 2 * slots, hot, 0.0)
            hot_a = pltpu.roll(own_hot, rows_sent - slots, 0).astype(BF16)
            first = lax.dot_general(received[...], hot_a, dims, preferred_element_type=F32)
            last = lax.dot_general(
                received[...], hot.astype(BF16), dims, preferred_element_type=F32
            )
        for copy in copies:
            copy.wait()
        value = trans[...]
        for inj in (first[:cases], first[cases:], last[:cases]):
            value = jnp.dot(value.astype(BF16), matrix[...], preferred_element_type=F32) + inj
        out[...] = value

    (trans,) = kernel(
        trans_body,
        (array(highvoltage_costate.shape, F32),),
        [(received, VM), (highvoltage_costate, HB), (highvoltage_derivative_matrix, HB)],
        scratch=[
            pltpu.VMEM(highvoltage_costate.shape, F32),
            pltpu.VMEM(highvoltage_derivative_matrix.shape, BF16),
            pltpu.SemaphoreType.DMA((2,)),
        ],
    )

    def last_body(arrived, low_next, lam_in, lam_out, rows, sems):
        del lam_in
        keep = lax.axis_index("blk") > 0
        copies = []
        part = low // 4
        for i in range(4):
            for b in range(i * part, (i + 1) * part):
                rows[b] = low_next[b] + jnp.where(keep, arrived[b].astype(F32), 0.0)
            here = pl.ds(i * part, part)
            copies.append(pltpu.make_async_copy(rows.at[here], lam_out.at[here], sems.at[i]))
            copies[-1].start()
        for copy in copies:
            copy.wait()

    (lam,) = kernel(
        last_body,
        (array(state, F32),),
        [(arriving, VM), (low_next, VM), (lam, HB)],
        scratch=[pltpu.VMEM(half, F32), pltpu.SemaphoreType.DMA((4,))],
        out_specs=(HB,),
        aliases={2: 0},
    )
    return (lam, icar, trans)


def solution(mesh):
    placed = (
        P(("sec", "blk"), "case", None),
        P(("sec", "blk"), "case", None),
        P("case", ("sec", "blk")),
        P(("sec", "blk", "case"), None, None),
        P(("sec", "blk", "case")),
        P(("sec", "blk", "case")),
        P(("sec", "blk"), None),
        P(("sec", "blk"), None),
        P(("sec", "blk"), None),
        P(("sec", "blk")),
        P(("sec", "blk"), None),
        P(("sec", "blk")),
        P(("sec", "blk"), None),
    )

    return jax.shard_map(
        local,
        mesh=mesh,
        in_specs=placed,
        out_specs=(
            P(("sec", "blk"), "case", None),
            P(("sec", "blk"), "case", None),
            P("case", ("sec", "blk")),
        ),
        check_vma=False,
    )
```

```python
import jax
import jax.numpy as jnp
from jax import lax
from jax.experimental import pallas as pl
from jax.experimental.pallas import tpu as pltpu
from jax.sharding import PartitionSpec as P


STEPS = 3
UNROLL = 16
FEW = 24
MANY = 40
CLASSES = 4
VMEM_LIMIT = 24 << 20

F32 = jnp.float32
BF16 = jnp.bfloat16
VM = pl.BlockSpec(memory_space=pltpu.VMEM)
SM = pl.BlockSpec(memory_space=pltpu.SMEM)
HB = pl.BlockSpec(memory_space=pltpu.HBM)
STRIDE = 128


def kernel(body, outs, ins, scratch=(), out_specs=None, aliases=None):
    return pl.pallas_call(
        body,
        out_shape=outs,
        in_specs=[spec for _, spec in ins],
        out_specs=out_specs or tuple(VM for _ in outs),
        scratch_shapes=list(scratch),
        input_output_aliases=aliases or {},
        compiler_params=pltpu.CompilerParams(vmem_limit_bytes=VMEM_LIMIT),
    )(*[in_hbm(array) if spec is HB else array for array, spec in ins])


def with_lists(body):
    return lambda own, other, *refs: body((own, other), *refs)


def in_hbm(array):
    return pltpu.with_memory_space_constraint(array, pltpu.HBM)


def array(shape, dtype):
    return jax.ShapeDtypeStruct(shape, dtype)


def hbm_array(shape, dtype):
    return pltpu.HBM(shape, dtype)


def local(
    vertex_costate,
    inverter_costate,
    highvoltage_costate,
    derivative_tiles,
    tile_source_index,
    tile_target_index,
    inverter_decay_factor,
    costate_to_inverter_factor,
    inverter_to_costate_factor,
    distribution_entry_vertex,
    distribution_entry_holder,
    distribution_entry_substation,
    highvoltage_derivative_matrix,
):
    blocks, cases, nodes = vertex_costate.shape
    rim = blocks // 2
    low = blocks // 2
    targets = blocks + rim
    stored = derivative_tiles.shape[0]
    sections = lax.axis_size("sec")
    owners = lax.axis_size("blk")
    network = sections * owners
    heads = distribution_entry_vertex.shape[0]
    slots = max(2, 2 * heads // network)
    buses = highvoltage_derivative_matrix.shape[1]
    rows_sent = network * 3 * slots
    assert -(-stored // MANY) * MANY <= STRIDE and -(-stored // FEW) * FEW <= STRIDE

    state = (blocks, cases, nodes)
    half = (low, cases, nodes)
    padded = (low + 1, cases, nodes)
    acc_shape = (targets, cases, nodes)
    hot_shape = (blocks, nodes, heads)
    factor_shape = inverter_decay_factor.shape
    swap = [(0, 1), (1, 0)]
    onward = [(i, (i + 1) % owners) for i in range(owners)]
    backward = [(j, i) for i, j in onward]

    own = derivative_tiles
    other_rows = lax.ppermute(tile_source_index, "case", swap)
    other_columns = lax.ppermute(tile_target_index, "case", swap)
    other = lax.ppermute(own, "case", swap)

    def sorted_list(rows, columns):
        is_low = jnp.where(rows < low, 1, 0)
        is_own = jnp.where(columns < blocks, 1, 0)
        kind = 2 * is_own + is_low
        place = lax.broadcasted_iota(jnp.int32, (1, stored), 1)
        word = place | ((rows - low * (1 - is_low)) << 8) | ((columns - blocks * (1 - is_own)) << 16)
        kind_row = jnp.broadcast_to(kind.astype(F32), (stored, stored))
        word_row = jnp.broadcast_to(word.astype(F32), (stored, stored))
        earlier = lax.broadcasted_iota(jnp.int32, (stored, stored), 0) > lax.broadcasted_iota(
            jnp.int32, (stored, stored), 1
        )
        kind_col = kind_row.T
        same = jnp.logical_and(kind_col == kind_row, earlier)
        rank = jnp.sum(jnp.where(same, 1.0, 0.0), axis=1, keepdims=True)
        spot = (kind_col[:, :1] * STRIDE + rank).astype(jnp.int32)
        hit = lax.broadcasted_iota(jnp.int32, (stored, CLASSES * STRIDE), 1) == spot
        words = jnp.sum(jnp.where(hit, word_row.T[:, :1], 0.0), axis=0, keepdims=True)
        taken = jnp.sum(jnp.where(hit, 1.0, 0.0), axis=0, keepdims=True)
        idle = jnp.full((1, CLASSES * STRIDE), low << 8, jnp.int32)
        lane = lax.broadcasted_iota(jnp.int32, (stored, 128), 1).astype(F32)
        counts = jnp.sum(jnp.where(kind_col[:, :1] == lane, 1.0, 0.0), axis=0, keepdims=True)
        return jnp.concatenate(
            [jnp.where(taken > 0, words.astype(jnp.int32), idle), counts.astype(jnp.int32)], axis=1
        )

    def word_of(lists, side, kind, i):
        return lists[side][0, kind * STRIDE + i]

    def count_of(lists, side, kind):
        return lists[side][0, CLASSES * STRIDE + kind]

    list_type = array((1, CLASSES * STRIDE + 128), jnp.int32)

    def run(lists, parts, width):
        def some(i, carry):
            words = [
                (word_of(lists, side, kind, i * width + u), lam, tiles, acc)
                for (side, kind), lam, tiles, acc in parts
                for u in range(width)
            ]
            prods = [
                jnp.dot(lam[(c >> 8) & 255], tiles[c & 255], preferred_element_type=F32)
                for c, lam, tiles, _ in words
            ]
            for (c, _, _, acc), prod in zip(words, prods):
                acc[c >> 16] += prod
            return carry

        longest = 0
        for (side, kind), _, _, _ in parts:
            longest = jnp.maximum(longest, count_of(lists, side, kind))
        lax.fori_loop(0, (longest + width - 1) // width, some, 0)

    def first_body(
        rows, columns, rows_in, columns_in, lam_in, own_in, acc, lo, hi, own_kept, listed,
        lam, lam_bf, rows_kept, columns_kept, sems,
    ):
        chunks = stored // UNROLL
        early = [
            pltpu.make_async_copy(rows_in, rows_kept, sems.at[chunks]),
            pltpu.make_async_copy(columns_in, columns_kept, sems.at[chunks + 1]),
            pltpu.make_async_copy(lam_in, lam, sems.at[chunks + 2]),
        ]
        copies = [
            pltpu.make_async_copy(
                own_in.at[pl.ds(i * UNROLL, UNROLL)], own_kept.at[pl.ds(i * UNROLL, UNROLL)], sems.at[i]
            )
            for i in range(chunks)
        ]
        for copy in early + copies:
            copy.start()
        for b in range(targets):
            acc[b] = jnp.zeros((cases, nodes), F32)
        zero = jnp.zeros((cases, nodes), BF16)
        lo[low] = zero
        hi[blocks - low] = zero
        early[0].wait()
        early[1].wait()
        listed[...] = sorted_list(rows_kept[...], columns_kept[...])
        early[2].wait()
        for b in range(blocks):
            rounded = lam[b].astype(BF16)
            lam_bf[b] = rounded
            if b < low:
                lo[b] = rounded
            else:
                hi[b - low] = rounded
        for i, copy in enumerate(copies):
            copy.wait()
            prods = [
                jnp.dot(
                    lam_bf[rows[i * UNROLL + u]],
                    own_kept[i * UNROLL + u],
                    preferred_element_type=F32,
                )
                for u in range(UNROLL)
            ]
            for u, prod in enumerate(prods):
                acc[columns[i * UNROLL + u]] += prod

    acc, lo, hi, own, own_list = kernel(
        first_body,
        (
            array(acc_shape, F32),
            array(padded, BF16),
            array(padded, BF16),
            array(own.shape, BF16),
            list_type,
        ),
        [
            (tile_source_index, SM),
            (tile_target_index, SM),
            (tile_source_index.reshape(1, stored), HB),
            (tile_target_index.reshape(1, stored), HB),
            (vertex_costate, HB),
            (own, HB),
        ],
        scratch=[
            pltpu.VMEM(state, F32),
            pltpu.VMEM(state, BF16),
            pltpu.VMEM((1, stored), jnp.int32),
            pltpu.VMEM((1, stored), jnp.int32),
            pltpu.SemaphoreType.DMA((stored // UNROLL + 3,)),
        ],
    )

    def sort_body(rows, columns, listed):
        listed[...] = sorted_list(rows[...], columns[...])

    (other_list,) = kernel(
        sort_body,
        (list_type,),
        [(other_rows.reshape(1, stored), VM), (other_columns.reshape(1, stored), VM)],
    )
    listed = [(own_list, SM), (other_list, SM)]

    def rim_first_body(lists, acc, lo, hi, other, out, sums):
        sums[...] = acc[blocks:]
        run(
            lists,
            [((1, 0), hi, other, sums), ((1, 1), lo, other, sums)],
            FEW,
        )
        out[...] = sums[...].astype(BF16)

    (leaving,) = kernel(
        with_lists(rim_first_body),
        (array((rim, cases, nodes), BF16),),
        listed + [(acc, VM), (lo, VM), (hi, VM), (other, VM)],
        scratch=[pltpu.VMEM((rim, cases, nodes), F32)],
    )
    arriving = lax.ppermute(leaving, "blk", onward)

    mine = jnp.concatenate(
        [
            distribution_entry_vertex.reshape(1, heads),
            distribution_entry_holder.reshape(1, heads),
            distribution_entry_substation.reshape(1, heads),
        ],
        axis=1,
    )
    theirs = lax.ppermute(mine, "blk", backward)

    def begin_next(lists, lam, icar, outflow, own, other, acc, acc_rim, hi):
        for b in range(blocks):
            acc[b] = outflow[b : b + 1, :] * icar[b]
        for b in range(rim):
            acc_rim[b] = jnp.zeros((cases, nodes), F32)
        for b in range(low, blocks):
            hi[b - low] = lam[b].astype(BF16)
        hi[blocks - low] = jnp.zeros((cases, nodes), BF16)
        run(lists, [((0, 0), hi, own, acc_rim), ((1, 0), hi, other, acc_rim)], FEW)
        run(lists, [((0, 2), hi, own, acc), ((1, 2), hi, other, acc)], MANY)

    def head_values(lo, hi, hot):
        total = jnp.dot(lo[0], hot[0], preferred_element_type=F32)
        for b in range(1, blocks):
            row = lo[b] if b < low else hi[b - low]
            total += jnp.dot(row, hot[b], preferred_element_type=F32)
        return total.astype(BF16)

    def main_first_body(
        lists, acc, lo, hi, own, other, vertex, lam_in, icar_in, decay_in, inflow_in, outflow_in,
        lam_next, acc_next, acc_rim, hi_next, icar_next, head, hot, decay, inflow, outflow, other_kept,
        lam, icar, sems,
    ):
        pairs = [
            (icar_in, icar), (outflow_in, outflow), (lam_in, lam), (decay_in, decay), (inflow_in, inflow)
        ]
        copies = [pltpu.make_async_copy(a, b, sems.at[i]) for i, (a, b) in enumerate(pairs)]
        kept = pltpu.make_async_copy(other, other_kept, sems.at[5])
        for copy in copies + [kept]:
            copy.start()
        lam_next[...] = acc[:blocks]
        run(
            lists,
            [((1, 2), hi, other, lam_next), ((1, 3), lo, other, lam_next)],
            MANY,
        )
        for copy in copies:
            copy.wait()
        for b in range(blocks):
            lam_next[b] += outflow[b : b + 1, :] * icar[b]
            icar_next[b] = decay[b : b + 1, :] * icar[b] + inflow[b : b + 1, :] * lam[b]
        begin_next(
            lists, lam_next, icar_next, outflow, own, other, acc_next, acc_rim, hi_next
        )
        node = lax.broadcasted_iota(jnp.int32, (nodes, heads), 0)
        for b in range(blocks):
            hot[b] = jnp.where(node + b * nodes == vertex[...], 1.0, 0.0).astype(BF16)
        head[...] = head_values(lo, hi, hot)
        kept.wait()

    factor = array(factor_shape, F32)
    lam, acc, acc_rim, hi_next, icar, head0, hot, decay, inflow, outflow, other_kept = kernel(
        with_lists(main_first_body),
        (
            array(state, F32),
            array(state, F32),
            array((rim, cases, nodes), F32),
            array(padded, BF16),
            array(state, F32),
            array((cases, heads), BF16),
            array(hot_shape, BF16),
            factor,
            factor,
            factor,
            hbm_array(other.shape, BF16),
        ),
        listed
        + [(acc, VM), (lo, VM), (hi, VM), (own, VM), (other, VM)]
        + [(distribution_entry_vertex.reshape(1, heads), VM)]
        + [(vertex_costate, HB), (inverter_costate, HB), (inverter_decay_factor, HB)]
        + [(costate_to_inverter_factor, HB), (inverter_to_costate_factor, HB)],
        scratch=[pltpu.VMEM(state, F32), pltpu.VMEM(state, F32), pltpu.SemaphoreType.DMA((6,))],
        out_specs=(VM,) * 10 + (HB,),
    )

    def take_arrived(arrived, lam, low_rows, lo):
        keep = lax.axis_index("blk") > 0
        for b in range(low):
            row = lam[b] + jnp.where(keep, arrived[b].astype(F32), 0.0)
            low_rows[b] = row
            lo[b] = row.astype(BF16)
        lo[low] = jnp.zeros((cases, nodes), BF16)

    def rim_sums(lists, acc_rim, lo, own, other, out, sums):
        sums[...] = acc_rim[...]
        run(lists, [((0, 1), lo, own, sums), ((1, 1), lo, other, sums)], FEW)
        out[...] = sums[...].astype(BF16)

    def rim_body(lists, arrived, lam, acc_rim, own, other, out, low_rows, lo, sums):
        take_arrived(arrived, lam, low_rows, lo)
        rim_sums(lists, acc_rim, lo, own, other, out, sums)

    def rim_last_body(
        lists, arrived, lam, acc_rim, own_in, other_in, out, low_rows, lo, sums, ready, sems
    ):
        sources = (own_in, other_in)
        for side in (0, 1):
            fetch(lists, side, 1, sources[side], ready, side * stored, sems.at[side])
        take_arrived(arrived, lam, low_rows, lo)
        sums[...] = acc_rim[...]
        for side in (0, 1):
            fetched(lists, side, 1, sources[side], ready, sems.at[side])
            run_fetched(lists, side, 1, lo, ready, side * stored, sums, FEW)
        out[...] = sums[...].astype(BF16)

    def rows_of(owner):
        names = jnp.broadcast_to(owner.astype(F32), (heads, heads))
        before = lax.broadcasted_iota(jnp.int32, (heads, heads), 0)
        after = lax.broadcasted_iota(jnp.int32, (heads, heads), 1)
        same = jnp.logical_and(names.T == names, before < after)
        slot = jnp.sum(jnp.where(same, 1.0, 0.0), axis=0, keepdims=True).astype(jnp.int32)
        return owner * slots + slot

    def main_body(
        lists, owner, bus, theirs, left,
        low_rows, lam, lo, hi, acc, icar, own, other, hot, head0, decay, inflow,
        lam_next, acc_rim, hi_next, sent, icar_out, icar_next, lo_base, sem,
    ):
        for b in range(blocks):
            row = low_rows[b] if b < low else lam[b]
            icar_next[b] = decay[b : b + 1, :] * icar[b] + inflow[b : b + 1, :] * row
        copy = pltpu.make_async_copy(icar_next, icar_out, sem)
        copy.start()
        lam_next[...] = acc[...]
        run(lists, [((0, 3), lo, own, lam_next), ((1, 3), lo, other, lam_next)], MANY)
        for b in range(low):
            lo_base[b] = lam_next[b].astype(BF16)
        for b in range(low, blocks):
            hi_next[b - low] = lam_next[b].astype(BF16)
        hi_next[blocks - low] = jnp.zeros((cases, nodes), BF16)
        acc_rim[...] = jnp.zeros(acc_rim.shape, F32)
        run(lists, [((0, 0), hi_next, own, acc_rim), ((1, 0), hi_next, other, acc_rim)], FEW)
        node = lax.broadcasted_iota(jnp.int32, (nodes, heads), 0)
        vertex_next, owner_next, bus_next = (theirs[:, i * heads : (i + 1) * heads] for i in range(3))
        head_next = jnp.zeros((cases, heads), F32)
        for b in range(low):
            hot_next = jnp.where(node + b * nodes == vertex_next, 1.0, 0.0).astype(BF16)
            head_next += jnp.dot(left[b], hot_next, preferred_element_type=F32)
        dest = rows_of(owner[...])
        followed = lax.axis_index("blk") < owners - 1
        dest_next = jnp.where(followed, rows_of(owner_next), -1)
        width = (nodes - cases, heads)
        label = jnp.broadcast_to((bus[...] + 1).astype(F32), width).astype(BF16)
        label_next = jnp.broadcast_to((bus_next + 1).astype(F32), width).astype(BF16)
        pairs = [
            (dest, head0[...], head_values(lo, hi, hot)),
            (dest, head_values(lo_base, hi_next, hot), label),
            (dest_next, head_next.astype(BF16), label_next),
        ]
        row = lax.broadcasted_iota(jnp.int32, (network * slots, heads), 0)
        for i, (where, first_half, second_half) in enumerate(pairs):
            place = jnp.where(row == where, 1.0, 0.0).astype(BF16)
            part = lax.dot_general(
                place,
                jnp.concatenate([first_half, second_half], axis=0),
                (((1,), (1,)), ((), ())),
                preferred_element_type=F32,
            )
            sent[:, i] = part.astype(BF16).reshape(network, slots, nodes)
        copy.wait()

    def fetch(lists, side, kind, source, dest, first, sem):
        def one(i, carry):
            c = word_of(lists, side, kind, i)
            pltpu.make_async_copy(source.at[c & 255], dest.at[first + i], sem).start()
            return carry

        lax.fori_loop(0, count_of(lists, side, kind), one, 0)

    def fetched(lists, side, kind, source, dest, sem):
        def one(i, carry):
            pltpu.make_async_copy(source.at[0], dest.at[0], sem).wait()
            return carry

        lax.fori_loop(0, count_of(lists, side, kind), one, 0)

    def run_fetched(lists, side, kind, lam, source, first, acc, width):
        def some(i, carry):
            words = []
            for u in range(width):
                at = jnp.minimum(i * width + u, count_of(lists, side, kind) - 1)
                words.append((word_of(lists, side, kind, i * width + u), first + at))
            prods = [
                jnp.dot(lam[(c >> 8) & 255], source[at], preferred_element_type=F32)
                for c, at in words
            ]
            for (c, _), prod in zip(words, prods):
                acc[c >> 16] += prod
            return carry

        lax.fori_loop(0, (count_of(lists, side, kind) + width - 1) // width, some, 0)

    tiles = [(own, VM), (other, VM)]
    rim_type = array((rim, cases, nodes), BF16)
    low_type = array(half, F32)
    sums = pltpu.VMEM((rim, cases, nodes), F32)
    assert STEPS == 3
    hi = hi_next
    leaving, low_rows, lo = kernel(
        with_lists(rim_body),
        (rim_type, low_type, array(padded, BF16)),
        listed + [(arriving, VM), (lam, VM), (acc_rim, VM)] + tiles,
        scratch=[sums],
    )
    arriving = lax.ppermute(leaving, "blk", onward)
    lam, acc_rim, hi_next, sent, icar = kernel(
        with_lists(main_body),
        (
            array(state, F32),
            array((rim, cases, nodes), F32),
            array(padded, BF16),
            array((network, 3, slots, nodes), BF16),
            hbm_array(state, F32),
        ),
        listed
        + [
            (distribution_entry_holder.reshape(1, heads), VM),
            (distribution_entry_substation.reshape(1, heads), VM),
            (theirs, VM),
            (leaving, VM),
        ]
        + [(low_rows, VM), (lam, VM), (lo, VM), (hi, VM), (acc, VM), (icar, VM)]
        + tiles
        + [(hot, VM), (head0, VM), (decay, VM), (inflow, VM)],
        scratch=[
            pltpu.VMEM(state, F32),
            pltpu.VMEM(half, BF16),
            pltpu.SemaphoreType.DMA,
        ],
        out_specs=(VM,) * 4 + (HB,),
    )
    received = lax.all_to_all(
        sent.reshape(network, 3 * slots, nodes),
        ("sec", "blk"),
        split_axis=0,
        concat_axis=0,
        tiled=True,
    )
    received = received.reshape(rows_sent, nodes)
    stored_in = [(derivative_tiles, HB), (other_kept, HB)]
    fetched_shape = (2 * stored, nodes, nodes)
    leaving, low_rows, lo = kernel(
        with_lists(rim_last_body),
        (rim_type, low_type, array(padded, BF16)),
        listed + [(arriving, VM), (lam, VM), (acc_rim, VM)] + stored_in,
        scratch=[sums, pltpu.VMEM(fetched_shape, BF16), pltpu.SemaphoreType.DMA((2,))],
    )
    arriving = lax.ppermute(leaving, "blk", onward)

    def main_last_body(
        lists, low_rows, lam, lo, hi, decay, inflow, outflow, own, other, icar,
        lam_out, low_next, icar_out, lam_next, icar_next, sems,
    ):
        for b in range(blocks):
            row = low_rows[b] if b < low else lam[b]
            before = icar[b]
            lam_next[b] = outflow[b : b + 1, :] * before
            icar_next[b] = decay[b : b + 1, :] * before + inflow[b : b + 1, :] * row
        icar_copy = pltpu.make_async_copy(icar_next, icar_out, sems.at[0])
        icar_copy.start()
        run(lists, [((0, 2), hi, own, lam_next), ((1, 2), hi, other, lam_next)], MANY)
        run(lists, [((0, 3), lo, own, lam_next), ((1, 3), lo, other, lam_next)], MANY)
        upper = pl.ds(low, blocks - low)
        lam_copy = pltpu.make_async_copy(lam_next.at[upper], lam_out.at[upper], sems.at[1])
        lam_copy.start()
        low_next[...] = lam_next[:low]
        icar_copy.wait()
        lam_copy.wait()

    lam, low_next, icar = kernel(
        with_lists(main_last_body),
        (hbm_array(state, F32), low_type, hbm_array(state, F32)),
        listed
        + [(low_rows, VM), (lam, VM), (lo, VM), (hi_next, VM)]
        + [(decay, VM), (inflow, VM), (outflow, VM)]
        + [(derivative_tiles, VM), (other_kept, VM), (icar, VM)],
        scratch=[
            pltpu.VMEM(state, F32),
            pltpu.VMEM(state, F32),
            pltpu.SemaphoreType.DMA((2,)),
        ],
        out_specs=(HB, VM, HB),
    )

    def trans_body(received, trans_in, matrix_in, out, trans, matrix, sems):
        copies = [
            pltpu.make_async_copy(trans_in, trans, sems.at[0]),
            pltpu.make_async_copy(matrix_in, matrix, sems.at[1]),
        ]
        for copy in copies:
            copy.start()
        dims = (((0,), (0,)), ((), ()))
        if slots % 16 == 0:
            parts = received[...].reshape(network, 3, slots, nodes)
            part = [parts[:, i].reshape(network * slots, nodes) for i in range(3)]
            column = lax.broadcasted_iota(jnp.int32, (network * slots, buses), 1)

            def hot_of(rows):
                label = rows[:, cases : cases + 1].astype(F32).astype(jnp.int32) - 1
                return jnp.where(label == column, 1.0, 0.0).astype(BF16)

            hot = hot_of(part[1])
            first = lax.dot_general(part[0], hot, dims, preferred_element_type=F32)
            last = lax.dot_general(part[1], hot, dims, preferred_element_type=F32)
            last += lax.dot_general(part[2], hot_of(part[2]), dims, preferred_element_type=F32)
        else:
            got = received[...].astype(F32)
            row = lax.broadcasted_iota(jnp.int32, (rows_sent, buses), 0)
            place = lax.rem(row, 3 * slots)
            column = lax.broadcasted_iota(jnp.int32, (rows_sent, buses), 1)
            label = got[:, cases : cases + 1].astype(jnp.int32) - 1
            hot = jnp.where(jnp.logical_and(label == column, place >= slots), 1.0, 0.0)
            own_hot = jnp.where(place < 2 * slots, hot, 0.0)
            hot_a = pltpu.roll(own_hot, rows_sent - slots, 0).astype(BF16)
            first = lax.dot_general(received[...], hot_a, dims, preferred_element_type=F32)
            last = lax.dot_general(
                received[...], hot.astype(BF16), dims, preferred_element_type=F32
            )
        for copy in copies:
            copy.wait()
        value = trans[...]
        for inj in (first[:cases], first[cases:], last[:cases]):
            value = jnp.dot(value.astype(BF16), matrix[...], preferred_element_type=F32) + inj
        out[...] = value

    (trans,) = kernel(
        trans_body,
        (array(highvoltage_costate.shape, F32),),
        [(received, VM), (highvoltage_costate, HB), (highvoltage_derivative_matrix, HB)],
        scratch=[
            pltpu.VMEM(highvoltage_costate.shape, F32),
            pltpu.VMEM(highvoltage_derivative_matrix.shape, BF16),
            pltpu.SemaphoreType.DMA((2,)),
        ],
    )

    def last_body(arrived, low_next, lam_in, lam_out, rows, sems):
        del lam_in
        keep = lax.axis_index("blk") > 0
        copies = []
        part = low // 4
        for i in range(4):
            for b in range(i * part, (i + 1) * part):
                rows[b] = low_next[b] + jnp.where(keep, arrived[b].astype(F32), 0.0)
            here = pl.ds(i * part, part)
            copies.append(pltpu.make_async_copy(rows.at[here], lam_out.at[here], sems.at[i]))
            copies[-1].start()
        for copy in copies:
            copy.wait()

    (lam,) = kernel(
        last_body,
        (array(state, F32),),
        [(arriving, VM), (low_next, VM), (lam, HB)],
        scratch=[pltpu.VMEM(half, F32), pltpu.SemaphoreType.DMA((4,))],
        out_specs=(HB,),
        aliases={2: 0},
    )
    return (lam, icar, trans)


def solution(mesh):
    placed = (
        P(("sec", "blk"), "case", None),
        P(("sec", "blk"), "case", None),
        P("case", ("sec", "blk")),
        P(("sec", "blk", "case"), None, None),
        P(("sec", "blk", "case")),
        P(("sec", "blk", "case")),
        P(("sec", "blk"), None),
        P(("sec", "blk"), None),
        P(("sec", "blk"), None),
        P(("sec", "blk")),
        P(("sec", "blk"), None),
        P(("sec", "blk")),
        P(("sec", "blk"), None),
    )

    return jax.shard_map(
        local,
        mesh=mesh,
        in_specs=placed,
        out_specs=(
            P(("sec", "blk"), "case", None),
            P(("sec", "blk"), "case", None),
            P("case", ("sec", "blk")),
        ),
        check_vma=False,
    )
```

```python
import jax
import jax.numpy as jnp
from jax import lax
from jax.experimental import pallas as pl
from jax.experimental.pallas import tpu as pltpu
from jax.sharding import PartitionSpec as P


STEPS = 3
UNROLL = 16
FEW = 24
MANY = 40
KEEP = 44
CLASSES = 4
VMEM_LIMIT = 24 << 20

F32 = jnp.float32
BF16 = jnp.bfloat16
VM = pl.BlockSpec(memory_space=pltpu.VMEM)
SM = pl.BlockSpec(memory_space=pltpu.SMEM)
HB = pl.BlockSpec(memory_space=pltpu.HBM)
STRIDE = 128


def kernel(body, outs, ins, scratch=(), out_specs=None, aliases=None):
    return pl.pallas_call(
        body,
        out_shape=outs,
        in_specs=[spec for _, spec in ins],
        out_specs=out_specs or tuple(VM for _ in outs),
        scratch_shapes=list(scratch),
        input_output_aliases=aliases or {},
        compiler_params=pltpu.CompilerParams(vmem_limit_bytes=VMEM_LIMIT),
    )(*[in_hbm(array) if spec is HB else array for array, spec in ins])


def with_lists(body):
    return lambda own, other, *refs: body((own, other), *refs)


def in_hbm(array):
    return pltpu.with_memory_space_constraint(array, pltpu.HBM)


def array(shape, dtype):
    return jax.ShapeDtypeStruct(shape, dtype)


def hbm_array(shape, dtype):
    return pltpu.HBM(shape, dtype)


def local(
    vertex_costate,
    inverter_costate,
    highvoltage_costate,
    derivative_tiles,
    tile_source_index,
    tile_target_index,
    inverter_decay_factor,
    costate_to_inverter_factor,
    inverter_to_costate_factor,
    distribution_entry_vertex,
    distribution_entry_holder,
    distribution_entry_substation,
    highvoltage_derivative_matrix,
):
    blocks, cases, nodes = vertex_costate.shape
    rim = blocks // 2
    low = blocks // 2
    targets = blocks + rim
    stored = derivative_tiles.shape[0]
    sections = lax.axis_size("sec")
    owners = lax.axis_size("blk")
    network = sections * owners
    heads = distribution_entry_vertex.shape[0]
    slots = max(2, 2 * heads // network)
    buses = highvoltage_derivative_matrix.shape[1]
    rows_sent = network * 3 * slots
    assert -(-stored // MANY) * MANY <= STRIDE and -(-stored // FEW) * FEW <= STRIDE

    state = (blocks, cases, nodes)
    half = (low, cases, nodes)
    padded = (low + 1, cases, nodes)
    acc_shape = (targets, cases, nodes)
    hot_shape = (blocks, nodes, heads)
    factor_shape = inverter_decay_factor.shape
    swap = [(0, 1), (1, 0)]
    onward = [(i, (i + 1) % owners) for i in range(owners)]
    backward = [(j, i) for i, j in onward]

    own = derivative_tiles
    other_rows = lax.ppermute(tile_source_index, "case", swap)
    other_columns = lax.ppermute(tile_target_index, "case", swap)
    other = lax.ppermute(own, "case", swap)

    def sorted_list(rows, columns):
        is_low = jnp.where(rows < low, 1, 0)
        is_own = jnp.where(columns < blocks, 1, 0)
        kind = 2 * is_own + is_low
        place = lax.broadcasted_iota(jnp.int32, (1, stored), 1)
        word = place | ((rows - low * (1 - is_low)) << 8) | ((columns - blocks * (1 - is_own)) << 16)
        kind_row = jnp.broadcast_to(kind.astype(F32), (stored, stored))
        word_row = jnp.broadcast_to(word.astype(F32), (stored, stored))
        earlier = lax.broadcasted_iota(jnp.int32, (stored, stored), 0) > lax.broadcasted_iota(
            jnp.int32, (stored, stored), 1
        )
        kind_col = kind_row.T
        same = jnp.logical_and(kind_col == kind_row, earlier)
        rank = jnp.sum(jnp.where(same, 1.0, 0.0), axis=1, keepdims=True)
        spot = (kind_col[:, :1] * STRIDE + rank).astype(jnp.int32)
        hit = lax.broadcasted_iota(jnp.int32, (stored, CLASSES * STRIDE), 1) == spot
        words = jnp.sum(jnp.where(hit, word_row.T[:, :1], 0.0), axis=0, keepdims=True)
        taken = jnp.sum(jnp.where(hit, 1.0, 0.0), axis=0, keepdims=True)
        idle = jnp.full((1, CLASSES * STRIDE), low << 8, jnp.int32)
        lane = lax.broadcasted_iota(jnp.int32, (stored, 128), 1).astype(F32)
        counts = jnp.sum(jnp.where(kind_col[:, :1] == lane, 1.0, 0.0), axis=0, keepdims=True)
        return jnp.concatenate(
            [jnp.where(taken > 0, words.astype(jnp.int32), idle), counts.astype(jnp.int32)], axis=1
        )

    def word_of(lists, side, kind, i):
        return lists[side][0, kind * STRIDE + i]

    def count_of(lists, side, kind):
        return lists[side][0, CLASSES * STRIDE + kind]

    list_type = array((1, CLASSES * STRIDE + 128), jnp.int32)

    def run(lists, parts, width):
        def some(i, carry):
            words = [
                (word_of(lists, side, kind, i * width + u), lam, tiles, acc)
                for (side, kind), lam, tiles, acc in parts
                for u in range(width)
            ]
            prods = [
                jnp.dot(lam[(c >> 8) & 255], tiles[c & 255], preferred_element_type=F32)
                for c, lam, tiles, _ in words
            ]
            for (c, _, _, acc), prod in zip(words, prods):
                acc[c >> 16] += prod
            return carry

        longest = 0
        for (side, kind), _, _, _ in parts:
            longest = jnp.maximum(longest, count_of(lists, side, kind))
        lax.fori_loop(0, (longest + width - 1) // width, some, 0)

    def first_body(
        rows, columns, rows_in, columns_in, lam_in, own_in, acc, lo, hi, own_kept, listed,
        lam, lam_bf, rows_kept, columns_kept, sems,
    ):
        chunks = stored // UNROLL
        early = [
            pltpu.make_async_copy(rows_in, rows_kept, sems.at[chunks]),
            pltpu.make_async_copy(columns_in, columns_kept, sems.at[chunks + 1]),
            pltpu.make_async_copy(lam_in, lam, sems.at[chunks + 2]),
        ]
        copies = [
            pltpu.make_async_copy(
                own_in.at[pl.ds(i * UNROLL, UNROLL)], own_kept.at[pl.ds(i * UNROLL, UNROLL)], sems.at[i]
            )
            for i in range(chunks)
        ]
        for copy in early + copies:
            copy.start()
        for b in range(targets):
            acc[b] = jnp.zeros((cases, nodes), F32)
        zero = jnp.zeros((cases, nodes), BF16)
        lo[low] = zero
        hi[blocks - low] = zero
        early[0].wait()
        early[1].wait()
        listed[...] = sorted_list(rows_kept[...], columns_kept[...])
        early[2].wait()
        for b in range(blocks):
            rounded = lam[b].astype(BF16)
            lam_bf[b] = rounded
            if b < low:
                lo[b] = rounded
            else:
                hi[b - low] = rounded
        for i, copy in enumerate(copies):
            copy.wait()
            prods = [
                jnp.dot(
                    lam_bf[rows[i * UNROLL + u]],
                    own_kept[i * UNROLL + u],
                    preferred_element_type=F32,
                )
                for u in range(UNROLL)
            ]
            for u, prod in enumerate(prods):
                acc[columns[i * UNROLL + u]] += prod

    acc, lo, hi, own, own_list = kernel(
        first_body,
        (
            array(acc_shape, F32),
            array(padded, BF16),
            array(padded, BF16),
            array(own.shape, BF16),
            list_type,
        ),
        [
            (tile_source_index, SM),
            (tile_target_index, SM),
            (tile_source_index.reshape(1, stored), HB),
            (tile_target_index.reshape(1, stored), HB),
            (vertex_costate, HB),
            (own, HB),
        ],
        scratch=[
            pltpu.VMEM(state, F32),
            pltpu.VMEM(state, BF16),
            pltpu.VMEM((1, stored), jnp.int32),
            pltpu.VMEM((1, stored), jnp.int32),
            pltpu.SemaphoreType.DMA((stored // UNROLL + 3,)),
        ],
    )

    def sort_body(rows, columns, listed):
        listed[...] = sorted_list(rows[...], columns[...])

    (other_list,) = kernel(
        sort_body,
        (list_type,),
        [(other_rows.reshape(1, stored), VM), (other_columns.reshape(1, stored), VM)],
    )
    listed = [(own_list, SM), (other_list, SM)]

    def head_values(lo, hi, hot):
        total = jnp.dot(lo[0], hot[0], preferred_element_type=F32)
        for b in range(1, blocks):
            row = lo[b] if b < low else hi[b - low]
            total += jnp.dot(row, hot[b], preferred_element_type=F32)
        return total.astype(BF16)

    def rows_of(owner):
        names = jnp.broadcast_to(owner.astype(F32), (heads, heads))
        before = lax.broadcasted_iota(jnp.int32, (heads, heads), 0)
        after = lax.broadcasted_iota(jnp.int32, (heads, heads), 1)
        same = jnp.logical_and(names.T == names, before < after)
        slot = jnp.sum(jnp.where(same, 1.0, 0.0), axis=0, keepdims=True).astype(jnp.int32)
        return owner * slots + slot

    def one_hots(vertex, count, out):
        node = lax.broadcasted_iota(jnp.int32, (nodes, heads), 0)
        for b in range(count):
            out[b] = jnp.where(node + b * nodes == vertex, 1.0, 0.0).astype(BF16)

    def place_rows(owner, keep, out):
        row = lax.broadcasted_iota(jnp.int32, (network * slots, heads), 0)
        out[...] = jnp.where(row == jnp.where(keep, rows_of(owner), -1), 1.0, 0.0).astype(BF16)

    place_type = array((network * slots, heads), BF16)

    def prepare_body(vertex, owner, lo, hi, hot, head, place):
        one_hots(vertex[...], blocks, hot)
        head[...] = head_values(lo, hi, hot)
        place_rows(owner[...], True, place)

    own_owner = distribution_entry_holder.reshape(1, heads)
    hot, head0, place = kernel(
        prepare_body,
        (array(hot_shape, BF16), array((cases, heads), BF16), place_type),
        [(distribution_entry_vertex.reshape(1, heads), VM), (own_owner, VM), (lo, VM), (hi, VM)],
    )
    mine = jnp.concatenate(
        [
            distribution_entry_vertex.reshape(1, heads),
            own_owner,
            distribution_entry_substation.reshape(1, heads),
        ],
        axis=1,
    )
    theirs = lax.ppermute(mine, "blk", backward)

    def rim_first_body(lists, acc, lo, hi, other, out, sums):
        sums[...] = acc[blocks:]
        run(
            lists,
            [((1, 0), hi, other, sums), ((1, 1), lo, other, sums)],
            FEW,
        )
        out[...] = sums[...].astype(BF16)

    (leaving,) = kernel(
        with_lists(rim_first_body),
        (array((rim, cases, nodes), BF16),),
        listed + [(acc, VM), (lo, VM), (hi, VM), (other, VM)],
        scratch=[pltpu.VMEM((rim, cases, nodes), F32)],
    )
    arriving = lax.ppermute(leaving, "blk", onward)

    def begin_next(lists, lam, icar, outflow, own, other, acc, acc_rim, hi):
        for b in range(blocks):
            acc[b] = outflow[b : b + 1, :] * icar[b]
        for b in range(rim):
            acc_rim[b] = jnp.zeros((cases, nodes), F32)
        for b in range(low, blocks):
            hi[b - low] = lam[b].astype(BF16)
        hi[blocks - low] = jnp.zeros((cases, nodes), BF16)
        run(lists, [((0, 0), hi, own, acc_rim), ((1, 0), hi, other, acc_rim)], FEW)
        run(lists, [((0, 2), hi, own, acc), ((1, 2), hi, other, acc)], MANY)

    def main_first_body(
        lists, acc, lo, hi, own, other, theirs, lam_in, icar_in, decay_in, inflow_in, outflow_in,
        lam_next, acc_next, acc_rim, hi_next, icar_next, hot_next, place_next, decay, inflow, outflow, other_kept,
        lam, icar, sems,
    ):
        pairs = [
            (icar_in, icar), (outflow_in, outflow), (lam_in, lam), (decay_in, decay), (inflow_in, inflow)
        ]
        copies = [pltpu.make_async_copy(a, b, sems.at[i]) for i, (a, b) in enumerate(pairs)]
        kept = pltpu.make_async_copy(other, other_kept, sems.at[5])
        for copy in copies + [kept]:
            copy.start()
        lam_next[...] = acc[:blocks]
        run(
            lists,
            [((1, 2), hi, other, lam_next), ((1, 3), lo, other, lam_next)],
            MANY,
        )
        for copy in copies:
            copy.wait()
        for b in range(blocks):
            lam_next[b] += outflow[b : b + 1, :] * icar[b]
            icar_next[b] = decay[b : b + 1, :] * icar[b] + inflow[b : b + 1, :] * lam[b]
        begin_next(
            lists, lam_next, icar_next, outflow, own, other, acc_next, acc_rim, hi_next
        )
        followed = lax.axis_index("blk") < owners - 1
        one_hots(theirs[:, :heads], low, hot_next)
        place_rows(theirs[:, heads : 2 * heads], followed, place_next)
        kept.wait()

    factor = array(factor_shape, F32)
    (
        lam, acc, acc_rim, hi_next, icar, hot_next, place_next, decay, inflow, outflow, other_kept
    ) = kernel(
        with_lists(main_first_body),
        (
            array(state, F32),
            array(state, F32),
            array((rim, cases, nodes), F32),
            array(padded, BF16),
            array(state, F32),
            array((low, nodes, heads), BF16),
            place_type,
            factor,
            factor,
            factor,
            hbm_array(other.shape, BF16),
        ),
        listed
        + [(acc, VM), (lo, VM), (hi, VM), (own, VM), (other, VM)]
        + [(theirs, VM)]
        + [(vertex_costate, HB), (inverter_costate, HB), (inverter_decay_factor, HB)]
        + [(costate_to_inverter_factor, HB), (inverter_to_costate_factor, HB)],
        scratch=[pltpu.VMEM(state, F32), pltpu.VMEM(state, F32), pltpu.SemaphoreType.DMA((6,))],
        out_specs=(VM,) * 10 + (HB,),
    )

    def take_arrived(arrived, lam, low_rows, lo):
        keep = lax.axis_index("blk") > 0
        for b in range(low):
            row = lam[b] + jnp.where(keep, arrived[b].astype(F32), 0.0)
            low_rows[b] = row
            lo[b] = row.astype(BF16)
        lo[low] = jnp.zeros((cases, nodes), BF16)

    def rim_sums(lists, acc_rim, lo, own, other, out, sums):
        sums[...] = acc_rim[...]
        run(lists, [((0, 1), lo, own, sums), ((1, 1), lo, other, sums)], FEW)
        out[...] = sums[...].astype(BF16)

    def rim_body(lists, arrived, lam, acc_rim, own, other, out, low_rows, lo, sums):
        take_arrived(arrived, lam, low_rows, lo)
        rim_sums(lists, acc_rim, lo, own, other, out, sums)

    def start_copies(lists, side, kind, first, count, source, dest, at, sem):
        def one(i, carry):
            c = word_of(lists, side, kind, first + i)
            pltpu.make_async_copy(source.at[c & 255], dest.at[at + i], sem).start()
            return carry

        lax.fori_loop(0, count, one, 0)

    def finish_copies(count, source, dest, sem):
        def one(i, carry):
            pltpu.make_async_copy(source.at[0], dest.at[0], sem).wait()
            return carry

        lax.fori_loop(0, count, one, 0)

    def run_copied(lists, first, count, lam, source, acc, width):
        total = count[0] + count[1]

        def some(i, carry):
            words = []
            for u in range(width):
                j = i * width + u
                is_own = j < count[0]
                at = jnp.where(is_own, first[0] + j, first[1] + j - count[0])
                at = jnp.clip(at, 0, STRIDE - 1)
                word = jnp.where(is_own, word_of(lists, 0, 1, at), word_of(lists, 1, 1, at))
                words.append((jnp.where(j < total, word, low << 8), jnp.minimum(j, total - 1)))
            prods = [
                jnp.dot(lam[(c >> 8) & 255], source[j], preferred_element_type=F32)
                for c, j in words
            ]
            for (c, _), prod in zip(words, prods):
                acc[c >> 16] += prod
            return carry

        lax.fori_loop(0, (total + width - 1) // width, some, 0)

    def rim_last_body(
        lists, arrived, lam, acc_rim, kept, own_in, other_in, out, low_rows, lo, sums, rest, sem
    ):
        count_own = count_of(lists, 0, 1)
        count_other = count_of(lists, 1, 1)
        keep_own = jnp.minimum(count_own, KEEP)
        keep_other = jnp.minimum(count_other, KEEP - keep_own)
        more_own = count_own - keep_own
        more_other = count_other - keep_other
        start_copies(lists, 0, 1, keep_own, more_own, own_in, rest, 0, sem)
        start_copies(lists, 1, 1, keep_other, more_other, other_in, rest, more_own, sem)
        take_arrived(arrived, lam, low_rows, lo)
        sums[...] = acc_rim[...]
        run_copied(lists, (0, 0), (keep_own, keep_other), lo, kept, sums, MANY)
        finish_copies(more_own + more_other, own_in, rest, sem)
        run_copied(
            lists, (keep_own, keep_other), (more_own, more_other), lo, rest, sums, FEW
        )
        out[...] = sums[...].astype(BF16)

    def main_body(
        lists, bus, theirs, left, low_rows, lam, lo, hi, acc, icar, own, other,
        hot, hot_next, head0, place, place_next, decay, inflow,
        lam_low, acc_rim, sent, kept, icar_out, lam_out, hi_out,
        icar_next, lo_base, lam_next, hi_next, sems,
    ):
        keep_own = jnp.minimum(count_of(lists, 0, 1), KEEP)
        keep_other = jnp.minimum(count_of(lists, 1, 1), KEEP - keep_own)
        start_copies(lists, 0, 1, 0, keep_own, own, kept, 0, sems.at[0])
        start_copies(lists, 1, 1, 0, keep_other, other, kept, keep_own, sems.at[0])
        for b in range(blocks):
            row = low_rows[b] if b < low else lam[b]
            icar_next[b] = decay[b : b + 1, :] * icar[b] + inflow[b : b + 1, :] * row
        icar_copy = pltpu.make_async_copy(icar_next, icar_out, sems.at[1])
        icar_copy.start()
        lam_next[...] = acc[...]
        run(lists, [((0, 3), lo, own, lam_next), ((1, 3), lo, other, lam_next)], MANY)
        upper = pl.ds(low, blocks - low)
        lam_copy = pltpu.make_async_copy(lam_next.at[upper], lam_out, sems.at[2])
        lam_copy.start()
        for b in range(low):
            lam_low[b] = lam_next[b]
            lo_base[b] = lam_next[b].astype(BF16)
        for b in range(low, blocks):
            hi_next[b - low] = lam_next[b].astype(BF16)
        hi_next[blocks - low] = jnp.zeros((cases, nodes), BF16)
        hi_copy = pltpu.make_async_copy(hi_next, hi_out, sems.at[3])
        hi_copy.start()
        acc_rim[...] = jnp.zeros(acc_rim.shape, F32)
        run(lists, [((0, 0), hi_next, own, acc_rim), ((1, 0), hi_next, other, acc_rim)], FEW)
        head_next = jnp.dot(left[0], hot_next[0], preferred_element_type=F32)
        for b in range(1, low):
            head_next += jnp.dot(left[b], hot_next[b], preferred_element_type=F32)
        width = (nodes - cases, heads)
        label = jnp.broadcast_to((bus[...] + 1).astype(F32), width).astype(BF16)
        bus_next = theirs[:, 2 * heads : 3 * heads]
        label_next = jnp.broadcast_to((bus_next + 1).astype(F32), width).astype(BF16)
        pairs = [
            (place, head0[...], head_values(lo, hi, hot)),
            (place, head_values(lo_base, hi_next, hot), label),
            (place_next, head_next.astype(BF16), label_next),
        ]
        for i, (where, first_half, second_half) in enumerate(pairs):
            part = lax.dot_general(
                where[...],
                jnp.concatenate([first_half, second_half], axis=0),
                (((1,), (1,)), ((), ())),
                preferred_element_type=F32,
            )
            sent[:, i] = part.astype(BF16).reshape(network, slots, nodes)
        finish_copies(keep_own + keep_other, own, kept, sems.at[0])
        icar_copy.wait()
        lam_copy.wait()
        hi_copy.wait()

    tiles = [(own, VM), (other, VM)]
    rim_type = array((rim, cases, nodes), BF16)
    low_type = array(half, F32)
    sums = pltpu.VMEM((rim, cases, nodes), F32)
    assert STEPS == 3
    hi = hi_next
    leaving, low_rows, lo = kernel(
        with_lists(rim_body),
        (rim_type, low_type, array(padded, BF16)),
        listed + [(arriving, VM), (lam, VM), (acc_rim, VM)] + tiles,
        scratch=[sums],
    )
    arriving = lax.ppermute(leaving, "blk", onward)
    lam_low, acc_rim, sent, kept, icar, lam_high, hi_next = kernel(
        with_lists(main_body),
        (
            low_type,
            array((rim, cases, nodes), F32),
            array((network, 3, slots, nodes), BF16),
            array((KEEP, nodes, nodes), BF16),
            hbm_array(state, F32),
            hbm_array((blocks - low, cases, nodes), F32),
            hbm_array(padded, BF16),
        ),
        listed
        + [(distribution_entry_substation.reshape(1, heads), VM), (theirs, VM), (leaving, VM)]
        + [(low_rows, VM), (lam, VM), (lo, VM), (hi, VM), (acc, VM), (icar, VM)]
        + tiles
        + [(hot, VM), (hot_next, VM), (head0, VM), (place, VM), (place_next, VM)]
        + [(decay, VM), (inflow, VM)],
        scratch=[
            pltpu.VMEM(state, F32),
            pltpu.VMEM(half, BF16),
            pltpu.VMEM(state, F32),
            pltpu.VMEM(padded, BF16),
            pltpu.SemaphoreType.DMA((4,)),
        ],
        out_specs=(VM,) * 4 + (HB,) * 3,
    )
    received = lax.all_to_all(
        sent.reshape(network, 3 * slots, nodes),
        ("sec", "blk"),
        split_axis=0,
        concat_axis=0,
        tiled=True,
    )
    received = received.reshape(rows_sent, nodes)
    stored_in = [(derivative_tiles, HB), (other_kept, HB)]
    fetched_shape = (2 * stored, nodes, nodes)
    leaving, low_rows, lo = kernel(
        with_lists(rim_last_body),
        (rim_type, low_type, array(padded, BF16)),
        listed + [(arriving, VM), (lam_low, VM), (acc_rim, VM), (kept, VM)] + stored_in,
        scratch=[sums, pltpu.VMEM(fetched_shape, BF16), pltpu.SemaphoreType.DMA],
    )
    arriving = lax.ppermute(leaving, "blk", onward)

    def main_last_body(
        lists, low_rows, lam_high, lo, hi, decay, inflow, outflow, own, other, icar,
        lam_out, low_next, icar_out, lam_next, icar_next, sems,
    ):
        for b in range(blocks):
            row = low_rows[b] if b < low else lam_high[b - low]
            before = icar[b]
            lam_next[b] = outflow[b : b + 1, :] * before
            icar_next[b] = decay[b : b + 1, :] * before + inflow[b : b + 1, :] * row
        icar_copy = pltpu.make_async_copy(icar_next, icar_out, sems.at[0])
        icar_copy.start()
        run(lists, [((0, 2), hi, own, lam_next), ((1, 2), hi, other, lam_next)], MANY)
        run(lists, [((0, 3), lo, own, lam_next), ((1, 3), lo, other, lam_next)], MANY)
        upper = pl.ds(low, blocks - low)
        lam_copy = pltpu.make_async_copy(lam_next.at[upper], lam_out.at[upper], sems.at[1])
        lam_copy.start()
        low_next[...] = lam_next[:low]
        icar_copy.wait()
        lam_copy.wait()

    lam, low_next, icar = kernel(
        with_lists(main_last_body),
        (hbm_array(state, F32), low_type, hbm_array(state, F32)),
        listed
        + [(low_rows, VM), (lam_high, VM), (lo, VM), (hi_next, VM)]
        + [(decay, VM), (inflow, VM), (outflow, VM)]
        + [(derivative_tiles, VM), (other_kept, VM), (icar, VM)],
        scratch=[
            pltpu.VMEM(state, F32),
            pltpu.VMEM(state, F32),
            pltpu.SemaphoreType.DMA((2,)),
        ],
        out_specs=(HB, VM, HB),
    )

    def trans_body(received, trans_in, matrix_in, out, trans, matrix, sems):
        copies = [
            pltpu.make_async_copy(trans_in, trans, sems.at[0]),
            pltpu.make_async_copy(matrix_in, matrix, sems.at[1]),
        ]
        for copy in copies:
            copy.start()
        dims = (((0,), (0,)), ((), ()))
        if slots % 16 == 0:
            parts = received[...].reshape(network, 3, slots, nodes)
            part = [parts[:, i].reshape(network * slots, nodes) for i in range(3)]
            column = lax.broadcasted_iota(jnp.int32, (network * slots, buses), 1)

            def hot_of(rows):
                label = rows[:, cases : cases + 1].astype(F32).astype(jnp.int32) - 1
                return jnp.where(label == column, 1.0, 0.0).astype(BF16)

            hot = hot_of(part[1])
            first = lax.dot_general(part[0], hot, dims, preferred_element_type=F32)
            last = lax.dot_general(part[1], hot, dims, preferred_element_type=F32)
            last += lax.dot_general(part[2], hot_of(part[2]), dims, preferred_element_type=F32)
        else:
            got = received[...].astype(F32)
            row = lax.broadcasted_iota(jnp.int32, (rows_sent, buses), 0)
            place = lax.rem(row, 3 * slots)
            column = lax.broadcasted_iota(jnp.int32, (rows_sent, buses), 1)
            label = got[:, cases : cases + 1].astype(jnp.int32) - 1
            hot = jnp.where(jnp.logical_and(label == column, place >= slots), 1.0, 0.0)
            own_hot = jnp.where(place < 2 * slots, hot, 0.0)
            hot_a = pltpu.roll(own_hot, rows_sent - slots, 0).astype(BF16)
            first = lax.dot_general(received[...], hot_a, dims, preferred_element_type=F32)
            last = lax.dot_general(
                received[...], hot.astype(BF16), dims, preferred_element_type=F32
            )
        for copy in copies:
            copy.wait()
        value = trans[...]
        for inj in (first[:cases], first[cases:], last[:cases]):
            value = jnp.dot(value.astype(BF16), matrix[...], preferred_element_type=F32) + inj
        out[...] = value

    (trans,) = kernel(
        trans_body,
        (array(highvoltage_costate.shape, F32),),
        [(received, VM), (highvoltage_costate, HB), (highvoltage_derivative_matrix, HB)],
        scratch=[
            pltpu.VMEM(highvoltage_costate.shape, F32),
            pltpu.VMEM(highvoltage_derivative_matrix.shape, BF16),
            pltpu.SemaphoreType.DMA((2,)),
        ],
    )

    def last_body(arrived, low_next, lam_in, lam_out, rows, sems):
        del lam_in
        keep = lax.axis_index("blk") > 0
        copies = []
        part = low // 4
        for i in range(4):
            for b in range(i * part, (i + 1) * part):
                rows[b] = low_next[b] + jnp.where(keep, arrived[b].astype(F32), 0.0)
            here = pl.ds(i * part, part)
            copies.append(pltpu.make_async_copy(rows.at[here], lam_out.at[here], sems.at[i]))
            copies[-1].start()
        for copy in copies:
            copy.wait()

    (lam,) = kernel(
        last_body,
        (array(state, F32),),
        [(arriving, VM), (low_next, VM), (lam, HB)],
        scratch=[pltpu.VMEM(half, F32), pltpu.SemaphoreType.DMA((4,))],
        out_specs=(HB,),
        aliases={2: 0},
    )
    return (lam, icar, trans)


def solution(mesh):
    placed = (
        P(("sec", "blk"), "case", None),
        P(("sec", "blk"), "case", None),
        P("case", ("sec", "blk")),
        P(("sec", "blk", "case"), None, None),
        P(("sec", "blk", "case")),
        P(("sec", "blk", "case")),
        P(("sec", "blk"), None),
        P(("sec", "blk"), None),
        P(("sec", "blk"), None),
        P(("sec", "blk")),
        P(("sec", "blk"), None),
        P(("sec", "blk")),
        P(("sec", "blk"), None),
    )

    return jax.shard_map(
        local,
        mesh=mesh,
        in_specs=placed,
        out_specs=(
            P(("sec", "blk"), "case", None),
            P(("sec", "blk"), "case", None),
            P("case", ("sec", "blk")),
        ),
        check_vma=False,
    )
```

```python
import jax
import jax.numpy as jnp
from jax import lax
from jax.experimental import pallas as pl
from jax.experimental.pallas import tpu as pltpu
from jax.sharding import PartitionSpec as P


STEPS = 3
UNROLL = 16
FEW = 24
MANY = 40
KEEP = 44
CLASSES = 4
VMEM_LIMIT = 24 << 20

F32 = jnp.float32
BF16 = jnp.bfloat16
VM = pl.BlockSpec(memory_space=pltpu.VMEM)
SM = pl.BlockSpec(memory_space=pltpu.SMEM)
HB = pl.BlockSpec(memory_space=pltpu.HBM)
STRIDE = 128


def kernel(body, outs, ins, scratch=(), out_specs=None, aliases=None):
    return pl.pallas_call(
        body,
        out_shape=outs,
        in_specs=[spec for _, spec in ins],
        out_specs=out_specs or tuple(VM for _ in outs),
        scratch_shapes=list(scratch),
        input_output_aliases=aliases or {},
        compiler_params=pltpu.CompilerParams(vmem_limit_bytes=VMEM_LIMIT),
    )(*[in_hbm(array) if spec is HB else array for array, spec in ins])


def with_lists(body):
    return lambda own, other, *refs: body((own, other), *refs)


def in_hbm(array):
    return pltpu.with_memory_space_constraint(array, pltpu.HBM)


def array(shape, dtype):
    return jax.ShapeDtypeStruct(shape, dtype)


def hbm_array(shape, dtype):
    return pltpu.HBM(shape, dtype)


def local(
    vertex_costate,
    inverter_costate,
    highvoltage_costate,
    derivative_tiles,
    tile_source_index,
    tile_target_index,
    inverter_decay_factor,
    costate_to_inverter_factor,
    inverter_to_costate_factor,
    distribution_entry_vertex,
    distribution_entry_holder,
    distribution_entry_substation,
    highvoltage_derivative_matrix,
):
    blocks, cases, nodes = vertex_costate.shape
    rim = blocks // 2
    low = blocks // 2
    targets = blocks + rim
    stored = derivative_tiles.shape[0]
    sections = lax.axis_size("sec")
    owners = lax.axis_size("blk")
    network = sections * owners
    heads = distribution_entry_vertex.shape[0]
    slots = max(2, 2 * heads // network)
    buses = highvoltage_derivative_matrix.shape[1]
    rows_sent = network * 3 * slots
    assert -(-stored // MANY) * MANY <= STRIDE and -(-stored // FEW) * FEW <= STRIDE

    state = (blocks, cases, nodes)
    half = (low, cases, nodes)
    padded = (low + 1, cases, nodes)
    acc_shape = (targets, cases, nodes)
    hot_shape = (blocks, nodes, heads)
    factor_shape = inverter_decay_factor.shape
    swap = [(0, 1), (1, 0)]
    onward = [(i, (i + 1) % owners) for i in range(owners)]
    backward = [(j, i) for i, j in onward]

    own = derivative_tiles
    other_rows = lax.ppermute(tile_source_index, "case", swap)
    other_columns = lax.ppermute(tile_target_index, "case", swap)
    other = lax.ppermute(own, "case", swap)

    def sorted_list(rows, columns):
        is_low = jnp.where(rows < low, 1, 0)
        is_own = jnp.where(columns < blocks, 1, 0)
        kind = 2 * is_own + is_low
        place = lax.broadcasted_iota(jnp.int32, (1, stored), 1)
        word = place | ((rows - low * (1 - is_low)) << 8) | ((columns - blocks * (1 - is_own)) << 16)
        kind_row = jnp.broadcast_to(kind.astype(F32), (stored, stored))
        word_row = jnp.broadcast_to(word.astype(F32), (stored, stored))
        earlier = lax.broadcasted_iota(jnp.int32, (stored, stored), 0) > lax.broadcasted_iota(
            jnp.int32, (stored, stored), 1
        )
        kind_col = kind_row.T
        same = jnp.logical_and(kind_col == kind_row, earlier)
        rank = jnp.sum(jnp.where(same, 1.0, 0.0), axis=1, keepdims=True)
        spot = (kind_col[:, :1] * STRIDE + rank).astype(jnp.int32)
        hit = lax.broadcasted_iota(jnp.int32, (stored, CLASSES * STRIDE), 1) == spot
        words = jnp.sum(jnp.where(hit, word_row.T[:, :1], 0.0), axis=0, keepdims=True)
        taken = jnp.sum(jnp.where(hit, 1.0, 0.0), axis=0, keepdims=True)
        idle = jnp.full((1, CLASSES * STRIDE), low << 8, jnp.int32)
        lane = lax.broadcasted_iota(jnp.int32, (stored, 128), 1).astype(F32)
        counts = jnp.sum(jnp.where(kind_col[:, :1] == lane, 1.0, 0.0), axis=0, keepdims=True)
        return jnp.concatenate(
            [jnp.where(taken > 0, words.astype(jnp.int32), idle), counts.astype(jnp.int32)], axis=1
        )

    def word_of(lists, side, kind, i):
        return lists[side][0, kind * STRIDE + i]

    def count_of(lists, side, kind):
        return lists[side][0, CLASSES * STRIDE + kind]

    list_type = array((1, CLASSES * STRIDE + 128), jnp.int32)

    def run(lists, parts, width):
        def some(i, carry):
            words = [
                (word_of(lists, side, kind, i * width + u), lam, tiles, acc)
                for (side, kind), lam, tiles, acc in parts
                for u in range(width)
            ]
            prods = [
                jnp.dot(lam[(c >> 8) & 255], tiles[c & 255], preferred_element_type=F32)
                for c, lam, tiles, _ in words
            ]
            for (c, _, _, acc), prod in zip(words, prods):
                acc[c >> 16] += prod
            return carry

        longest = 0
        for (side, kind), _, _, _ in parts:
            longest = jnp.maximum(longest, count_of(lists, side, kind))
        lax.fori_loop(0, (longest + width - 1) // width, some, 0)

    def first_body(
        rows, columns, rows_in, columns_in, lam_in, own_in, acc, lo, hi, own_kept, listed,
        lam, lam_bf, rows_kept, columns_kept, sems,
    ):
        chunks = stored // UNROLL
        early = [
            pltpu.make_async_copy(rows_in, rows_kept, sems.at[chunks]),
            pltpu.make_async_copy(columns_in, columns_kept, sems.at[chunks + 1]),
            pltpu.make_async_copy(lam_in, lam, sems.at[chunks + 2]),
        ]
        copies = [
            pltpu.make_async_copy(
                own_in.at[pl.ds(i * UNROLL, UNROLL)], own_kept.at[pl.ds(i * UNROLL, UNROLL)], sems.at[i]
            )
            for i in range(chunks)
        ]
        for copy in early + copies:
            copy.start()
        for b in range(targets):
            acc[b] = jnp.zeros((cases, nodes), F32)
        zero = jnp.zeros((cases, nodes), BF16)
        lo[low] = zero
        hi[blocks - low] = zero
        early[0].wait()
        early[1].wait()
        listed[...] = sorted_list(rows_kept[...], columns_kept[...])
        early[2].wait()
        for b in range(blocks):
            rounded = lam[b].astype(BF16)
            lam_bf[b] = rounded
            if b < low:
                lo[b] = rounded
            else:
                hi[b - low] = rounded
        for i, copy in enumerate(copies):
            copy.wait()
            prods = [
                jnp.dot(
                    lam_bf[rows[i * UNROLL + u]],
                    own_kept[i * UNROLL + u],
                    preferred_element_type=F32,
                )
                for u in range(UNROLL)
            ]
            for u, prod in enumerate(prods):
                acc[columns[i * UNROLL + u]] += prod

    acc, lo, hi, own, own_list = kernel(
        first_body,
        (
            array(acc_shape, F32),
            array(padded, BF16),
            array(padded, BF16),
            array(own.shape, BF16),
            list_type,
        ),
        [
            (tile_source_index, SM),
            (tile_target_index, SM),
            (tile_source_index.reshape(1, stored), HB),
            (tile_target_index.reshape(1, stored), HB),
            (vertex_costate, HB),
            (own, HB),
        ],
        scratch=[
            pltpu.VMEM(state, F32),
            pltpu.VMEM(state, BF16),
            pltpu.VMEM((1, stored), jnp.int32),
            pltpu.VMEM((1, stored), jnp.int32),
            pltpu.SemaphoreType.DMA((stored // UNROLL + 3,)),
        ],
    )

    def sort_body(rows, columns, listed):
        listed[...] = sorted_list(rows[...], columns[...])

    (other_list,) = kernel(
        sort_body,
        (list_type,),
        [(other_rows.reshape(1, stored), VM), (other_columns.reshape(1, stored), VM)],
    )
    listed = [(own_list, SM), (other_list, SM)]

    def head_values(lo, hi, hot):
        total = jnp.dot(lo[0], hot[0], preferred_element_type=F32)
        for b in range(1, blocks):
            row = lo[b] if b < low else hi[b - low]
            total += jnp.dot(row, hot[b], preferred_element_type=F32)
        return total.astype(BF16)

    def rows_of(owner):
        names = jnp.broadcast_to(owner.astype(F32), (heads, heads))
        before = lax.broadcasted_iota(jnp.int32, (heads, heads), 0)
        after = lax.broadcasted_iota(jnp.int32, (heads, heads), 1)
        same = jnp.logical_and(names.T == names, before < after)
        slot = jnp.sum(jnp.where(same, 1.0, 0.0), axis=0, keepdims=True).astype(jnp.int32)
        return owner * slots + slot

    def one_hots(vertex, count, out):
        node = lax.broadcasted_iota(jnp.int32, (nodes, heads), 0)
        for b in range(count):
            out[b] = jnp.where(node + b * nodes == vertex, 1.0, 0.0).astype(BF16)

    def place_rows(owner, keep, out):
        row = lax.broadcasted_iota(jnp.int32, (network * slots, heads), 0)
        out[...] = jnp.where(row == jnp.where(keep, rows_of(owner), -1), 1.0, 0.0).astype(BF16)

    place_type = array((network * slots, heads), BF16)

    def prepare_body(vertex, owner, lo, hi, hot, head, place):
        one_hots(vertex[...], blocks, hot)
        head[...] = head_values(lo, hi, hot)
        place_rows(owner[...], True, place)

    own_owner = distribution_entry_holder.reshape(1, heads)
    hot, head0, place = kernel(
        prepare_body,
        (array(hot_shape, BF16), array((cases, heads), BF16), place_type),
        [(distribution_entry_vertex.reshape(1, heads), VM), (own_owner, VM), (lo, VM), (hi, VM)],
    )

    def rim_first_body(lists, acc, lo, hi, other, out, sums):
        sums[...] = acc[blocks:]
        run(
            lists,
            [((1, 0), hi, other, sums), ((1, 1), lo, other, sums)],
            FEW,
        )
        out[...] = sums[...].astype(BF16)

    (leaving,) = kernel(
        with_lists(rim_first_body),
        (array((rim, cases, nodes), BF16),),
        listed + [(acc, VM), (lo, VM), (hi, VM), (other, VM)],
        scratch=[pltpu.VMEM((rim, cases, nodes), F32)],
    )
    arriving = lax.ppermute(leaving, "blk", onward)

    mine = jnp.concatenate(
        [
            distribution_entry_vertex.reshape(1, heads),
            own_owner,
            distribution_entry_substation.reshape(1, heads),
        ],
        axis=1,
    )
    theirs = lax.ppermute(mine, "blk", backward)

    def begin_next(lists, lam, icar, outflow, own, other, acc, acc_rim, hi):
        for b in range(blocks):
            acc[b] = outflow[b : b + 1, :] * icar[b]
        for b in range(rim):
            acc_rim[b] = jnp.zeros((cases, nodes), F32)
        for b in range(low, blocks):
            hi[b - low] = lam[b].astype(BF16)
        hi[blocks - low] = jnp.zeros((cases, nodes), BF16)
        run(lists, [((0, 0), hi, own, acc_rim), ((1, 0), hi, other, acc_rim)], FEW)
        run(lists, [((0, 2), hi, own, acc), ((1, 2), hi, other, acc)], MANY)

    def main_first_body(
        lists, acc, lo, hi, own, other, lam_in, icar_in, decay_in, inflow_in, outflow_in,
        lam_next, acc_next, acc_rim, hi_next, icar_next, decay, inflow, outflow, other_kept,
        lam, icar, sems,
    ):
        pairs = [
            (icar_in, icar), (outflow_in, outflow), (lam_in, lam), (decay_in, decay), (inflow_in, inflow)
        ]
        copies = [pltpu.make_async_copy(a, b, sems.at[i]) for i, (a, b) in enumerate(pairs)]
        kept = pltpu.make_async_copy(other, other_kept, sems.at[5])
        for copy in copies + [kept]:
            copy.start()
        lam_next[...] = acc[:blocks]
        run(
            lists,
            [((1, 2), hi, other, lam_next), ((1, 3), lo, other, lam_next)],
            MANY,
        )
        for copy in copies:
            copy.wait()
        for b in range(blocks):
            lam_next[b] += outflow[b : b + 1, :] * icar[b]
            icar_next[b] = decay[b : b + 1, :] * icar[b] + inflow[b : b + 1, :] * lam[b]
        begin_next(
            lists, lam_next, icar_next, outflow, own, other, acc_next, acc_rim, hi_next
        )
        kept.wait()

    factor = array(factor_shape, F32)
    lam, acc, acc_rim, hi_next, icar, decay, inflow, outflow, other_kept = kernel(
        with_lists(main_first_body),
        (
            array(state, F32),
            array(state, F32),
            array((rim, cases, nodes), F32),
            array(padded, BF16),
            array(state, F32),
            factor,
            factor,
            factor,
            hbm_array(other.shape, BF16),
        ),
        listed
        + [(acc, VM), (lo, VM), (hi, VM), (own, VM), (other, VM)]
        + [(vertex_costate, HB), (inverter_costate, HB), (inverter_decay_factor, HB)]
        + [(costate_to_inverter_factor, HB), (inverter_to_costate_factor, HB)],
        scratch=[pltpu.VMEM(state, F32), pltpu.VMEM(state, F32), pltpu.SemaphoreType.DMA((6,))],
        out_specs=(VM,) * 8 + (HB,),
    )

    def take_arrived(arrived, lam, low_rows, lo):
        keep = lax.axis_index("blk") > 0
        for b in range(low):
            row = lam[b] + jnp.where(keep, arrived[b].astype(F32), 0.0)
            low_rows[b] = row
            lo[b] = row.astype(BF16)
        lo[low] = jnp.zeros((cases, nodes), BF16)

    def rim_sums(lists, acc_rim, lo, own, other, out, sums):
        sums[...] = acc_rim[...]
        run(lists, [((0, 1), lo, own, sums), ((1, 1), lo, other, sums)], FEW)
        out[...] = sums[...].astype(BF16)

    def rim_body(lists, arrived, lam, acc_rim, own, other, out, low_rows, lo, sums):
        take_arrived(arrived, lam, low_rows, lo)
        rim_sums(lists, acc_rim, lo, own, other, out, sums)

    def start_copies(lists, side, kind, first, count, source, dest, at, sem):
        def one(i, carry):
            c = word_of(lists, side, kind, first + i)
            pltpu.make_async_copy(source.at[c & 255], dest.at[at + i], sem).start()
            return carry

        lax.fori_loop(0, count, one, 0)

    def finish_copies(count, source, dest, sem):
        def one(i, carry):
            pltpu.make_async_copy(source.at[0], dest.at[0], sem).wait()
            return carry

        lax.fori_loop(0, count, one, 0)

    def run_copied(lists, first, count, lam, source, acc, width):
        total = count[0] + count[1]

        def some(i, carry):
            words = []
            for u in range(width):
                j = i * width + u
                is_own = j < count[0]
                at = jnp.where(is_own, first[0] + j, first[1] + j - count[0])
                at = jnp.clip(at, 0, STRIDE - 1)
                word = jnp.where(is_own, word_of(lists, 0, 1, at), word_of(lists, 1, 1, at))
                words.append((jnp.where(j < total, word, low << 8), jnp.minimum(j, total - 1)))
            prods = [
                jnp.dot(lam[(c >> 8) & 255], source[j], preferred_element_type=F32)
                for c, j in words
            ]
            for (c, _), prod in zip(words, prods):
                acc[c >> 16] += prod
            return carry

        lax.fori_loop(0, (total + width - 1) // width, some, 0)

    def rim_last_body(
        lists, arrived, lam, acc_rim, kept, own_in, other_in, out, low_rows, lo, sums, rest, sem
    ):
        count_own = count_of(lists, 0, 1)
        count_other = count_of(lists, 1, 1)
        keep_own = jnp.minimum(count_own, KEEP)
        keep_other = jnp.minimum(count_other, KEEP - keep_own)
        more_own = count_own - keep_own
        more_other = count_other - keep_other
        start_copies(lists, 0, 1, keep_own, more_own, own_in, rest, 0, sem)
        start_copies(lists, 1, 1, keep_other, more_other, other_in, rest, more_own, sem)
        take_arrived(arrived, lam, low_rows, lo)
        sums[...] = acc_rim[...]
        run_copied(lists, (0, 0), (keep_own, keep_other), lo, kept, sums, MANY)
        finish_copies(more_own + more_other, own_in, rest, sem)
        run_copied(
            lists, (keep_own, keep_other), (more_own, more_other), lo, rest, sums, FEW
        )
        out[...] = sums[...].astype(BF16)

    def main_body(
        lists, bus, theirs, left, low_rows, lam, lo, hi, acc, icar, own, other,
        hot, head0, place, decay, inflow,
        lam_low, acc_rim, sent, kept, icar_out, lam_out, hi_out,
        icar_next, lo_base, lam_next, hi_next, hot_next, place_next, sems,
    ):
        keep_own = jnp.minimum(count_of(lists, 0, 1), KEEP)
        keep_other = jnp.minimum(count_of(lists, 1, 1), KEEP - keep_own)
        for b in range(blocks):
            row = low_rows[b] if b < low else lam[b]
            icar_next[b] = decay[b : b + 1, :] * icar[b] + inflow[b : b + 1, :] * row
        icar_copy = pltpu.make_async_copy(icar_next, icar_out, sems.at[0])
        icar_copy.start()
        lam_next[...] = acc[...]
        run(lists, [((0, 3), lo, own, lam_next), ((1, 3), lo, other, lam_next)], MANY)
        upper = pl.ds(low, blocks - low)
        lam_copy = pltpu.make_async_copy(lam_next.at[upper], lam_out, sems.at[1])
        lam_copy.start()
        for b in range(low):
            lam_low[b] = lam_next[b]
            lo_base[b] = lam_next[b].astype(BF16)
        for b in range(low, blocks):
            hi_next[b - low] = lam_next[b].astype(BF16)
        hi_next[blocks - low] = jnp.zeros((cases, nodes), BF16)
        hi_copy = pltpu.make_async_copy(hi_next, hi_out, sems.at[2])
        hi_copy.start()
        acc_rim[...] = jnp.zeros(acc_rim.shape, F32)
        run(lists, [((0, 0), hi_next, own, acc_rim), ((1, 0), hi_next, other, acc_rim)], FEW)
        followed = lax.axis_index("blk") < owners - 1
        one_hots(theirs[:, :heads], low, hot_next)
        place_rows(theirs[:, heads : 2 * heads], followed, place_next)
        head_next = jnp.dot(left[0], hot_next[0], preferred_element_type=F32)
        for b in range(1, low):
            head_next += jnp.dot(left[b], hot_next[b], preferred_element_type=F32)
        width = (nodes - cases, heads)
        label = jnp.broadcast_to((bus[...] + 1).astype(F32), width).astype(BF16)
        bus_next = theirs[:, 2 * heads : 3 * heads]
        label_next = jnp.broadcast_to((bus_next + 1).astype(F32), width).astype(BF16)
        pairs = [
            (place, head0[...], head_values(lo, hi, hot)),
            (place, head_values(lo_base, hi_next, hot), label),
            (place_next, head_next.astype(BF16), label_next),
        ]
        for i, (where, first_half, second_half) in enumerate(pairs):
            part = lax.dot_general(
                where[...],
                jnp.concatenate([first_half, second_half], axis=0),
                (((1,), (1,)), ((), ())),
                preferred_element_type=F32,
            )
            sent[:, i] = part.astype(BF16).reshape(network, slots, nodes)

        def keep_own_block(i, carry):
            kept[i] = own[word_of(lists, 0, 1, i) & 255]
            return carry

        def keep_other_block(i, carry):
            kept[keep_own + i] = other[word_of(lists, 1, 1, i) & 255]
            return carry

        lax.fori_loop(0, keep_own, keep_own_block, 0)
        lax.fori_loop(0, keep_other, keep_other_block, 0)
        icar_copy.wait()
        lam_copy.wait()
        hi_copy.wait()

    tiles = [(own, VM), (other, VM)]
    rim_type = array((rim, cases, nodes), BF16)
    low_type = array(half, F32)
    sums = pltpu.VMEM((rim, cases, nodes), F32)
    assert STEPS == 3
    hi = hi_next
    leaving, low_rows, lo = kernel(
        with_lists(rim_body),
        (rim_type, low_type, array(padded, BF16)),
        listed + [(arriving, VM), (lam, VM), (acc_rim, VM)] + tiles,
        scratch=[sums],
    )
    arriving = lax.ppermute(leaving, "blk", onward)
    lam_low, acc_rim, sent, kept, icar, lam_high, hi_next = kernel(
        with_lists(main_body),
        (
            low_type,
            array((rim, cases, nodes), F32),
            array((network, 3, slots, nodes), BF16),
            array((KEEP, nodes, nodes), BF16),
            hbm_array(state, F32),
            hbm_array((blocks - low, cases, nodes), F32),
            hbm_array(padded, BF16),
        ),
        listed
        + [(distribution_entry_substation.reshape(1, heads), VM), (theirs, VM), (leaving, VM)]
        + [(low_rows, VM), (lam, VM), (lo, VM), (hi, VM), (acc, VM), (icar, VM)]
        + tiles
        + [(hot, VM), (head0, VM), (place, VM)]
        + [(decay, VM), (inflow, VM)],
        scratch=[
            pltpu.VMEM(state, F32),
            pltpu.VMEM(half, BF16),
            pltpu.VMEM(state, F32),
            pltpu.VMEM(padded, BF16),
            pltpu.VMEM((low, nodes, heads), BF16),
            pltpu.VMEM(place_type.shape, BF16),
            pltpu.SemaphoreType.DMA((3,)),
        ],
        out_specs=(VM,) * 4 + (HB,) * 3,
    )
    received = lax.all_to_all(
        sent.reshape(network, 3 * slots, nodes),
        ("sec", "blk"),
        split_axis=0,
        concat_axis=0,
        tiled=True,
    )
    received = received.reshape(rows_sent, nodes)
    stored_in = [(derivative_tiles, HB), (other_kept, HB)]
    fetched_shape = (2 * stored, nodes, nodes)
    leaving, low_rows, lo = kernel(
        with_lists(rim_last_body),
        (rim_type, low_type, array(padded, BF16)),
        listed + [(arriving, VM), (lam_low, VM), (acc_rim, VM), (kept, VM)] + stored_in,
        scratch=[sums, pltpu.VMEM(fetched_shape, BF16), pltpu.SemaphoreType.DMA],
    )
    arriving = lax.ppermute(leaving, "blk", onward)

    def main_last_body(
        lists, low_rows, lam_high, lo, hi, decay, inflow, outflow, own, other, icar,
        lam_out, low_next, icar_out, lam_next, icar_next, sems,
    ):
        for b in range(blocks):
            row = low_rows[b] if b < low else lam_high[b - low]
            before = icar[b]
            lam_next[b] = outflow[b : b + 1, :] * before
            icar_next[b] = decay[b : b + 1, :] * before + inflow[b : b + 1, :] * row
        icar_copy = pltpu.make_async_copy(icar_next, icar_out, sems.at[0])
        icar_copy.start()
        run(lists, [((0, 2), hi, own, lam_next), ((1, 2), hi, other, lam_next)], MANY)
        run(lists, [((0, 3), lo, own, lam_next), ((1, 3), lo, other, lam_next)], MANY)
        upper = pl.ds(low, blocks - low)
        lam_copy = pltpu.make_async_copy(lam_next.at[upper], lam_out.at[upper], sems.at[1])
        lam_copy.start()
        low_next[...] = lam_next[:low]
        icar_copy.wait()
        lam_copy.wait()

    lam, low_next, icar = kernel(
        with_lists(main_last_body),
        (hbm_array(state, F32), low_type, hbm_array(state, F32)),
        listed
        + [(low_rows, VM), (lam_high, VM), (lo, VM), (hi_next, VM)]
        + [(decay, VM), (inflow, VM), (outflow, VM)]
        + [(derivative_tiles, VM), (other_kept, VM), (icar, VM)],
        scratch=[
            pltpu.VMEM(state, F32),
            pltpu.VMEM(state, F32),
            pltpu.SemaphoreType.DMA((2,)),
        ],
        out_specs=(HB, VM, HB),
    )

    def trans_body(received, trans_in, matrix_in, out, trans, matrix, sems):
        copies = [
            pltpu.make_async_copy(trans_in, trans, sems.at[0]),
            pltpu.make_async_copy(matrix_in, matrix, sems.at[1]),
        ]
        for copy in copies:
            copy.start()
        dims = (((0,), (0,)), ((), ()))
        if slots % 16 == 0:
            parts = received[...].reshape(network, 3, slots, nodes)
            part = [parts[:, i].reshape(network * slots, nodes) for i in range(3)]
            column = lax.broadcasted_iota(jnp.int32, (network * slots, buses), 1)

            def hot_of(rows):
                label = rows[:, cases : cases + 1].astype(F32).astype(jnp.int32) - 1
                return jnp.where(label == column, 1.0, 0.0).astype(BF16)

            hot = hot_of(part[1])
            first = lax.dot_general(part[0], hot, dims, preferred_element_type=F32)
            last = lax.dot_general(part[1], hot, dims, preferred_element_type=F32)
            last += lax.dot_general(part[2], hot_of(part[2]), dims, preferred_element_type=F32)
        else:
            got = received[...].astype(F32)
            row = lax.broadcasted_iota(jnp.int32, (rows_sent, buses), 0)
            place = lax.rem(row, 3 * slots)
            column = lax.broadcasted_iota(jnp.int32, (rows_sent, buses), 1)
            label = got[:, cases : cases + 1].astype(jnp.int32) - 1
            hot = jnp.where(jnp.logical_and(label == column, place >= slots), 1.0, 0.0)
            own_hot = jnp.where(place < 2 * slots, hot, 0.0)
            hot_a = pltpu.roll(own_hot, rows_sent - slots, 0).astype(BF16)
            first = lax.dot_general(received[...], hot_a, dims, preferred_element_type=F32)
            last = lax.dot_general(
                received[...], hot.astype(BF16), dims, preferred_element_type=F32
            )
        for copy in copies:
            copy.wait()
        value = trans[...]
        for inj in (first[:cases], first[cases:], last[:cases]):
            value = jnp.dot(value.astype(BF16), matrix[...], preferred_element_type=F32) + inj
        out[...] = value

    (trans,) = kernel(
        trans_body,
        (array(highvoltage_costate.shape, F32),),
        [(received, VM), (highvoltage_costate, HB), (highvoltage_derivative_matrix, HB)],
        scratch=[
            pltpu.VMEM(highvoltage_costate.shape, F32),
            pltpu.VMEM(highvoltage_derivative_matrix.shape, BF16),
            pltpu.SemaphoreType.DMA((2,)),
        ],
    )

    def last_body(arrived, low_next, lam_in, lam_out, rows, sems):
        del lam_in
        keep = lax.axis_index("blk") > 0
        copies = []
        part = low // 4
        for i in range(4):
            for b in range(i * part, (i + 1) * part):
                rows[b] = low_next[b] + jnp.where(keep, arrived[b].astype(F32), 0.0)
            here = pl.ds(i * part, part)
            copies.append(pltpu.make_async_copy(rows.at[here], lam_out.at[here], sems.at[i]))
            copies[-1].start()
        for copy in copies:
            copy.wait()

    (lam,) = kernel(
        last_body,
        (array(state, F32),),
        [(arriving, VM), (low_next, VM), (lam, HB)],
        scratch=[pltpu.VMEM(half, F32), pltpu.SemaphoreType.DMA((4,))],
        out_specs=(HB,),
        aliases={2: 0},
    )
    return (lam, icar, trans)


def solution(mesh):
    placed = (
        P(("sec", "blk"), "case", None),
        P(("sec", "blk"), "case", None),
        P("case", ("sec", "blk")),
        P(("sec", "blk", "case"), None, None),
        P(("sec", "blk", "case")),
        P(("sec", "blk", "case")),
        P(("sec", "blk"), None),
        P(("sec", "blk"), None),
        P(("sec", "blk"), None),
        P(("sec", "blk")),
        P(("sec", "blk"), None),
        P(("sec", "blk")),
        P(("sec", "blk"), None),
    )

    return jax.shard_map(
        local,
        mesh=mesh,
        in_specs=placed,
        out_specs=(
            P(("sec", "blk"), "case", None),
            P(("sec", "blk"), "case", None),
            P("case", ("sec", "blk")),
        ),
        check_vma=False,
    )
```

```python
import jax
import jax.numpy as jnp
from jax import lax
from jax.experimental import pallas as pl
from jax.experimental.pallas import tpu as pltpu
from jax.sharding import PartitionSpec as P


STEPS = 3
UNROLL = 16
FEW = 24
MANY = 40
KEEP = 44
CLASSES = 4
VMEM_LIMIT = 24 << 20

F32 = jnp.float32
BF16 = jnp.bfloat16
VM = pl.BlockSpec(memory_space=pltpu.VMEM)
SM = pl.BlockSpec(memory_space=pltpu.SMEM)
HB = pl.BlockSpec(memory_space=pltpu.HBM)
STRIDE = 128


def kernel(body, outs, ins, scratch=(), out_specs=None, aliases=None):
    return pl.pallas_call(
        body,
        out_shape=outs,
        in_specs=[spec for _, spec in ins],
        out_specs=out_specs or tuple(VM for _ in outs),
        scratch_shapes=list(scratch),
        input_output_aliases=aliases or {},
        compiler_params=pltpu.CompilerParams(vmem_limit_bytes=VMEM_LIMIT),
    )(*[in_hbm(array) if spec is HB else array for array, spec in ins])


def with_lists(body):
    return lambda own, other, *refs: body((own, other), *refs)


def in_hbm(array):
    return pltpu.with_memory_space_constraint(array, pltpu.HBM)


def array(shape, dtype):
    return jax.ShapeDtypeStruct(shape, dtype)


def hbm_array(shape, dtype):
    return pltpu.HBM(shape, dtype)


def local(
    vertex_costate,
    inverter_costate,
    highvoltage_costate,
    derivative_tiles,
    tile_source_index,
    tile_target_index,
    inverter_decay_factor,
    costate_to_inverter_factor,
    inverter_to_costate_factor,
    distribution_entry_vertex,
    distribution_entry_holder,
    distribution_entry_substation,
    highvoltage_derivative_matrix,
):
    blocks, cases, nodes = vertex_costate.shape
    rim = blocks // 2
    low = blocks // 2
    targets = blocks + rim
    stored = derivative_tiles.shape[0]
    sections = lax.axis_size("sec")
    owners = lax.axis_size("blk")
    network = sections * owners
    heads = distribution_entry_vertex.shape[0]
    slots = max(2, 2 * heads // network)
    buses = highvoltage_derivative_matrix.shape[1]
    rows_sent = network * 3 * slots
    assert -(-stored // MANY) * MANY <= STRIDE and -(-stored // FEW) * FEW <= STRIDE

    state = (blocks, cases, nodes)
    half = (low, cases, nodes)
    padded = (low + 1, cases, nodes)
    acc_shape = (targets, cases, nodes)
    hot_shape = (blocks, nodes, heads)
    factor_shape = inverter_decay_factor.shape
    swap = [(0, 1), (1, 0)]
    onward = [(i, (i + 1) % owners) for i in range(owners)]
    backward = [(j, i) for i, j in onward]

    own = derivative_tiles
    other_rows = lax.ppermute(tile_source_index, "case", swap)
    other_columns = lax.ppermute(tile_target_index, "case", swap)
    other = lax.ppermute(own, "case", swap)

    def sorted_list(rows, columns):
        is_low = jnp.where(rows < low, 1, 0)
        is_own = jnp.where(columns < blocks, 1, 0)
        kind = 2 * is_own + is_low
        place = lax.broadcasted_iota(jnp.int32, (1, stored), 1)
        word = place | ((rows - low * (1 - is_low)) << 8) | ((columns - blocks * (1 - is_own)) << 16)
        kind_row = jnp.broadcast_to(kind.astype(F32), (stored, stored))
        word_row = jnp.broadcast_to(word.astype(F32), (stored, stored))
        earlier = lax.broadcasted_iota(jnp.int32, (stored, stored), 0) > lax.broadcasted_iota(
            jnp.int32, (stored, stored), 1
        )
        kind_col = kind_row.T
        same = jnp.logical_and(kind_col == kind_row, earlier)
        rank = jnp.sum(jnp.where(same, 1.0, 0.0), axis=1, keepdims=True)
        spot = (kind_col[:, :1] * STRIDE + rank).astype(jnp.int32)
        hit = lax.broadcasted_iota(jnp.int32, (stored, CLASSES * STRIDE), 1) == spot
        words = jnp.sum(jnp.where(hit, word_row.T[:, :1], 0.0), axis=0, keepdims=True)
        taken = jnp.sum(jnp.where(hit, 1.0, 0.0), axis=0, keepdims=True)
        idle = jnp.full((1, CLASSES * STRIDE), low << 8, jnp.int32)
        lane = lax.broadcasted_iota(jnp.int32, (stored, 128), 1).astype(F32)
        counts = jnp.sum(jnp.where(kind_col[:, :1] == lane, 1.0, 0.0), axis=0, keepdims=True)
        return jnp.concatenate(
            [jnp.where(taken > 0, words.astype(jnp.int32), idle), counts.astype(jnp.int32)], axis=1
        )

    def word_of(lists, side, kind, i):
        return lists[side][0, kind * STRIDE + i]

    def count_of(lists, side, kind):
        return lists[side][0, CLASSES * STRIDE + kind]

    list_type = array((1, CLASSES * STRIDE + 128), jnp.int32)

    def run(lists, parts, width):
        def some(i, carry):
            words = [
                (word_of(lists, side, kind, i * width + u), lam, tiles, acc)
                for (side, kind), lam, tiles, acc in parts
                for u in range(width)
            ]
            prods = [
                jnp.dot(lam[(c >> 8) & 255], tiles[c & 255], preferred_element_type=F32)
                for c, lam, tiles, _ in words
            ]
            for (c, _, _, acc), prod in zip(words, prods):
                acc[c >> 16] += prod
            return carry

        longest = 0
        for (side, kind), _, _, _ in parts:
            longest = jnp.maximum(longest, count_of(lists, side, kind))
        lax.fori_loop(0, (longest + width - 1) // width, some, 0)

    def first_body(
        rows, columns, rows_in, columns_in, lam_in, own_in, acc, lo, hi, own_kept, listed,
        lam, lam_bf, rows_kept, columns_kept, sems,
    ):
        chunks = stored // UNROLL
        early = [
            pltpu.make_async_copy(rows_in, rows_kept, sems.at[chunks]),
            pltpu.make_async_copy(columns_in, columns_kept, sems.at[chunks + 1]),
            pltpu.make_async_copy(lam_in, lam, sems.at[chunks + 2]),
        ]
        copies = [
            pltpu.make_async_copy(
                own_in.at[pl.ds(i * UNROLL, UNROLL)], own_kept.at[pl.ds(i * UNROLL, UNROLL)], sems.at[i]
            )
            for i in range(chunks)
        ]
        for copy in early + copies:
            copy.start()
        for b in range(targets):
            acc[b] = jnp.zeros((cases, nodes), F32)
        zero = jnp.zeros((cases, nodes), BF16)
        lo[low] = zero
        hi[blocks - low] = zero
        early[0].wait()
        early[1].wait()
        listed[...] = sorted_list(rows_kept[...], columns_kept[...])
        early[2].wait()
        for b in range(blocks):
            rounded = lam[b].astype(BF16)
            lam_bf[b] = rounded
            if b < low:
                lo[b] = rounded
            else:
                hi[b - low] = rounded
        for i, copy in enumerate(copies):
            copy.wait()
            prods = [
                jnp.dot(
                    lam_bf[rows[i * UNROLL + u]],
                    own_kept[i * UNROLL + u],
                    preferred_element_type=F32,
                )
                for u in range(UNROLL)
            ]
            for u, prod in enumerate(prods):
                acc[columns[i * UNROLL + u]] += prod

    acc, lo, hi, own, own_list = kernel(
        first_body,
        (
            array(acc_shape, F32),
            array(padded, BF16),
            array(padded, BF16),
            array(own.shape, BF16),
            list_type,
        ),
        [
            (tile_source_index, SM),
            (tile_target_index, SM),
            (tile_source_index.reshape(1, stored), HB),
            (tile_target_index.reshape(1, stored), HB),
            (vertex_costate, HB),
            (own, HB),
        ],
        scratch=[
            pltpu.VMEM(state, F32),
            pltpu.VMEM(state, BF16),
            pltpu.VMEM((1, stored), jnp.int32),
            pltpu.VMEM((1, stored), jnp.int32),
            pltpu.SemaphoreType.DMA((stored // UNROLL + 3,)),
        ],
    )

    def sort_body(rows, columns, listed):
        listed[...] = sorted_list(rows[...], columns[...])

    (other_list,) = kernel(
        sort_body,
        (list_type,),
        [(other_rows.reshape(1, stored), VM), (other_columns.reshape(1, stored), VM)],
    )
    listed = [(own_list, SM), (other_list, SM)]

    def head_values(lo, hi, hot):
        total = jnp.dot(lo[0], hot[0], preferred_element_type=F32)
        for b in range(1, blocks):
            row = lo[b] if b < low else hi[b - low]
            total += jnp.dot(row, hot[b], preferred_element_type=F32)
        return total.astype(BF16)

    def rows_of(owner):
        names = jnp.broadcast_to(owner.astype(F32), (heads, heads))
        before = lax.broadcasted_iota(jnp.int32, (heads, heads), 0)
        after = lax.broadcasted_iota(jnp.int32, (heads, heads), 1)
        same = jnp.logical_and(names.T == names, before < after)
        slot = jnp.sum(jnp.where(same, 1.0, 0.0), axis=0, keepdims=True).astype(jnp.int32)
        return owner * slots + slot

    def one_hots(vertex, count, out):
        node = lax.broadcasted_iota(jnp.int32, (nodes, heads), 0)
        for b in range(count):
            out[b] = jnp.where(node + b * nodes == vertex, 1.0, 0.0).astype(BF16)

    def place_rows(owner, keep, out):
        row = lax.broadcasted_iota(jnp.int32, (network * slots, heads), 0)
        out[...] = jnp.where(row == jnp.where(keep, rows_of(owner), -1), 1.0, 0.0).astype(BF16)

    place_type = array((network * slots, heads), BF16)

    def prepare_body(vertex, owner, lo, hi, trans, matrix, hot, head, place, product):
        one_hots(vertex[...], blocks, hot)
        head[...] = head_values(lo, hi, hot)
        place_rows(owner[...], True, place)
        product[...] = jnp.dot(
            trans[...].astype(BF16), matrix[...], preferred_element_type=F32
        )

    own_owner = distribution_entry_holder.reshape(1, heads)
    hot, head0, place, product = kernel(
        prepare_body,
        (
            array(hot_shape, BF16),
            array((cases, heads), BF16),
            place_type,
            hbm_array(highvoltage_costate.shape, F32),
        ),
        [(distribution_entry_vertex.reshape(1, heads), VM), (own_owner, VM), (lo, VM), (hi, VM)]
        + [(highvoltage_costate, VM), (highvoltage_derivative_matrix, VM)],
    )

    def rim_first_body(lists, acc, lo, hi, other, out, sums):
        sums[...] = acc[blocks:]
        run(
            lists,
            [((1, 0), hi, other, sums), ((1, 1), lo, other, sums)],
            FEW,
        )
        out[...] = sums[...].astype(BF16)

    (leaving,) = kernel(
        with_lists(rim_first_body),
        (array((rim, cases, nodes), BF16),),
        listed + [(acc, VM), (lo, VM), (hi, VM), (other, VM)],
        scratch=[pltpu.VMEM((rim, cases, nodes), F32)],
    )
    arriving = lax.ppermute(leaving, "blk", onward)

    mine = jnp.concatenate(
        [
            distribution_entry_vertex.reshape(1, heads),
            own_owner,
            distribution_entry_substation.reshape(1, heads),
        ],
        axis=1,
    )
    theirs = lax.ppermute(mine, "blk", backward)

    def begin_next(lists, lam, icar, outflow, own, other, acc, acc_rim, hi):
        for b in range(blocks):
            acc[b] = outflow[b : b + 1, :] * icar[b]
        for b in range(rim):
            acc_rim[b] = jnp.zeros((cases, nodes), F32)
        for b in range(low, blocks):
            hi[b - low] = lam[b].astype(BF16)
        hi[blocks - low] = jnp.zeros((cases, nodes), BF16)
        run(lists, [((0, 0), hi, own, acc_rim), ((1, 0), hi, other, acc_rim)], FEW)
        run(lists, [((0, 2), hi, own, acc), ((1, 2), hi, other, acc)], MANY)

    def main_first_body(
        lists, acc, lo, hi, own, other, lam_in, icar_in, decay_in, inflow_in, outflow_in,
        lam_next, acc_next, acc_rim, hi_next, icar_next, decay, inflow, outflow, other_kept,
        lam, icar, sems,
    ):
        pairs = [
            (icar_in, icar), (outflow_in, outflow), (lam_in, lam), (decay_in, decay), (inflow_in, inflow)
        ]
        copies = [pltpu.make_async_copy(a, b, sems.at[i]) for i, (a, b) in enumerate(pairs)]
        kept = pltpu.make_async_copy(other, other_kept, sems.at[5])
        for copy in copies + [kept]:
            copy.start()
        lam_next[...] = acc[:blocks]
        run(
            lists,
            [((1, 2), hi, other, lam_next), ((1, 3), lo, other, lam_next)],
            MANY,
        )
        for copy in copies:
            copy.wait()
        for b in range(blocks):
            lam_next[b] += outflow[b : b + 1, :] * icar[b]
            icar_next[b] = decay[b : b + 1, :] * icar[b] + inflow[b : b + 1, :] * lam[b]
        begin_next(
            lists, lam_next, icar_next, outflow, own, other, acc_next, acc_rim, hi_next
        )
        kept.wait()

    factor = array(factor_shape, F32)
    lam, acc, acc_rim, hi_next, icar, decay, inflow, outflow, other_kept = kernel(
        with_lists(main_first_body),
        (
            array(state, F32),
            array(state, F32),
            array((rim, cases, nodes), F32),
            array(padded, BF16),
            array(state, F32),
            factor,
            factor,
            factor,
            hbm_array(other.shape, BF16),
        ),
        listed
        + [(acc, VM), (lo, VM), (hi, VM), (own, VM), (other, VM)]
        + [(vertex_costate, HB), (inverter_costate, HB), (inverter_decay_factor, HB)]
        + [(costate_to_inverter_factor, HB), (inverter_to_costate_factor, HB)],
        scratch=[pltpu.VMEM(state, F32), pltpu.VMEM(state, F32), pltpu.SemaphoreType.DMA((6,))],
        out_specs=(VM,) * 8 + (HB,),
    )

    def take_arrived(arrived, lam, low_rows, lo):
        keep = lax.axis_index("blk") > 0
        for b in range(low):
            row = lam[b] + jnp.where(keep, arrived[b].astype(F32), 0.0)
            low_rows[b] = row
            lo[b] = row.astype(BF16)
        lo[low] = jnp.zeros((cases, nodes), BF16)

    def rim_sums(lists, acc_rim, lo, own, other, out, sums):
        sums[...] = acc_rim[...]
        run(lists, [((0, 1), lo, own, sums), ((1, 1), lo, other, sums)], FEW)
        out[...] = sums[...].astype(BF16)

    def rim_body(lists, arrived, lam, acc_rim, own, other, out, low_rows, lo, sums):
        take_arrived(arrived, lam, low_rows, lo)
        rim_sums(lists, acc_rim, lo, own, other, out, sums)

    def start_copies(lists, side, kind, first, count, source, dest, at, sem):
        def one(i, carry):
            c = word_of(lists, side, kind, first + i)
            pltpu.make_async_copy(source.at[c & 255], dest.at[at + i], sem).start()
            return carry

        lax.fori_loop(0, count, one, 0)

    def finish_copies(count, source, dest, sem):
        def one(i, carry):
            pltpu.make_async_copy(source.at[0], dest.at[0], sem).wait()
            return carry

        lax.fori_loop(0, count, one, 0)

    def run_copied(lists, first, count, lam, source, acc, width):
        total = count[0] + count[1]

        def some(i, carry):
            words = []
            for u in range(width):
                j = i * width + u
                is_own = j < count[0]
                at = jnp.where(is_own, first[0] + j, first[1] + j - count[0])
                at = jnp.clip(at, 0, STRIDE - 1)
                word = jnp.where(is_own, word_of(lists, 0, 1, at), word_of(lists, 1, 1, at))
                words.append((jnp.where(j < total, word, low << 8), jnp.minimum(j, total - 1)))
            prods = [
                jnp.dot(lam[(c >> 8) & 255], source[j], preferred_element_type=F32)
                for c, j in words
            ]
            for (c, _), prod in zip(words, prods):
                acc[c >> 16] += prod
            return carry

        lax.fori_loop(0, (total + width - 1) // width, some, 0)

    def rim_last_body(
        lists, arrived, lam, acc_rim, kept, own_in, other_in, out, low_rows, lo, sums, rest, sem
    ):
        count_own = count_of(lists, 0, 1)
        count_other = count_of(lists, 1, 1)
        keep_own = jnp.minimum(count_own, KEEP)
        keep_other = jnp.minimum(count_other, KEEP - keep_own)
        more_own = count_own - keep_own
        more_other = count_other - keep_other
        start_copies(lists, 0, 1, keep_own, more_own, own_in, rest, 0, sem)
        start_copies(lists, 1, 1, keep_other, more_other, other_in, rest, more_own, sem)
        take_arrived(arrived, lam, low_rows, lo)
        sums[...] = acc_rim[...]
        run_copied(lists, (0, 0), (keep_own, keep_other), lo, kept, sums, MANY)
        finish_copies(more_own + more_other, own_in, rest, sem)
        run_copied(
            lists, (keep_own, keep_other), (more_own, more_other), lo, rest, sums, FEW
        )
        out[...] = sums[...].astype(BF16)

    def main_body(
        lists, bus, theirs, left, low_rows, lam, lo, hi, acc, icar, own, other,
        hot, head0, place, decay, inflow,
        lam_low, acc_rim, sent, kept, icar_out, lam_out, hi_out,
        icar_next, lo_base, lam_next, hi_next, hot_next, place_next, sems,
    ):
        keep_own = jnp.minimum(count_of(lists, 0, 1), KEEP)
        keep_other = jnp.minimum(count_of(lists, 1, 1), KEEP - keep_own)
        for b in range(blocks):
            row = low_rows[b] if b < low else lam[b]
            icar_next[b] = decay[b : b + 1, :] * icar[b] + inflow[b : b + 1, :] * row
        icar_copy = pltpu.make_async_copy(icar_next, icar_out, sems.at[0])
        icar_copy.start()
        lam_next[...] = acc[...]
        run(lists, [((0, 3), lo, own, lam_next), ((1, 3), lo, other, lam_next)], MANY)
        upper = pl.ds(low, blocks - low)
        lam_copy = pltpu.make_async_copy(lam_next.at[upper], lam_out, sems.at[1])
        lam_copy.start()
        for b in range(low):
            lam_low[b] = lam_next[b]
            lo_base[b] = lam_next[b].astype(BF16)
        for b in range(low, blocks):
            hi_next[b - low] = lam_next[b].astype(BF16)
        hi_next[blocks - low] = jnp.zeros((cases, nodes), BF16)
        hi_copy = pltpu.make_async_copy(hi_next, hi_out, sems.at[2])
        hi_copy.start()
        acc_rim[...] = jnp.zeros(acc_rim.shape, F32)
        run(lists, [((0, 0), hi_next, own, acc_rim), ((1, 0), hi_next, other, acc_rim)], FEW)
        followed = lax.axis_index("blk") < owners - 1
        one_hots(theirs[:, :heads], low, hot_next)
        place_rows(theirs[:, heads : 2 * heads], followed, place_next)
        head_next = jnp.dot(left[0], hot_next[0], preferred_element_type=F32)
        for b in range(1, low):
            head_next += jnp.dot(left[b], hot_next[b], preferred_element_type=F32)
        width = (nodes - cases, heads)
        label = jnp.broadcast_to((bus[...] + 1).astype(F32), width).astype(BF16)
        bus_next = theirs[:, 2 * heads : 3 * heads]
        label_next = jnp.broadcast_to((bus_next + 1).astype(F32), width).astype(BF16)
        pairs = [
            (place, head0[...], head_values(lo, hi, hot)),
            (place, head_values(lo_base, hi_next, hot), label),
            (place_next, head_next.astype(BF16), label_next),
        ]
        for i, (where, first_half, second_half) in enumerate(pairs):
            part = lax.dot_general(
                where[...],
                jnp.concatenate([first_half, second_half], axis=0),
                (((1,), (1,)), ((), ())),
                preferred_element_type=F32,
            )
            sent[:, i] = part.astype(BF16).reshape(network, slots, nodes)

        def keep_own_block(i, carry):
            kept[i] = own[word_of(lists, 0, 1, i) & 255]
            return carry

        def keep_other_block(i, carry):
            kept[keep_own + i] = other[word_of(lists, 1, 1, i) & 255]
            return carry

        lax.fori_loop(0, keep_own, keep_own_block, 0)
        lax.fori_loop(0, keep_other, keep_other_block, 0)
        icar_copy.wait()
        lam_copy.wait()
        hi_copy.wait()

    tiles = [(own, VM), (other, VM)]
    rim_type = array((rim, cases, nodes), BF16)
    low_type = array(half, F32)
    sums = pltpu.VMEM((rim, cases, nodes), F32)
    assert STEPS == 3
    hi = hi_next
    leaving, low_rows, lo = kernel(
        with_lists(rim_body),
        (rim_type, low_type, array(padded, BF16)),
        listed + [(arriving, VM), (lam, VM), (acc_rim, VM)] + tiles,
        scratch=[sums],
    )
    arriving = lax.ppermute(leaving, "blk", onward)
    lam_low, acc_rim, sent, kept, icar, lam_high, hi_next = kernel(
        with_lists(main_body),
        (
            low_type,
            array((rim, cases, nodes), F32),
            array((network, 3, slots, nodes), BF16),
            array((KEEP, nodes, nodes), BF16),
            hbm_array(state, F32),
            hbm_array((blocks - low, cases, nodes), F32),
            hbm_array(padded, BF16),
        ),
        listed
        + [(distribution_entry_substation.reshape(1, heads), VM), (theirs, VM), (leaving, VM)]
        + [(low_rows, VM), (lam, VM), (lo, VM), (hi, VM), (acc, VM), (icar, VM)]
        + tiles
        + [(hot, VM), (head0, VM), (place, VM)]
        + [(decay, VM), (inflow, VM)],
        scratch=[
            pltpu.VMEM(state, F32),
            pltpu.VMEM(half, BF16),
            pltpu.VMEM(state, F32),
            pltpu.VMEM(padded, BF16),
            pltpu.VMEM((low, nodes, heads), BF16),
            pltpu.VMEM(place_type.shape, BF16),
            pltpu.SemaphoreType.DMA((3,)),
        ],
        out_specs=(VM,) * 4 + (HB,) * 3,
    )
    received = lax.all_to_all(
        sent.reshape(network, 3 * slots, nodes),
        ("sec", "blk"),
        split_axis=0,
        concat_axis=0,
        tiled=True,
    )
    received = received.reshape(rows_sent, nodes)
    stored_in = [(derivative_tiles, HB), (other_kept, HB)]
    fetched_shape = (2 * stored, nodes, nodes)
    leaving, low_rows, lo = kernel(
        with_lists(rim_last_body),
        (rim_type, low_type, array(padded, BF16)),
        listed + [(arriving, VM), (lam_low, VM), (acc_rim, VM), (kept, VM)] + stored_in,
        scratch=[sums, pltpu.VMEM(fetched_shape, BF16), pltpu.SemaphoreType.DMA],
    )
    arriving = lax.ppermute(leaving, "blk", onward[:-1])

    def main_last_body(
        lists, low_rows, lam_high, lo, hi, decay, inflow, outflow, own, other, icar,
        lam_out, low_next, icar_out, lam_next, icar_next, sems,
    ):
        for b in range(blocks):
            row = low_rows[b] if b < low else lam_high[b - low]
            before = icar[b]
            lam_next[b] = outflow[b : b + 1, :] * before
            icar_next[b] = decay[b : b + 1, :] * before + inflow[b : b + 1, :] * row
        icar_copy = pltpu.make_async_copy(icar_next, icar_out, sems.at[0])
        icar_copy.start()
        run(lists, [((0, 2), hi, own, lam_next), ((1, 2), hi, other, lam_next)], MANY)
        run(lists, [((0, 3), lo, own, lam_next), ((1, 3), lo, other, lam_next)], MANY)
        upper = pl.ds(low, blocks - low)
        lam_copy = pltpu.make_async_copy(lam_next.at[upper], lam_out.at[upper], sems.at[1])
        lam_copy.start()
        low_next[...] = lam_next[:low]
        icar_copy.wait()
        lam_copy.wait()

    lam, low_next, icar = kernel(
        with_lists(main_last_body),
        (hbm_array(state, F32), low_type, hbm_array(state, F32)),
        listed
        + [(low_rows, VM), (lam_high, VM), (lo, VM), (hi_next, VM)]
        + [(decay, VM), (inflow, VM), (outflow, VM)]
        + [(derivative_tiles, VM), (other_kept, VM), (icar, VM)],
        scratch=[
            pltpu.VMEM(state, F32),
            pltpu.VMEM(state, F32),
            pltpu.SemaphoreType.DMA((2,)),
        ],
        out_specs=(HB, VM, HB),
    )

    def trans_body(received, product, matrix, out):
        dims = (((0,), (0,)), ((), ()))
        if slots % 16 == 0:
            parts = received[...].reshape(network, 3, slots, nodes)
            part = [parts[:, i].reshape(network * slots, nodes) for i in range(3)]
            column = lax.broadcasted_iota(jnp.int32, (network * slots, buses), 1)

            def hot_of(rows):
                label = rows[:, cases : cases + 1].astype(F32).astype(jnp.int32) - 1
                return jnp.where(label == column, 1.0, 0.0).astype(BF16)

            hot = hot_of(part[1])
            first = lax.dot_general(part[0], hot, dims, preferred_element_type=F32)
            last = lax.dot_general(part[1], hot, dims, preferred_element_type=F32)
            last += lax.dot_general(part[2], hot_of(part[2]), dims, preferred_element_type=F32)
        else:
            got = received[...].astype(F32)
            row = lax.broadcasted_iota(jnp.int32, (rows_sent, buses), 0)
            place = lax.rem(row, 3 * slots)
            column = lax.broadcasted_iota(jnp.int32, (rows_sent, buses), 1)
            label = got[:, cases : cases + 1].astype(jnp.int32) - 1
            hot = jnp.where(jnp.logical_and(label == column, place >= slots), 1.0, 0.0)
            own_hot = jnp.where(place < 2 * slots, hot, 0.0)
            hot_a = pltpu.roll(own_hot, rows_sent - slots, 0).astype(BF16)
            first = lax.dot_general(received[...], hot_a, dims, preferred_element_type=F32)
            last = lax.dot_general(
                received[...], hot.astype(BF16), dims, preferred_element_type=F32
            )
        value = product[...] + first[:cases]
        for inj in (first[cases:], last[:cases]):
            value = jnp.dot(value.astype(BF16), matrix[...], preferred_element_type=F32) + inj
        out[...] = value

    (trans,) = kernel(
        trans_body,
        (array(highvoltage_costate.shape, F32),),
        [(received, VM), (product, VM), (highvoltage_derivative_matrix, VM)],
    )

    def last_body(arrived, low_next, lam_in, lam_out, rows, sems):
        del lam_in
        keep = lax.axis_index("blk") > 0
        copies = []
        part = low // 4
        for i in range(4):
            for b in range(i * part, (i + 1) * part):
                rows[b] = low_next[b] + jnp.where(keep, arrived[b].astype(F32), 0.0)
            here = pl.ds(i * part, part)
            copies.append(pltpu.make_async_copy(rows.at[here], lam_out.at[here], sems.at[i]))
            copies[-1].start()
        for copy in copies:
            copy.wait()

    (lam,) = kernel(
        last_body,
        (array(state, F32),),
        [(arriving, VM), (low_next, VM), (lam, HB)],
        scratch=[pltpu.VMEM(half, F32), pltpu.SemaphoreType.DMA((4,))],
        out_specs=(HB,),
        aliases={2: 0},
    )
    return (lam, icar, trans)


def solution(mesh):
    placed = (
        P(("sec", "blk"), "case", None),
        P(("sec", "blk"), "case", None),
        P("case", ("sec", "blk")),
        P(("sec", "blk", "case"), None, None),
        P(("sec", "blk", "case")),
        P(("sec", "blk", "case")),
        P(("sec", "blk"), None),
        P(("sec", "blk"), None),
        P(("sec", "blk"), None),
        P(("sec", "blk")),
        P(("sec", "blk"), None),
        P(("sec", "blk")),
        P(("sec", "blk"), None),
    )

    return jax.shard_map(
        local,
        mesh=mesh,
        in_specs=placed,
        out_specs=(
            P(("sec", "blk"), "case", None),
            P(("sec", "blk"), "case", None),
            P("case", ("sec", "blk")),
        ),
        check_vma=False,
    )
```

```python
import jax
import jax.numpy as jnp
from jax import lax
from jax.experimental import pallas as pl
from jax.experimental.pallas import tpu as pltpu
from jax.sharding import PartitionSpec as P


STEPS = 3
UNROLL = 16
FEW = 24
MANY = 40
KEEP = 44
CLASSES = 4
VMEM_LIMIT = 24 << 20

F32 = jnp.float32
BF16 = jnp.bfloat16
VM = pl.BlockSpec(memory_space=pltpu.VMEM)
SM = pl.BlockSpec(memory_space=pltpu.SMEM)
HB = pl.BlockSpec(memory_space=pltpu.HBM)
STRIDE = 128


def kernel(body, outs, ins, scratch=(), out_specs=None, aliases=None):
    return pl.pallas_call(
        body,
        out_shape=outs,
        in_specs=[spec for _, spec in ins],
        out_specs=out_specs or tuple(VM for _ in outs),
        scratch_shapes=list(scratch),
        input_output_aliases=aliases or {},
        compiler_params=pltpu.CompilerParams(vmem_limit_bytes=VMEM_LIMIT),
    )(*[in_hbm(array) if spec is HB else array for array, spec in ins])


def with_lists(body):
    return lambda own, other, *refs: body((own, other), *refs)


def in_hbm(array):
    return pltpu.with_memory_space_constraint(array, pltpu.HBM)


def array(shape, dtype):
    return jax.ShapeDtypeStruct(shape, dtype)


def hbm_array(shape, dtype):
    return pltpu.HBM(shape, dtype)


def local(
    vertex_costate,
    inverter_costate,
    highvoltage_costate,
    derivative_tiles,
    tile_source_index,
    tile_target_index,
    inverter_decay_factor,
    costate_to_inverter_factor,
    inverter_to_costate_factor,
    distribution_entry_vertex,
    distribution_entry_holder,
    distribution_entry_substation,
    highvoltage_derivative_matrix,
):
    blocks, cases, nodes = vertex_costate.shape
    rim = blocks // 2
    low = blocks // 2
    targets = blocks + rim
    stored = derivative_tiles.shape[0]
    sections = lax.axis_size("sec")
    owners = lax.axis_size("blk")
    network = sections * owners
    heads = distribution_entry_vertex.shape[0]
    slots = max(2, 2 * heads // network)
    buses = highvoltage_derivative_matrix.shape[1]
    rows_sent = network * 3 * slots
    assert -(-stored // MANY) * MANY <= STRIDE and -(-stored // FEW) * FEW <= STRIDE

    state = (blocks, cases, nodes)
    half = (low, cases, nodes)
    padded = (low + 1, cases, nodes)
    acc_shape = (targets, cases, nodes)
    hot_shape = (blocks, nodes, heads)
    swap = [(0, 1), (1, 0)]
    onward = [(i, (i + 1) % owners) for i in range(owners)]
    backward = [(j, i) for i, j in onward]

    own = derivative_tiles
    other_rows = lax.ppermute(tile_source_index, "case", swap)
    other_columns = lax.ppermute(tile_target_index, "case", swap)
    other = lax.ppermute(own, "case", swap)

    def sorted_list(rows, columns):
        is_low = jnp.where(rows < low, 1, 0)
        is_own = jnp.where(columns < blocks, 1, 0)
        kind = 2 * is_own + is_low
        place = lax.broadcasted_iota(jnp.int32, (1, stored), 1)
        word = place | ((rows - low * (1 - is_low)) << 8) | ((columns - blocks * (1 - is_own)) << 16)
        kind_row = jnp.broadcast_to(kind.astype(F32), (stored, stored))
        word_row = jnp.broadcast_to(word.astype(F32), (stored, stored))
        earlier = lax.broadcasted_iota(jnp.int32, (stored, stored), 0) > lax.broadcasted_iota(
            jnp.int32, (stored, stored), 1
        )
        kind_col = kind_row.T
        same = jnp.logical_and(kind_col == kind_row, earlier)
        rank = jnp.sum(jnp.where(same, 1.0, 0.0), axis=1, keepdims=True)
        spot = (kind_col[:, :1] * STRIDE + rank).astype(jnp.int32)
        hit = lax.broadcasted_iota(jnp.int32, (stored, CLASSES * STRIDE), 1) == spot
        words = jnp.sum(jnp.where(hit, word_row.T[:, :1], 0.0), axis=0, keepdims=True)
        taken = jnp.sum(jnp.where(hit, 1.0, 0.0), axis=0, keepdims=True)
        idle = jnp.full((1, CLASSES * STRIDE), low << 8, jnp.int32)
        lane = lax.broadcasted_iota(jnp.int32, (stored, 128), 1).astype(F32)
        counts = jnp.sum(jnp.where(kind_col[:, :1] == lane, 1.0, 0.0), axis=0, keepdims=True)
        return jnp.concatenate(
            [jnp.where(taken > 0, words.astype(jnp.int32), idle), counts.astype(jnp.int32)], axis=1
        )

    def word_of(lists, side, kind, i):
        return lists[side][0, kind * STRIDE + i]

    def count_of(lists, side, kind):
        return lists[side][0, CLASSES * STRIDE + kind]

    list_type = array((1, CLASSES * STRIDE + 128), jnp.int32)

    def run(lists, parts, width):
        def some(i, carry):
            words = [
                (word_of(lists, side, kind, i * width + u), lam, tiles, acc)
                for (side, kind), lam, tiles, acc in parts
                for u in range(width)
            ]
            prods = [
                jnp.dot(lam[(c >> 8) & 255], tiles[c & 255], preferred_element_type=F32)
                for c, lam, tiles, _ in words
            ]
            for (c, _, _, acc), prod in zip(words, prods):
                acc[c >> 16] += prod
            return carry

        longest = 0
        for (side, kind), _, _, _ in parts:
            longest = jnp.maximum(longest, count_of(lists, side, kind))
        lax.fori_loop(0, (longest + width - 1) // width, some, 0)

    def first_body(
        rows, columns, rows_in, columns_in, lam_in, own_in, acc, lo, hi, own_kept, listed,
        lam, lam_bf, rows_kept, columns_kept, sems,
    ):
        chunks = stored // UNROLL
        early = [
            pltpu.make_async_copy(rows_in, rows_kept, sems.at[chunks]),
            pltpu.make_async_copy(columns_in, columns_kept, sems.at[chunks + 1]),
            pltpu.make_async_copy(lam_in, lam, sems.at[chunks + 2]),
        ]
        copies = [
            pltpu.make_async_copy(
                own_in.at[pl.ds(i * UNROLL, UNROLL)], own_kept.at[pl.ds(i * UNROLL, UNROLL)], sems.at[i]
            )
            for i in range(chunks)
        ]
        for copy in early + copies:
            copy.start()
        for b in range(targets):
            acc[b] = jnp.zeros((cases, nodes), F32)
        zero = jnp.zeros((cases, nodes), BF16)
        lo[low] = zero
        hi[blocks - low] = zero
        early[0].wait()
        early[1].wait()
        listed[...] = sorted_list(rows_kept[...], columns_kept[...])
        early[2].wait()
        for b in range(blocks):
            rounded = lam[b].astype(BF16)
            lam_bf[b] = rounded
            if b < low:
                lo[b] = rounded
            else:
                hi[b - low] = rounded
        for i, copy in enumerate(copies):
            copy.wait()
            prods = [
                jnp.dot(
                    lam_bf[rows[i * UNROLL + u]],
                    own_kept[i * UNROLL + u],
                    preferred_element_type=F32,
                )
                for u in range(UNROLL)
            ]
            for u, prod in enumerate(prods):
                acc[columns[i * UNROLL + u]] += prod

    acc, lo, hi, own, own_list = kernel(
        first_body,
        (
            array(acc_shape, F32),
            array(padded, BF16),
            array(padded, BF16),
            array(own.shape, BF16),
            list_type,
        ),
        [
            (tile_source_index, SM),
            (tile_target_index, SM),
            (tile_source_index.reshape(1, stored), HB),
            (tile_target_index.reshape(1, stored), HB),
            (vertex_costate, HB),
            (own, HB),
        ],
        scratch=[
            pltpu.VMEM(state, F32),
            pltpu.VMEM(state, BF16),
            pltpu.VMEM((1, stored), jnp.int32),
            pltpu.VMEM((1, stored), jnp.int32),
            pltpu.SemaphoreType.DMA((stored // UNROLL + 3,)),
        ],
    )

    def sort_body(rows, columns, listed):
        listed[...] = sorted_list(rows[...], columns[...])

    (other_list,) = kernel(
        sort_body,
        (list_type,),
        [(other_rows.reshape(1, stored), VM), (other_columns.reshape(1, stored), VM)],
    )
    listed = [(own_list, SM), (other_list, SM)]

    def head_values(lo, hi, hot):
        total = jnp.dot(lo[0], hot[0], preferred_element_type=F32)
        for b in range(1, blocks):
            row = lo[b] if b < low else hi[b - low]
            total += jnp.dot(row, hot[b], preferred_element_type=F32)
        return total.astype(BF16)

    def rows_of(owner):
        names = jnp.broadcast_to(owner.astype(F32), (heads, heads))
        before = lax.broadcasted_iota(jnp.int32, (heads, heads), 0)
        after = lax.broadcasted_iota(jnp.int32, (heads, heads), 1)
        same = jnp.logical_and(names.T == names, before < after)
        slot = jnp.sum(jnp.where(same, 1.0, 0.0), axis=0, keepdims=True).astype(jnp.int32)
        return owner * slots + slot

    def one_hots(vertex, count, out):
        node = lax.broadcasted_iota(jnp.int32, (nodes, heads), 0)
        for b in range(count):
            out[b] = jnp.where(node + b * nodes == vertex, 1.0, 0.0).astype(BF16)

    def place_rows(owner, keep, out):
        row = lax.broadcasted_iota(jnp.int32, (network * slots, heads), 0)
        out[...] = jnp.where(row == jnp.where(keep, rows_of(owner), -1), 1.0, 0.0).astype(BF16)

    place_type = array((network * slots, heads), BF16)

    def prepare_body(vertex, owner, lo, hi, trans, matrix, hot, head, place, product):
        one_hots(vertex[...], blocks, hot)
        head[...] = head_values(lo, hi, hot)
        place_rows(owner[...], True, place)
        product[...] = jnp.dot(
            trans[...].astype(BF16), matrix[...], preferred_element_type=F32
        )

    own_owner = distribution_entry_holder.reshape(1, heads)
    hot, head0, place, product = kernel(
        prepare_body,
        (
            array(hot_shape, BF16),
            array((cases, heads), BF16),
            place_type,
            hbm_array(highvoltage_costate.shape, F32),
        ),
        [(distribution_entry_vertex.reshape(1, heads), VM), (own_owner, VM), (lo, VM), (hi, VM)]
        + [(highvoltage_costate, VM), (highvoltage_derivative_matrix, VM)],
    )

    def rim_first_body(lists, acc, lo, hi, other, out, sums):
        sums[...] = acc[blocks:]
        run(
            lists,
            [((1, 0), hi, other, sums), ((1, 1), lo, other, sums)],
            FEW,
        )
        out[...] = sums[...].astype(BF16)

    (leaving,) = kernel(
        with_lists(rim_first_body),
        (array((rim, cases, nodes), BF16),),
        listed + [(acc, VM), (lo, VM), (hi, VM), (other, VM)],
        scratch=[pltpu.VMEM((rim, cases, nodes), F32)],
    )
    arriving = lax.ppermute(leaving, "blk", onward[:-1])

    mine = jnp.concatenate(
        [
            distribution_entry_vertex.reshape(1, heads),
            own_owner,
            distribution_entry_substation.reshape(1, heads),
        ],
        axis=1,
    )
    theirs = lax.ppermute(mine, "blk", backward)

    def begin_next(lists, lam, icar, outflow, own, other, acc, acc_rim, hi):
        for b in range(blocks):
            acc[b] = outflow[b : b + 1, :] * icar[b]
        for b in range(rim):
            acc_rim[b] = jnp.zeros((cases, nodes), F32)
        for b in range(low, blocks):
            hi[b - low] = lam[b].astype(BF16)
        hi[blocks - low] = jnp.zeros((cases, nodes), BF16)
        run(lists, [((0, 0), hi, own, acc_rim), ((1, 0), hi, other, acc_rim)], FEW)
        run(lists, [((0, 2), hi, own, acc), ((1, 2), hi, other, acc)], MANY)

    def main_first_body(
        lists, acc, lo, hi, own, other, lam, icar, decay, inflow, outflow,
        lam_next, acc_next, acc_rim, hi_next, icar_next, other_kept, sem,
    ):
        kept = pltpu.make_async_copy(other, other_kept, sem)
        kept.start()
        for b in range(blocks):
            lam_next[b] = acc[b] + outflow[b : b + 1, :] * icar[b]
            icar_next[b] = decay[b : b + 1, :] * icar[b] + inflow[b : b + 1, :] * lam[b]
        run(lists, [((1, 2), hi, other, lam_next), ((1, 3), lo, other, lam_next)], MANY)
        begin_next(
            lists, lam_next, icar_next, outflow, own, other, acc_next, acc_rim, hi_next
        )
        kept.wait()

    decay, inflow, outflow = (
        inverter_decay_factor, costate_to_inverter_factor, inverter_to_costate_factor
    )
    lam, acc, acc_rim, hi_next, icar, other_kept = kernel(
        with_lists(main_first_body),
        (
            array(state, F32),
            array(state, F32),
            array((rim, cases, nodes), F32),
            array(padded, BF16),
            array(state, F32),
            hbm_array(other.shape, BF16),
        ),
        listed
        + [(acc, VM), (lo, VM), (hi, VM), (own, VM), (other, VM)]
        + [(vertex_costate, VM), (inverter_costate, VM), (decay, VM), (inflow, VM), (outflow, VM)],
        scratch=[pltpu.SemaphoreType.DMA],
        out_specs=(VM,) * 5 + (HB,),
    )

    def take_arrived(arrived, lam, low_rows, lo):
        keep = lax.axis_index("blk") > 0
        for b in range(low):
            row = lam[b] + jnp.where(keep, arrived[b].astype(F32), 0.0)
            low_rows[b] = row
            lo[b] = row.astype(BF16)
        lo[low] = jnp.zeros((cases, nodes), BF16)

    def rim_sums(lists, acc_rim, lo, own, other, out, sums):
        sums[...] = acc_rim[...]
        run(lists, [((0, 1), lo, own, sums), ((1, 1), lo, other, sums)], FEW)
        out[...] = sums[...].astype(BF16)

    def rim_body(lists, arrived, lam, acc_rim, own, other, out, low_rows, lo, sums):
        take_arrived(arrived, lam, low_rows, lo)
        rim_sums(lists, acc_rim, lo, own, other, out, sums)

    def start_copies(lists, side, kind, first, count, source, dest, at, sem):
        def one(i, carry):
            c = word_of(lists, side, kind, first + i)
            pltpu.make_async_copy(source.at[c & 255], dest.at[at + i], sem).start()
            return carry

        lax.fori_loop(0, count, one, 0)

    def finish_copies(count, source, dest, sem):
        def one(i, carry):
            pltpu.make_async_copy(source.at[0], dest.at[0], sem).wait()
            return carry

        lax.fori_loop(0, count, one, 0)

    def run_copied(lists, first, count, lam, source, acc, width):
        total = count[0] + count[1]

        def some(i, carry):
            words = []
            for u in range(width):
                j = i * width + u
                is_own = j < count[0]
                at = jnp.where(is_own, first[0] + j, first[1] + j - count[0])
                at = jnp.clip(at, 0, STRIDE - 1)
                word = jnp.where(is_own, word_of(lists, 0, 1, at), word_of(lists, 1, 1, at))
                words.append((jnp.where(j < total, word, low << 8), jnp.minimum(j, total - 1)))
            prods = [
                jnp.dot(lam[(c >> 8) & 255], source[j], preferred_element_type=F32)
                for c, j in words
            ]
            for (c, _), prod in zip(words, prods):
                acc[c >> 16] += prod
            return carry

        lax.fori_loop(0, (total + width - 1) // width, some, 0)

    def rim_last_body(
        lists, arrived, lam, acc_rim, kept, own_in, other_in, out, low_rows, lo, sums, rest, sem
    ):
        count_own = count_of(lists, 0, 1)
        count_other = count_of(lists, 1, 1)
        keep_own = jnp.minimum(count_own, KEEP)
        keep_other = jnp.minimum(count_other, KEEP - keep_own)
        more_own = count_own - keep_own
        more_other = count_other - keep_other
        start_copies(lists, 0, 1, keep_own, more_own, own_in, rest, 0, sem)
        start_copies(lists, 1, 1, keep_other, more_other, other_in, rest, more_own, sem)
        take_arrived(arrived, lam, low_rows, lo)
        sums[...] = acc_rim[...]
        run_copied(lists, (0, 0), (keep_own, keep_other), lo, kept, sums, MANY)
        finish_copies(more_own + more_other, own_in, rest, sem)
        run_copied(
            lists, (keep_own, keep_other), (more_own, more_other), lo, rest, sums, FEW
        )
        out[...] = sums[...].astype(BF16)

    def main_body(
        lists, bus, theirs, left, low_rows, lam, lo, hi, acc, icar, own, other,
        hot, head0, place, decay, inflow,
        lam_low, acc_rim, sent, kept, icar_out, lam_out, hi_out,
        icar_next, lo_base, lam_next, hi_next, hot_next, place_next, sems,
    ):
        keep_own = jnp.minimum(count_of(lists, 0, 1), KEEP)
        keep_other = jnp.minimum(count_of(lists, 1, 1), KEEP - keep_own)
        for b in range(blocks):
            row = low_rows[b] if b < low else lam[b]
            icar_next[b] = decay[b : b + 1, :] * icar[b] + inflow[b : b + 1, :] * row
        icar_copy = pltpu.make_async_copy(icar_next, icar_out, sems.at[0])
        icar_copy.start()
        lam_next[...] = acc[...]
        run(lists, [((0, 3), lo, own, lam_next), ((1, 3), lo, other, lam_next)], MANY)
        upper = pl.ds(low, blocks - low)
        lam_copy = pltpu.make_async_copy(lam_next.at[upper], lam_out, sems.at[1])
        lam_copy.start()
        for b in range(low):
            lam_low[b] = lam_next[b]
            lo_base[b] = lam_next[b].astype(BF16)
        for b in range(low, blocks):
            hi_next[b - low] = lam_next[b].astype(BF16)
        hi_next[blocks - low] = jnp.zeros((cases, nodes), BF16)
        hi_copy = pltpu.make_async_copy(hi_next, hi_out, sems.at[2])
        hi_copy.start()
        acc_rim[...] = jnp.zeros(acc_rim.shape, F32)
        run(lists, [((0, 0), hi_next, own, acc_rim), ((1, 0), hi_next, other, acc_rim)], FEW)
        followed = lax.axis_index("blk") < owners - 1
        one_hots(theirs[:, :heads], low, hot_next)
        place_rows(theirs[:, heads : 2 * heads], followed, place_next)
        head_next = jnp.dot(left[0], hot_next[0], preferred_element_type=F32)
        for b in range(1, low):
            head_next += jnp.dot(left[b], hot_next[b], preferred_element_type=F32)
        width = (nodes - cases, heads)
        label = jnp.broadcast_to((bus[...] + 1).astype(F32), width).astype(BF16)
        bus_next = theirs[:, 2 * heads : 3 * heads]
        label_next = jnp.broadcast_to((bus_next + 1).astype(F32), width).astype(BF16)
        pairs = [
            (place, head0[...], head_values(lo, hi, hot)),
            (place, head_values(lo_base, hi_next, hot), label),
            (place_next, head_next.astype(BF16), label_next),
        ]
        for i, (where, first_half, second_half) in enumerate(pairs):
            part = lax.dot_general(
                where[...],
                jnp.concatenate([first_half, second_half], axis=0),
                (((1,), (1,)), ((), ())),
                preferred_element_type=F32,
            )
            sent[:, i] = part.astype(BF16).reshape(network, slots, nodes)

        def keep_own_block(i, carry):
            kept[i] = own[word_of(lists, 0, 1, i) & 255]
            return carry

        def keep_other_block(i, carry):
            kept[keep_own + i] = other[word_of(lists, 1, 1, i) & 255]
            return carry

        lax.fori_loop(0, keep_own, keep_own_block, 0)
        lax.fori_loop(0, keep_other, keep_other_block, 0)
        icar_copy.wait()
        lam_copy.wait()
        hi_copy.wait()

    tiles = [(own, VM), (other, VM)]
    rim_type = array((rim, cases, nodes), BF16)
    low_type = array(half, F32)
    sums = pltpu.VMEM((rim, cases, nodes), F32)
    assert STEPS == 3
    hi = hi_next
    leaving, low_rows, lo = kernel(
        with_lists(rim_body),
        (rim_type, low_type, array(padded, BF16)),
        listed + [(arriving, VM), (lam, VM), (acc_rim, VM)] + tiles,
        scratch=[sums],
    )
    arriving = lax.ppermute(leaving, "blk", onward)
    lam_low, acc_rim, sent, kept, icar, lam_high, hi_next = kernel(
        with_lists(main_body),
        (
            low_type,
            array((rim, cases, nodes), F32),
            array((network, 3, slots, nodes), BF16),
            array((KEEP, nodes, nodes), BF16),
            hbm_array(state, F32),
            hbm_array((blocks - low, cases, nodes), F32),
            hbm_array(padded, BF16),
        ),
        listed
        + [(distribution_entry_substation.reshape(1, heads), VM), (theirs, VM), (leaving, VM)]
        + [(low_rows, VM), (lam, VM), (lo, VM), (hi, VM), (acc, VM), (icar, VM)]
        + tiles
        + [(hot, VM), (head0, VM), (place, VM)]
        + [(decay, VM), (inflow, VM)],
        scratch=[
            pltpu.VMEM(state, F32),
            pltpu.VMEM(half, BF16),
            pltpu.VMEM(state, F32),
            pltpu.VMEM(padded, BF16),
            pltpu.VMEM((low, nodes, heads), BF16),
            pltpu.VMEM(place_type.shape, BF16),
            pltpu.SemaphoreType.DMA((3,)),
        ],
        out_specs=(VM,) * 4 + (HB,) * 3,
    )
    received = lax.all_to_all(
        sent.reshape(network, 3 * slots, nodes),
        ("sec", "blk"),
        split_axis=0,
        concat_axis=0,
        tiled=True,
    )
    received = received.reshape(rows_sent, nodes)
    stored_in = [(derivative_tiles, HB), (other_kept, HB)]
    fetched_shape = (2 * stored, nodes, nodes)
    leaving, low_rows, lo = kernel(
        with_lists(rim_last_body),
        (rim_type, low_type, array(padded, BF16)),
        listed + [(arriving, VM), (lam_low, VM), (acc_rim, VM), (kept, VM)] + stored_in,
        scratch=[sums, pltpu.VMEM(fetched_shape, BF16), pltpu.SemaphoreType.DMA],
    )
    arriving = lax.ppermute(leaving, "blk", onward[:-1])

    def main_last_body(
        lists, low_rows, lam_high, lo, hi, decay, inflow, outflow, own, other, icar,
        lam_out, low_next, icar_out, lam_next, icar_next, sems,
    ):
        for b in range(blocks):
            row = low_rows[b] if b < low else lam_high[b - low]
            before = icar[b]
            lam_next[b] = outflow[b : b + 1, :] * before
            icar_next[b] = decay[b : b + 1, :] * before + inflow[b : b + 1, :] * row
        icar_copy = pltpu.make_async_copy(icar_next, icar_out, sems.at[0])
        icar_copy.start()
        run(lists, [((0, 2), hi, own, lam_next), ((1, 2), hi, other, lam_next)], MANY)
        run(lists, [((0, 3), lo, own, lam_next), ((1, 3), lo, other, lam_next)], MANY)
        upper = pl.ds(low, blocks - low)
        lam_copy = pltpu.make_async_copy(lam_next.at[upper], lam_out.at[upper], sems.at[1])
        lam_copy.start()
        low_next[...] = lam_next[:low]
        icar_copy.wait()
        lam_copy.wait()

    lam, low_next, icar = kernel(
        with_lists(main_last_body),
        (hbm_array(state, F32), low_type, hbm_array(state, F32)),
        listed
        + [(low_rows, VM), (lam_high, VM), (lo, VM), (hi_next, VM)]
        + [(decay, VM), (inflow, VM), (outflow, VM)]
        + [(derivative_tiles, VM), (other_kept, VM), (icar, VM)],
        scratch=[
            pltpu.VMEM(state, F32),
            pltpu.VMEM(state, F32),
            pltpu.SemaphoreType.DMA((2,)),
        ],
        out_specs=(HB, VM, HB),
    )

    def trans_body(received, product, matrix, out):
        dims = (((0,), (0,)), ((), ()))
        if slots % 16 == 0:
            parts = received[...].reshape(network, 3, slots, nodes)
            part = [parts[:, i].reshape(network * slots, nodes) for i in range(3)]
            column = lax.broadcasted_iota(jnp.int32, (network * slots, buses), 1)

            def hot_of(rows):
                label = rows[:, cases : cases + 1].astype(F32).astype(jnp.int32) - 1
                return jnp.where(label == column, 1.0, 0.0).astype(BF16)

            hot = hot_of(part[1])
            first = lax.dot_general(part[0], hot, dims, preferred_element_type=F32)
            last = lax.dot_general(part[1], hot, dims, preferred_element_type=F32)
            last += lax.dot_general(part[2], hot_of(part[2]), dims, preferred_element_type=F32)
        else:
            got = received[...].astype(F32)
            row = lax.broadcasted_iota(jnp.int32, (rows_sent, buses), 0)
            place = lax.rem(row, 3 * slots)
            column = lax.broadcasted_iota(jnp.int32, (rows_sent, buses), 1)
            label = got[:, cases : cases + 1].astype(jnp.int32) - 1
            hot = jnp.where(jnp.logical_and(label == column, place >= slots), 1.0, 0.0)
            own_hot = jnp.where(place < 2 * slots, hot, 0.0)
            hot_a = pltpu.roll(own_hot, rows_sent - slots, 0).astype(BF16)
            first = lax.dot_general(received[...], hot_a, dims, preferred_element_type=F32)
            last = lax.dot_general(
                received[...], hot.astype(BF16), dims, preferred_element_type=F32
            )
        value = product[...] + first[:cases]
        for inj in (first[cases:], last[:cases]):
            value = jnp.dot(value.astype(BF16), matrix[...], preferred_element_type=F32) + inj
        out[...] = value

    (trans,) = kernel(
        trans_body,
        (array(highvoltage_costate.shape, F32),),
        [(received, VM), (product, VM), (highvoltage_derivative_matrix, VM)],
    )

    def last_body(arrived, low_next, lam_in, lam_out, rows, sems):
        del lam_in
        keep = lax.axis_index("blk") > 0
        copies = []
        part = low // 4
        for i in range(4):
            for b in range(i * part, (i + 1) * part):
                rows[b] = low_next[b] + jnp.where(keep, arrived[b].astype(F32), 0.0)
            here = pl.ds(i * part, part)
            copies.append(pltpu.make_async_copy(rows.at[here], lam_out.at[here], sems.at[i]))
            copies[-1].start()
        for copy in copies:
            copy.wait()

    (lam,) = kernel(
        last_body,
        (array(state, F32),),
        [(arriving, VM), (low_next, VM), (lam, HB)],
        scratch=[pltpu.VMEM(half, F32), pltpu.SemaphoreType.DMA((4,))],
        out_specs=(HB,),
        aliases={2: 0},
    )
    return (lam, icar, trans)


def solution(mesh):
    placed = (
        P(("sec", "blk"), "case", None),
        P(("sec", "blk"), "case", None),
        P("case", ("sec", "blk")),
        P(("sec", "blk", "case"), None, None),
        P(("sec", "blk", "case")),
        P(("sec", "blk", "case")),
        P(("sec", "blk"), None),
        P(("sec", "blk"), None),
        P(("sec", "blk"), None),
        P(("sec", "blk")),
        P(("sec", "blk"), None),
        P(("sec", "blk")),
        P(("sec", "blk"), None),
    )

    return jax.shard_map(
        local,
        mesh=mesh,
        in_specs=placed,
        out_specs=(
            P(("sec", "blk"), "case", None),
            P(("sec", "blk"), "case", None),
            P("case", ("sec", "blk")),
        ),
        check_vma=False,
    )
```

```python
import jax
import jax.numpy as jnp
from jax import lax
from jax.experimental import pallas as pl
from jax.experimental.pallas import tpu as pltpu
from jax.sharding import PartitionSpec as P


STEPS = 3
UNROLL = 16
FEW = 28
MANY = 48
KEEP = 44
CLASSES = 4
VMEM_LIMIT = 24 << 20

F32 = jnp.float32
BF16 = jnp.bfloat16
VM = pl.BlockSpec(memory_space=pltpu.VMEM)
SM = pl.BlockSpec(memory_space=pltpu.SMEM)
HB = pl.BlockSpec(memory_space=pltpu.HBM)
STRIDE = 128


def kernel(body, outs, ins, scratch=(), out_specs=None, aliases=None):
    return pl.pallas_call(
        body,
        out_shape=outs,
        in_specs=[spec for _, spec in ins],
        out_specs=out_specs or tuple(VM for _ in outs),
        scratch_shapes=list(scratch),
        input_output_aliases=aliases or {},
        compiler_params=pltpu.CompilerParams(vmem_limit_bytes=VMEM_LIMIT),
    )(*[in_hbm(array) if spec is HB else array for array, spec in ins])


def with_lists(body):
    return lambda own, other, *refs: body((own, other), *refs)


def in_hbm(array):
    return pltpu.with_memory_space_constraint(array, pltpu.HBM)


def array(shape, dtype):
    return jax.ShapeDtypeStruct(shape, dtype)


def hbm_array(shape, dtype):
    return pltpu.HBM(shape, dtype)


def local(
    vertex_costate,
    inverter_costate,
    highvoltage_costate,
    derivative_tiles,
    tile_source_index,
    tile_target_index,
    inverter_decay_factor,
    costate_to_inverter_factor,
    inverter_to_costate_factor,
    distribution_entry_vertex,
    distribution_entry_holder,
    distribution_entry_substation,
    highvoltage_derivative_matrix,
):
    blocks, cases, nodes = vertex_costate.shape
    rim = blocks // 2
    low = blocks // 2
    targets = blocks + rim
    stored = derivative_tiles.shape[0]
    sections = lax.axis_size("sec")
    owners = lax.axis_size("blk")
    network = sections * owners
    heads = distribution_entry_vertex.shape[0]
    slots = max(2, 2 * heads // network)
    buses = highvoltage_derivative_matrix.shape[1]
    rows_sent = network * 3 * slots
    assert -(-stored // MANY) * MANY <= STRIDE and -(-stored // FEW) * FEW <= STRIDE

    state = (blocks, cases, nodes)
    half = (low, cases, nodes)
    padded = (low + 1, cases, nodes)
    acc_shape = (targets, cases, nodes)
    hot_shape = (blocks, nodes, heads)
    swap = [(0, 1), (1, 0)]
    onward = [(i, (i + 1) % owners) for i in range(owners)]
    backward = [(j, i) for i, j in onward]

    own = derivative_tiles
    other_rows = lax.ppermute(tile_source_index, "case", swap)
    other_columns = lax.ppermute(tile_target_index, "case", swap)
    other = lax.ppermute(own, "case", swap)

    def sorted_list(rows, columns):
        is_low = jnp.where(rows < low, 1, 0)
        is_own = jnp.where(columns < blocks, 1, 0)
        kind = 2 * is_own + is_low
        place = lax.broadcasted_iota(jnp.int32, (1, stored), 1)
        word = place | ((rows - low * (1 - is_low)) << 8) | ((columns - blocks * (1 - is_own)) << 16)
        kind_row = jnp.broadcast_to(kind.astype(F32), (stored, stored))
        word_row = jnp.broadcast_to(word.astype(F32), (stored, stored))
        earlier = lax.broadcasted_iota(jnp.int32, (stored, stored), 0) > lax.broadcasted_iota(
            jnp.int32, (stored, stored), 1
        )
        kind_col = kind_row.T
        same = jnp.logical_and(kind_col == kind_row, earlier)
        rank = jnp.sum(jnp.where(same, 1.0, 0.0), axis=1, keepdims=True)
        spot = (kind_col[:, :1] * STRIDE + rank).astype(jnp.int32)
        hit = lax.broadcasted_iota(jnp.int32, (stored, CLASSES * STRIDE), 1) == spot
        words = jnp.sum(jnp.where(hit, word_row.T[:, :1], 0.0), axis=0, keepdims=True)
        taken = jnp.sum(jnp.where(hit, 1.0, 0.0), axis=0, keepdims=True)
        idle = jnp.full((1, CLASSES * STRIDE), low << 8, jnp.int32)
        lane = lax.broadcasted_iota(jnp.int32, (stored, 128), 1).astype(F32)
        counts = jnp.sum(jnp.where(kind_col[:, :1] == lane, 1.0, 0.0), axis=0, keepdims=True)
        return jnp.concatenate(
            [jnp.where(taken > 0, words.astype(jnp.int32), idle), counts.astype(jnp.int32)], axis=1
        )

    def word_of(lists, side, kind, i):
        return lists[side][0, kind * STRIDE + i]

    def count_of(lists, side, kind):
        return lists[side][0, CLASSES * STRIDE + kind]

    list_type = array((1, CLASSES * STRIDE + 128), jnp.int32)

    def run(lists, parts, width):
        def some(i, carry):
            words = [
                (word_of(lists, side, kind, i * width + u), lam, tiles, acc)
                for (side, kind), lam, tiles, acc in parts
                for u in range(width)
            ]
            prods = [
                jnp.dot(lam[(c >> 8) & 255], tiles[c & 255], preferred_element_type=F32)
                for c, lam, tiles, _ in words
            ]
            for (c, _, _, acc), prod in zip(words, prods):
                acc[c >> 16] += prod
            return carry

        longest = 0
        for (side, kind), _, _, _ in parts:
            longest = jnp.maximum(longest, count_of(lists, side, kind))
        lax.fori_loop(0, (longest + width - 1) // width, some, 0)

    def first_body(
        rows, columns, rows_in, columns_in, lam_in, own_in, acc, lo, hi, own_kept, listed,
        lam, lam_bf, rows_kept, columns_kept, sems,
    ):
        chunks = stored // UNROLL
        early = [
            pltpu.make_async_copy(rows_in, rows_kept, sems.at[chunks]),
            pltpu.make_async_copy(columns_in, columns_kept, sems.at[chunks + 1]),
            pltpu.make_async_copy(lam_in, lam, sems.at[chunks + 2]),
        ]
        copies = [
            pltpu.make_async_copy(
                own_in.at[pl.ds(i * UNROLL, UNROLL)], own_kept.at[pl.ds(i * UNROLL, UNROLL)], sems.at[i]
            )
            for i in range(chunks)
        ]
        for copy in early + copies:
            copy.start()
        for b in range(targets):
            acc[b] = jnp.zeros((cases, nodes), F32)
        zero = jnp.zeros((cases, nodes), BF16)
        lo[low] = zero
        hi[blocks - low] = zero
        early[0].wait()
        early[1].wait()
        listed[...] = sorted_list(rows_kept[...], columns_kept[...])
        early[2].wait()
        for b in range(blocks):
            rounded = lam[b].astype(BF16)
            lam_bf[b] = rounded
            if b < low:
                lo[b] = rounded
            else:
                hi[b - low] = rounded
        for i, copy in enumerate(copies):
            copy.wait()
            prods = [
                jnp.dot(
                    lam_bf[rows[i * UNROLL + u]],
                    own_kept[i * UNROLL + u],
                    preferred_element_type=F32,
                )
                for u in range(UNROLL)
            ]
            for u, prod in enumerate(prods):
                acc[columns[i * UNROLL + u]] += prod

    acc, lo, hi, own, own_list = kernel(
        first_body,
        (
            array(acc_shape, F32),
            array(padded, BF16),
            array(padded, BF16),
            array(own.shape, BF16),
            list_type,
        ),
        [
            (tile_source_index, SM),
            (tile_target_index, SM),
            (tile_source_index.reshape(1, stored), HB),
            (tile_target_index.reshape(1, stored), HB),
            (vertex_costate, HB),
            (own, HB),
        ],
        scratch=[
            pltpu.VMEM(state, F32),
            pltpu.VMEM(state, BF16),
            pltpu.VMEM((1, stored), jnp.int32),
            pltpu.VMEM((1, stored), jnp.int32),
            pltpu.SemaphoreType.DMA((stored // UNROLL + 3,)),
        ],
    )

    def sort_body(rows, columns, listed):
        listed[...] = sorted_list(rows[...], columns[...])

    (other_list,) = kernel(
        sort_body,
        (list_type,),
        [(other_rows.reshape(1, stored), VM), (other_columns.reshape(1, stored), VM)],
    )
    listed = [(own_list, SM), (other_list, SM)]

    def head_values(lo, hi, hot):
        total = jnp.dot(lo[0], hot[0], preferred_element_type=F32)
        for b in range(1, blocks):
            row = lo[b] if b < low else hi[b - low]
            total += jnp.dot(row, hot[b], preferred_element_type=F32)
        return total.astype(BF16)

    def rows_of(owner):
        names = jnp.broadcast_to(owner.astype(F32), (heads, heads))
        before = lax.broadcasted_iota(jnp.int32, (heads, heads), 0)
        after = lax.broadcasted_iota(jnp.int32, (heads, heads), 1)
        same = jnp.logical_and(names.T == names, before < after)
        slot = jnp.sum(jnp.where(same, 1.0, 0.0), axis=0, keepdims=True).astype(jnp.int32)
        return owner * slots + slot

    def one_hots(vertex, count, out):
        node = lax.broadcasted_iota(jnp.int32, (nodes, heads), 0)
        for b in range(count):
            out[b] = jnp.where(node + b * nodes == vertex, 1.0, 0.0).astype(BF16)

    def place_rows(owner, keep, out):
        row = lax.broadcasted_iota(jnp.int32, (network * slots, heads), 0)
        out[...] = jnp.where(row == jnp.where(keep, rows_of(owner), -1), 1.0, 0.0).astype(BF16)

    place_type = array((network * slots, heads), BF16)

    def prepare_body(vertex, owner, lo, hi, trans, matrix, hot, head, place, product):
        one_hots(vertex[...], blocks, hot)
        head[...] = head_values(lo, hi, hot)
        place_rows(owner[...], True, place)
        product[...] = jnp.dot(
            trans[...].astype(BF16), matrix[...], preferred_element_type=F32
        )

    own_owner = distribution_entry_holder.reshape(1, heads)
    hot, head0, place, product = kernel(
        prepare_body,
        (
            array(hot_shape, BF16),
            array((cases, heads), BF16),
            place_type,
            hbm_array(highvoltage_costate.shape, F32),
        ),
        [(distribution_entry_vertex.reshape(1, heads), VM), (own_owner, VM), (lo, VM), (hi, VM)]
        + [(highvoltage_costate, VM), (highvoltage_derivative_matrix, VM)],
    )

    def rim_first_body(lists, acc, lo, hi, other, out, sums):
        sums[...] = acc[blocks:]
        run(
            lists,
            [((1, 0), hi, other, sums), ((1, 1), lo, other, sums)],
            FEW,
        )
        out[...] = sums[...].astype(BF16)

    (leaving,) = kernel(
        with_lists(rim_first_body),
        (array((rim, cases, nodes), BF16),),
        listed + [(acc, VM), (lo, VM), (hi, VM), (other, VM)],
        scratch=[pltpu.VMEM((rim, cases, nodes), F32)],
    )
    arriving = lax.ppermute(leaving, "blk", onward[:-1])

    mine = jnp.concatenate(
        [
            distribution_entry_vertex.reshape(1, heads),
            own_owner,
            distribution_entry_substation.reshape(1, heads),
        ],
        axis=1,
    )
    theirs = lax.ppermute(mine, "blk", backward)

    def prepare_next_body(theirs, hot, place, label):
        one_hots(theirs[:, :heads], low, hot)
        followed = lax.axis_index("blk") < owners - 1
        place_rows(theirs[:, heads : 2 * heads], followed, place)
        bus = (theirs[:, 2 * heads : 3 * heads] + 1).astype(F32)
        label[...] = jnp.broadcast_to(bus, (nodes - cases, heads)).astype(BF16)

    hot_next, place_next, label_next = kernel(
        prepare_next_body,
        (array((low, nodes, heads), BF16), place_type, array((nodes - cases, heads), BF16)),
        [(theirs, VM)],
    )

    def begin_next(lists, lam, icar, outflow, own, other, acc, acc_rim, hi):
        for b in range(blocks):
            acc[b] = outflow[b : b + 1, :] * icar[b]
        for b in range(rim):
            acc_rim[b] = jnp.zeros((cases, nodes), F32)
        for b in range(low, blocks):
            hi[b - low] = lam[b].astype(BF16)
        hi[blocks - low] = jnp.zeros((cases, nodes), BF16)
        run(lists, [((0, 0), hi, own, acc_rim), ((1, 0), hi, other, acc_rim)], FEW)
        run(lists, [((0, 2), hi, own, acc), ((1, 2), hi, other, acc)], MANY)

    def main_first_body(
        lists, acc, lo, hi, own, other, lam, icar, decay, inflow, outflow,
        lam_next, acc_next, acc_rim, hi_next, icar_next, other_kept, sem,
    ):
        kept = pltpu.make_async_copy(other, other_kept, sem)
        kept.start()
        for b in range(blocks):
            lam_next[b] = acc[b] + outflow[b : b + 1, :] * icar[b]
            icar_next[b] = decay[b : b + 1, :] * icar[b] + inflow[b : b + 1, :] * lam[b]
        run(lists, [((1, 2), hi, other, lam_next), ((1, 3), lo, other, lam_next)], MANY)
        begin_next(
            lists, lam_next, icar_next, outflow, own, other, acc_next, acc_rim, hi_next
        )
        kept.wait()

    decay, inflow, outflow = (
        inverter_decay_factor, costate_to_inverter_factor, inverter_to_costate_factor
    )
    lam, acc, acc_rim, hi_next, icar, other_kept = kernel(
        with_lists(main_first_body),
        (
            array(state, F32),
            array(state, F32),
            array((rim, cases, nodes), F32),
            array(padded, BF16),
            array(state, F32),
            hbm_array(other.shape, BF16),
        ),
        listed
        + [(acc, VM), (lo, VM), (hi, VM), (own, VM), (other, VM)]
        + [(vertex_costate, VM), (inverter_costate, VM), (decay, VM), (inflow, VM), (outflow, VM)],
        scratch=[pltpu.SemaphoreType.DMA],
        out_specs=(VM,) * 5 + (HB,),
    )

    def take_arrived(arrived, lam, low_rows, lo):
        keep = lax.axis_index("blk") > 0
        for b in range(low):
            row = lam[b] + jnp.where(keep, arrived[b].astype(F32), 0.0)
            low_rows[b] = row
            lo[b] = row.astype(BF16)
        lo[low] = jnp.zeros((cases, nodes), BF16)

    def rim_sums(lists, acc_rim, lo, own, other, out, sums):
        sums[...] = acc_rim[...]
        run(lists, [((0, 1), lo, own, sums), ((1, 1), lo, other, sums)], FEW)
        out[...] = sums[...].astype(BF16)

    def rim_body(lists, arrived, lam, acc_rim, own, other, out, low_rows, lo, sums):
        take_arrived(arrived, lam, low_rows, lo)
        rim_sums(lists, acc_rim, lo, own, other, out, sums)

    def start_copies(lists, side, kind, first, count, source, dest, at, sem):
        def one(i, carry):
            c = word_of(lists, side, kind, first + i)
            pltpu.make_async_copy(source.at[c & 255], dest.at[at + i], sem).start()
            return carry

        lax.fori_loop(0, count, one, 0)

    def finish_copies(count, source, dest, sem):
        def one(i, carry):
            pltpu.make_async_copy(source.at[0], dest.at[0], sem).wait()
            return carry

        lax.fori_loop(0, count, one, 0)

    def run_copied(lists, first, count, lam, source, acc, width):
        total = count[0] + count[1]

        def some(i, carry):
            words = []
            for u in range(width):
                j = i * width + u
                is_own = j < count[0]
                at = jnp.where(is_own, first[0] + j, first[1] + j - count[0])
                at = jnp.clip(at, 0, STRIDE - 1)
                word = jnp.where(is_own, word_of(lists, 0, 1, at), word_of(lists, 1, 1, at))
                words.append((jnp.where(j < total, word, low << 8), jnp.minimum(j, total - 1)))
            prods = [
                jnp.dot(lam[(c >> 8) & 255], source[j], preferred_element_type=F32)
                for c, j in words
            ]
            for (c, _), prod in zip(words, prods):
                acc[c >> 16] += prod
            return carry

        lax.fori_loop(0, (total + width - 1) // width, some, 0)

    def rim_last_body(
        lists, arrived, lam, acc_rim, kept, own_in, other_in, out, low_rows, lo, sums, rest, sem
    ):
        count_own = count_of(lists, 0, 1)
        count_other = count_of(lists, 1, 1)
        keep_own = jnp.minimum(count_own, KEEP)
        keep_other = jnp.minimum(count_other, KEEP - keep_own)
        more_own = count_own - keep_own
        more_other = count_other - keep_other
        start_copies(lists, 0, 1, keep_own, more_own, own_in, rest, 0, sem)
        start_copies(lists, 1, 1, keep_other, more_other, other_in, rest, more_own, sem)
        take_arrived(arrived, lam, low_rows, lo)
        sums[...] = acc_rim[...]
        run_copied(lists, (0, 0), (keep_own, keep_other), lo, kept, sums, MANY)
        finish_copies(more_own + more_other, own_in, rest, sem)
        run_copied(
            lists, (keep_own, keep_other), (more_own, more_other), lo, rest, sums, FEW
        )
        out[...] = sums[...].astype(BF16)

    def main_body(
        lists, bus, left, low_rows, lam, lo, hi, acc, icar, own, other,
        hot, hot_next, head0, place, place_next, label_next, decay, inflow,
        lam_low, acc_rim, sent, kept, icar_out, lam_out, hi_out,
        icar_next, lo_base, lam_next, hi_next, sems,
    ):
        keep_own = jnp.minimum(count_of(lists, 0, 1), KEEP)
        keep_other = jnp.minimum(count_of(lists, 1, 1), KEEP - keep_own)
        for b in range(blocks):
            row = low_rows[b] if b < low else lam[b]
            icar_next[b] = decay[b : b + 1, :] * icar[b] + inflow[b : b + 1, :] * row
        icar_copy = pltpu.make_async_copy(icar_next, icar_out, sems.at[0])
        icar_copy.start()
        lam_next[...] = acc[...]
        run(lists, [((0, 3), lo, own, lam_next), ((1, 3), lo, other, lam_next)], MANY)
        upper = pl.ds(low, blocks - low)
        lam_copy = pltpu.make_async_copy(lam_next.at[upper], lam_out, sems.at[1])
        lam_copy.start()
        for b in range(low):
            lam_low[b] = lam_next[b]
            lo_base[b] = lam_next[b].astype(BF16)
        for b in range(low, blocks):
            hi_next[b - low] = lam_next[b].astype(BF16)
        hi_next[blocks - low] = jnp.zeros((cases, nodes), BF16)
        hi_copy = pltpu.make_async_copy(hi_next, hi_out, sems.at[2])
        hi_copy.start()
        acc_rim[...] = jnp.zeros(acc_rim.shape, F32)
        run(lists, [((0, 0), hi_next, own, acc_rim), ((1, 0), hi_next, other, acc_rim)], FEW)
        head_next = jnp.dot(left[0], hot_next[0], preferred_element_type=F32)
        for b in range(1, low):
            head_next += jnp.dot(left[b], hot_next[b], preferred_element_type=F32)
        width = (nodes - cases, heads)
        label = jnp.broadcast_to((bus[...] + 1).astype(F32), width).astype(BF16)
        pairs = [
            (place, head0[...], head_values(lo, hi, hot)),
            (place, head_values(lo_base, hi_next, hot), label),
            (place_next, head_next.astype(BF16), label_next[...]),
        ]
        for i, (where, first_half, second_half) in enumerate(pairs):
            part = lax.dot_general(
                where[...],
                jnp.concatenate([first_half, second_half], axis=0),
                (((1,), (1,)), ((), ())),
                preferred_element_type=F32,
            )
            sent[:, i] = part.astype(BF16).reshape(network, slots, nodes)

        def keep_own_block(i, carry):
            kept[i] = own[word_of(lists, 0, 1, i) & 255]
            return carry

        def keep_other_block(i, carry):
            kept[keep_own + i] = other[word_of(lists, 1, 1, i) & 255]
            return carry

        lax.fori_loop(0, keep_own, keep_own_block, 0)
        lax.fori_loop(0, keep_other, keep_other_block, 0)
        icar_copy.wait()
        lam_copy.wait()
        hi_copy.wait()

    tiles = [(own, VM), (other, VM)]
    rim_type = array((rim, cases, nodes), BF16)
    low_type = array(half, F32)
    sums = pltpu.VMEM((rim, cases, nodes), F32)
    assert STEPS == 3
    hi = hi_next
    leaving, low_rows, lo = kernel(
        with_lists(rim_body),
        (rim_type, low_type, array(padded, BF16)),
        listed + [(arriving, VM), (lam, VM), (acc_rim, VM)] + tiles,
        scratch=[sums],
    )
    arriving = lax.ppermute(leaving, "blk", onward)
    lam_low, acc_rim, sent, kept, icar, lam_high, hi_next = kernel(
        with_lists(main_body),
        (
            low_type,
            array((rim, cases, nodes), F32),
            array((network, 3, slots, nodes), BF16),
            array((KEEP, nodes, nodes), BF16),
            hbm_array(state, F32),
            hbm_array((blocks - low, cases, nodes), F32),
            hbm_array(padded, BF16),
        ),
        listed
        + [(distribution_entry_substation.reshape(1, heads), VM), (leaving, VM)]
        + [(low_rows, VM), (lam, VM), (lo, VM), (hi, VM), (acc, VM), (icar, VM)]
        + tiles
        + [(hot, VM), (hot_next, VM), (head0, VM), (place, VM), (place_next, VM), (label_next, VM)]
        + [(decay, VM), (inflow, VM)],
        scratch=[
            pltpu.VMEM(state, F32),
            pltpu.VMEM(half, BF16),
            pltpu.VMEM(state, F32),
            pltpu.VMEM(padded, BF16),
            pltpu.SemaphoreType.DMA((3,)),
        ],
        out_specs=(VM,) * 4 + (HB,) * 3,
    )
    received = lax.all_to_all(
        sent.reshape(network, 3 * slots, nodes),
        ("sec", "blk"),
        split_axis=0,
        concat_axis=0,
        tiled=True,
    )
    received = received.reshape(rows_sent, nodes)
    stored_in = [(derivative_tiles, HB), (other_kept, HB)]
    fetched_shape = (2 * stored, nodes, nodes)
    leaving, low_rows, lo = kernel(
        with_lists(rim_last_body),
        (rim_type, low_type, array(padded, BF16)),
        listed + [(arriving, VM), (lam_low, VM), (acc_rim, VM), (kept, VM)] + stored_in,
        scratch=[sums, pltpu.VMEM(fetched_shape, BF16), pltpu.SemaphoreType.DMA],
    )
    arriving = lax.ppermute(leaving, "blk", onward[:-1])

    def main_last_body(
        lists, low_rows, lam_high, lo, hi, decay, inflow, outflow, own, other, icar,
        lam_out, low_next, icar_out, lam_next, icar_next, sems,
    ):
        for b in range(blocks):
            row = low_rows[b] if b < low else lam_high[b - low]
            before = icar[b]
            lam_next[b] = outflow[b : b + 1, :] * before
            icar_next[b] = decay[b : b + 1, :] * before + inflow[b : b + 1, :] * row
        icar_copy = pltpu.make_async_copy(icar_next, icar_out, sems.at[0])
        icar_copy.start()
        run(lists, [((0, 2), hi, own, lam_next), ((1, 2), hi, other, lam_next)], MANY)
        run(lists, [((0, 3), lo, own, lam_next), ((1, 3), lo, other, lam_next)], MANY)
        upper = pl.ds(low, blocks - low)
        lam_copy = pltpu.make_async_copy(lam_next.at[upper], lam_out.at[upper], sems.at[1])
        lam_copy.start()
        low_next[...] = lam_next[:low]
        icar_copy.wait()
        lam_copy.wait()

    lam, low_next, icar = kernel(
        with_lists(main_last_body),
        (hbm_array(state, F32), low_type, hbm_array(state, F32)),
        listed
        + [(low_rows, VM), (lam_high, VM), (lo, VM), (hi_next, VM)]
        + [(decay, VM), (inflow, VM), (outflow, VM)]
        + [(derivative_tiles, VM), (other_kept, VM), (icar, VM)],
        scratch=[
            pltpu.VMEM(state, F32),
            pltpu.VMEM(state, F32),
            pltpu.SemaphoreType.DMA((2,)),
        ],
        out_specs=(HB, VM, HB),
    )

    def trans_body(received, product, matrix, out):
        dims = (((0,), (0,)), ((), ()))
        if slots % 16 == 0:
            parts = received[...].reshape(network, 3, slots, nodes)
            part = [parts[:, i].reshape(network * slots, nodes) for i in range(3)]
            column = lax.broadcasted_iota(jnp.int32, (network * slots, buses), 1)

            def hot_of(rows):
                label = rows[:, cases : cases + 1].astype(F32).astype(jnp.int32) - 1
                return jnp.where(label == column, 1.0, 0.0).astype(BF16)

            hot = hot_of(part[1])
            first = lax.dot_general(part[0], hot, dims, preferred_element_type=F32)
            last = lax.dot_general(part[1], hot, dims, preferred_element_type=F32)
            last += lax.dot_general(part[2], hot_of(part[2]), dims, preferred_element_type=F32)
        else:
            got = received[...].astype(F32)
            row = lax.broadcasted_iota(jnp.int32, (rows_sent, buses), 0)
            place = lax.rem(row, 3 * slots)
            column = lax.broadcasted_iota(jnp.int32, (rows_sent, buses), 1)
            label = got[:, cases : cases + 1].astype(jnp.int32) - 1
            hot = jnp.where(jnp.logical_and(label == column, place >= slots), 1.0, 0.0)
            own_hot = jnp.where(place < 2 * slots, hot, 0.0)
            hot_a = pltpu.roll(own_hot, rows_sent - slots, 0).astype(BF16)
            first = lax.dot_general(received[...], hot_a, dims, preferred_element_type=F32)
            last = lax.dot_general(
                received[...], hot.astype(BF16), dims, preferred_element_type=F32
            )
        value = product[...] + first[:cases]
        for inj in (first[cases:], last[:cases]):
            value = jnp.dot(value.astype(BF16), matrix[...], preferred_element_type=F32) + inj
        out[...] = value

    (trans,) = kernel(
        trans_body,
        (array(highvoltage_costate.shape, F32),),
        [(received, VM), (product, VM), (highvoltage_derivative_matrix, VM)],
    )

    def last_body(arrived, low_next, lam_in, lam_out, rows, sems):
        del lam_in
        keep = lax.axis_index("blk") > 0
        copies = []
        part = low // 4
        for i in range(4):
            for b in range(i * part, (i + 1) * part):
                rows[b] = low_next[b] + jnp.where(keep, arrived[b].astype(F32), 0.0)
            here = pl.ds(i * part, part)
            copies.append(pltpu.make_async_copy(rows.at[here], lam_out.at[here], sems.at[i]))
            copies[-1].start()
        for copy in copies:
            copy.wait()

    (lam,) = kernel(
        last_body,
        (array(state, F32),),
        [(arriving, VM), (low_next, VM), (lam, HB)],
        scratch=[pltpu.VMEM(half, F32), pltpu.SemaphoreType.DMA((4,))],
        out_specs=(HB,),
        aliases={2: 0},
    )
    return (lam, icar, trans)


def solution(mesh):
    placed = (
        P(("sec", "blk"), "case", None),
        P(("sec", "blk"), "case", None),
        P("case", ("sec", "blk")),
        P(("sec", "blk", "case"), None, None),
        P(("sec", "blk", "case")),
        P(("sec", "blk", "case")),
        P(("sec", "blk"), None),
        P(("sec", "blk"), None),
        P(("sec", "blk"), None),
        P(("sec", "blk")),
        P(("sec", "blk"), None),
        P(("sec", "blk")),
        P(("sec", "blk"), None),
    )

    return jax.shard_map(
        local,
        mesh=mesh,
        in_specs=placed,
        out_specs=(
            P(("sec", "blk"), "case", None),
            P(("sec", "blk"), "case", None),
            P("case", ("sec", "blk")),
        ),
        check_vma=False,
    )
```

```python
import jax
import jax.numpy as jnp
from jax import lax
from jax.experimental import pallas as pl
from jax.experimental.pallas import tpu as pltpu
from jax.sharding import PartitionSpec as P


STEPS = 3
UNROLL = 16
FEW = 24
MANY = 40
KEEP = 44
CLASSES = 4
VMEM_LIMIT = 24 << 20

F32 = jnp.float32
BF16 = jnp.bfloat16
VM = pl.BlockSpec(memory_space=pltpu.VMEM)
SM = pl.BlockSpec(memory_space=pltpu.SMEM)
HB = pl.BlockSpec(memory_space=pltpu.HBM)
STRIDE = 128


def kernel(body, outs, ins, scratch=(), out_specs=None, aliases=None):
    return pl.pallas_call(
        body,
        out_shape=outs,
        in_specs=[spec for _, spec in ins],
        out_specs=out_specs or tuple(VM for _ in outs),
        scratch_shapes=list(scratch),
        input_output_aliases=aliases or {},
        compiler_params=pltpu.CompilerParams(vmem_limit_bytes=VMEM_LIMIT),
    )(*[in_hbm(array) if spec is HB else array for array, spec in ins])


def with_lists(body):
    return lambda own, other, *refs: body((own, other), *refs)


def in_hbm(array):
    return pltpu.with_memory_space_constraint(array, pltpu.HBM)


def array(shape, dtype):
    return jax.ShapeDtypeStruct(shape, dtype)


def hbm_array(shape, dtype):
    return pltpu.HBM(shape, dtype)


def local(
    vertex_costate,
    inverter_costate,
    highvoltage_costate,
    derivative_tiles,
    tile_source_index,
    tile_target_index,
    inverter_decay_factor,
    costate_to_inverter_factor,
    inverter_to_costate_factor,
    distribution_entry_vertex,
    distribution_entry_holder,
    distribution_entry_substation,
    highvoltage_derivative_matrix,
):
    blocks, cases, nodes = vertex_costate.shape
    rim = blocks // 2
    low = blocks // 2
    targets = blocks + rim
    stored = derivative_tiles.shape[0]
    sections = lax.axis_size("sec")
    owners = lax.axis_size("blk")
    network = sections * owners
    heads = distribution_entry_vertex.shape[0]
    slots = max(2, 2 * heads // network)
    buses = highvoltage_derivative_matrix.shape[1]
    rows_sent = network * 3 * slots
    assert -(-stored // MANY) * MANY <= STRIDE and -(-stored // FEW) * FEW <= STRIDE

    state = (blocks, cases, nodes)
    half = (low, cases, nodes)
    padded = (low + 1, cases, nodes)
    acc_shape = (targets, cases, nodes)
    hot_shape = (blocks, nodes, heads)
    swap = [(0, 1), (1, 0)]
    onward = [(i, (i + 1) % owners) for i in range(owners)]
    backward = [(j, i) for i, j in onward]

    own = derivative_tiles
    other_rows = lax.ppermute(tile_source_index, "case", swap)
    other_columns = lax.ppermute(tile_target_index, "case", swap)
    other = lax.ppermute(own, "case", swap)

    def sorted_list(rows, columns):
        is_low = jnp.where(rows < low, 1, 0)
        is_own = jnp.where(columns < blocks, 1, 0)
        kind = 2 * is_own + is_low
        place = lax.broadcasted_iota(jnp.int32, (1, stored), 1)
        word = place | ((rows - low * (1 - is_low)) << 8) | ((columns - blocks * (1 - is_own)) << 16)
        kind_row = jnp.broadcast_to(kind.astype(F32), (stored, stored))
        word_row = jnp.broadcast_to(word.astype(F32), (stored, stored))
        earlier = lax.broadcasted_iota(jnp.int32, (stored, stored), 0) > lax.broadcasted_iota(
            jnp.int32, (stored, stored), 1
        )
        kind_col = kind_row.T
        same = jnp.logical_and(kind_col == kind_row, earlier)
        rank = jnp.sum(jnp.where(same, 1.0, 0.0), axis=1, keepdims=True)
        spot = (kind_col[:, :1] * STRIDE + rank).astype(jnp.int32)
        hit = lax.broadcasted_iota(jnp.int32, (stored, CLASSES * STRIDE), 1) == spot
        words = jnp.sum(jnp.where(hit, word_row.T[:, :1], 0.0), axis=0, keepdims=True)
        taken = jnp.sum(jnp.where(hit, 1.0, 0.0), axis=0, keepdims=True)
        idle = jnp.full((1, CLASSES * STRIDE), low << 8, jnp.int32)
        lane = lax.broadcasted_iota(jnp.int32, (stored, 128), 1).astype(F32)
        counts = jnp.sum(jnp.where(kind_col[:, :1] == lane, 1.0, 0.0), axis=0, keepdims=True)
        return jnp.concatenate(
            [jnp.where(taken > 0, words.astype(jnp.int32), idle), counts.astype(jnp.int32)], axis=1
        )

    def word_of(lists, side, kind, i):
        return lists[side][0, kind * STRIDE + i]

    def count_of(lists, side, kind):
        return lists[side][0, CLASSES * STRIDE + kind]

    list_type = array((1, CLASSES * STRIDE + 128), jnp.int32)

    def run(lists, parts, width):
        def some(i, carry):
            words = [
                (word_of(lists, side, kind, i * width + u), lam, tiles, acc)
                for (side, kind), lam, tiles, acc in parts
                for u in range(width)
            ]
            prods = [
                jnp.dot(lam[(c >> 8) & 255], tiles[c & 255], preferred_element_type=F32)
                for c, lam, tiles, _ in words
            ]
            for (c, _, _, acc), prod in zip(words, prods):
                acc[c >> 16] += prod
            return carry

        longest = 0
        for (side, kind), _, _, _ in parts:
            longest = jnp.maximum(longest, count_of(lists, side, kind))
        lax.fori_loop(0, (longest + width - 1) // width, some, 0)

    def first_body(
        rows, columns, rows_in, columns_in, lam_in, own_in, acc, lo, hi, own_kept, listed,
        lam, lam_bf, rows_kept, columns_kept, sems,
    ):
        chunks = stored // UNROLL
        early = [
            pltpu.make_async_copy(rows_in, rows_kept, sems.at[chunks]),
            pltpu.make_async_copy(columns_in, columns_kept, sems.at[chunks + 1]),
            pltpu.make_async_copy(lam_in, lam, sems.at[chunks + 2]),
        ]
        copies = [
            pltpu.make_async_copy(
                own_in.at[pl.ds(i * UNROLL, UNROLL)], own_kept.at[pl.ds(i * UNROLL, UNROLL)], sems.at[i]
            )
            for i in range(chunks)
        ]
        for copy in early + copies:
            copy.start()
        for b in range(targets):
            acc[b] = jnp.zeros((cases, nodes), F32)
        zero = jnp.zeros((cases, nodes), BF16)
        lo[low] = zero
        hi[blocks - low] = zero
        early[0].wait()
        early[1].wait()
        listed[...] = sorted_list(rows_kept[...], columns_kept[...])
        early[2].wait()
        for b in range(blocks):
            rounded = lam[b].astype(BF16)
            lam_bf[b] = rounded
            if b < low:
                lo[b] = rounded
            else:
                hi[b - low] = rounded
        for i, copy in enumerate(copies):
            copy.wait()
            prods = [
                jnp.dot(
                    lam_bf[rows[i * UNROLL + u]],
                    own_kept[i * UNROLL + u],
                    preferred_element_type=F32,
                )
                for u in range(UNROLL)
            ]
            for u, prod in enumerate(prods):
                acc[columns[i * UNROLL + u]] += prod

    acc, lo, hi, own, own_list = kernel(
        first_body,
        (
            array(acc_shape, F32),
            array(padded, BF16),
            array(padded, BF16),
            array(own.shape, BF16),
            list_type,
        ),
        [
            (tile_source_index, SM),
            (tile_target_index, SM),
            (tile_source_index.reshape(1, stored), HB),
            (tile_target_index.reshape(1, stored), HB),
            (vertex_costate, HB),
            (own, HB),
        ],
        scratch=[
            pltpu.VMEM(state, F32),
            pltpu.VMEM(state, BF16),
            pltpu.VMEM((1, stored), jnp.int32),
            pltpu.VMEM((1, stored), jnp.int32),
            pltpu.SemaphoreType.DMA((stored // UNROLL + 3,)),
        ],
    )

    def sort_body(rows, columns, listed):
        listed[...] = sorted_list(rows[...], columns[...])

    (other_list,) = kernel(
        sort_body,
        (list_type,),
        [(other_rows.reshape(1, stored), VM), (other_columns.reshape(1, stored), VM)],
    )
    listed = [(own_list, SM), (other_list, SM)]

    def head_values(lo, hi, hot):
        total = jnp.dot(lo[0], hot[0], preferred_element_type=F32)
        for b in range(1, blocks):
            row = lo[b] if b < low else hi[b - low]
            total += jnp.dot(row, hot[b], preferred_element_type=F32)
        return total.astype(BF16)

    def rows_of(owner):
        names = jnp.broadcast_to(owner.astype(F32), (heads, heads))
        before = lax.broadcasted_iota(jnp.int32, (heads, heads), 0)
        after = lax.broadcasted_iota(jnp.int32, (heads, heads), 1)
        same = jnp.logical_and(names.T == names, before < after)
        slot = jnp.sum(jnp.where(same, 1.0, 0.0), axis=0, keepdims=True).astype(jnp.int32)
        return owner * slots + slot

    def one_hots(vertex, count, out):
        node = lax.broadcasted_iota(jnp.int32, (nodes, heads), 0)
        for b in range(count):
            out[b] = jnp.where(node + b * nodes == vertex, 1.0, 0.0).astype(BF16)

    def place_rows(owner, keep, out):
        row = lax.broadcasted_iota(jnp.int32, (network * slots, heads), 0)
        out[...] = jnp.where(row == jnp.where(keep, rows_of(owner), -1), 1.0, 0.0).astype(BF16)

    place_type = array((network * slots, heads), BF16)

    def prepare_body(vertex, owner, lo, hi, trans, matrix, hot, head, place, product):
        one_hots(vertex[...], blocks, hot)
        head[...] = head_values(lo, hi, hot)
        place_rows(owner[...], True, place)
        product[...] = jnp.dot(
            trans[...].astype(BF16), matrix[...], preferred_element_type=F32
        )

    own_owner = distribution_entry_holder.reshape(1, heads)
    hot, head0, place, product = kernel(
        prepare_body,
        (
            array(hot_shape, BF16),
            array((cases, heads), BF16),
            place_type,
            hbm_array(highvoltage_costate.shape, F32),
        ),
        [(distribution_entry_vertex.reshape(1, heads), VM), (own_owner, VM), (lo, VM), (hi, VM)]
        + [(highvoltage_costate, VM), (highvoltage_derivative_matrix, VM)],
    )

    def rim_first_body(lists, acc, lo, hi, other, out, sums):
        sums[...] = acc[blocks:]
        run(
            lists,
            [((1, 0), hi, other, sums), ((1, 1), lo, other, sums)],
            FEW,
        )
        out[...] = sums[...].astype(BF16)

    (leaving,) = kernel(
        with_lists(rim_first_body),
        (array((rim, cases, nodes), BF16),),
        listed + [(acc, VM), (lo, VM), (hi, VM), (other, VM)],
        scratch=[pltpu.VMEM((rim, cases, nodes), F32)],
    )
    arriving = lax.ppermute(leaving, "blk", onward)

    mine = jnp.concatenate(
        [
            distribution_entry_vertex.reshape(1, heads),
            own_owner,
            distribution_entry_substation.reshape(1, heads),
        ],
        axis=1,
    )
    theirs = lax.ppermute(mine, "blk", backward)

    def prepare_next_body(theirs, hot, place, label):
        one_hots(theirs[:, :heads], low, hot)
        followed = lax.axis_index("blk") < owners - 1
        place_rows(theirs[:, heads : 2 * heads], followed, place)
        bus = (theirs[:, 2 * heads : 3 * heads] + 1).astype(F32)
        label[...] = jnp.broadcast_to(bus, (nodes - cases, heads)).astype(BF16)

    hot_next, place_next, label_next = kernel(
        prepare_next_body,
        (array((low, nodes, heads), BF16), place_type, array((nodes - cases, heads), BF16)),
        [(theirs, VM)],
    )

    def begin_next(lists, lam, icar, outflow, own, other, acc, acc_rim, hi):
        for b in range(blocks):
            acc[b] = outflow[b : b + 1, :] * icar[b]
        for b in range(rim):
            acc_rim[b] = jnp.zeros((cases, nodes), F32)
        for b in range(low, blocks):
            hi[b - low] = lam[b].astype(BF16)
        hi[blocks - low] = jnp.zeros((cases, nodes), BF16)
        run(lists, [((0, 0), hi, own, acc_rim), ((1, 0), hi, other, acc_rim)], FEW)
        run(lists, [((0, 2), hi, own, acc), ((1, 2), hi, other, acc)], MANY)

    def main_first_body(
        lists, acc, lo, hi, own, other, lam, icar, decay, inflow, outflow,
        lam_next, acc_next, acc_rim, hi_next, icar_next, other_kept, sem,
    ):
        kept = pltpu.make_async_copy(other, other_kept, sem)
        kept.start()
        for b in range(blocks):
            lam_next[b] = acc[b] + outflow[b : b + 1, :] * icar[b]
            icar_next[b] = decay[b : b + 1, :] * icar[b] + inflow[b : b + 1, :] * lam[b]
        run(lists, [((1, 2), hi, other, lam_next), ((1, 3), lo, other, lam_next)], MANY)
        begin_next(
            lists, lam_next, icar_next, outflow, own, other, acc_next, acc_rim, hi_next
        )
        kept.wait()

    decay, inflow, outflow = (
        inverter_decay_factor, costate_to_inverter_factor, inverter_to_costate_factor
    )
    lam, acc, acc_rim, hi_next, icar, other_kept = kernel(
        with_lists(main_first_body),
        (
            array(state, F32),
            array(state, F32),
            array((rim, cases, nodes), F32),
            array(padded, BF16),
            array(state, F32),
            hbm_array(other.shape, BF16),
        ),
        listed
        + [(acc, VM), (lo, VM), (hi, VM), (own, VM), (other, VM)]
        + [(vertex_costate, VM), (inverter_costate, VM), (decay, VM), (inflow, VM), (outflow, VM)],
        scratch=[pltpu.SemaphoreType.DMA],
        out_specs=(VM,) * 5 + (HB,),
    )

    def take_arrived(arrived, lam, low_rows, lo):
        keep = lax.axis_index("blk") > 0
        for b in range(low):
            row = lam[b] + jnp.where(keep, arrived[b].astype(F32), 0.0)
            low_rows[b] = row
            lo[b] = row.astype(BF16)
        lo[low] = jnp.zeros((cases, nodes), BF16)

    def rim_sums(lists, acc_rim, lo, own, other, out, sums):
        sums[...] = acc_rim[...]
        run(lists, [((0, 1), lo, own, sums), ((1, 1), lo, other, sums)], FEW)
        out[...] = sums[...].astype(BF16)

    def rim_body(lists, arrived, lam, acc_rim, own, other, out, low_rows, lo, sums):
        take_arrived(arrived, lam, low_rows, lo)
        rim_sums(lists, acc_rim, lo, own, other, out, sums)

    def start_copies(lists, side, kind, first, count, source, dest, at, sem):
        def one(i, carry):
            c = word_of(lists, side, kind, first + i)
            pltpu.make_async_copy(source.at[c & 255], dest.at[at + i], sem).start()
            return carry

        lax.fori_loop(0, count, one, 0)

    def finish_copies(count, source, dest, sem):
        def one(i, carry):
            pltpu.make_async_copy(source.at[0], dest.at[0], sem).wait()
            return carry

        lax.fori_loop(0, count, one, 0)

    def run_copied(lists, first, count, lam, source, acc, width):
        total = count[0] + count[1]

        def some(i, carry):
            words = []
            for u in range(width):
                j = i * width + u
                is_own = j < count[0]
                at = jnp.where(is_own, first[0] + j, first[1] + j - count[0])
                at = jnp.clip(at, 0, STRIDE - 1)
                word = jnp.where(is_own, word_of(lists, 0, 1, at), word_of(lists, 1, 1, at))
                words.append((jnp.where(j < total, word, low << 8), jnp.minimum(j, total - 1)))
            prods = [
                jnp.dot(lam[(c >> 8) & 255], source[j], preferred_element_type=F32)
                for c, j in words
            ]
            for (c, _), prod in zip(words, prods):
                acc[c >> 16] += prod
            return carry

        lax.fori_loop(0, (total + width - 1) // width, some, 0)

    def rim_last_body(
        lists, arrived, lam, acc_rim, kept, own_in, other_in, out, low_rows, lo, sums, rest, sem
    ):
        count_own = count_of(lists, 0, 1)
        count_other = count_of(lists, 1, 1)
        keep_own = jnp.minimum(count_own, KEEP)
        keep_other = jnp.minimum(count_other, KEEP - keep_own)
        more_own = count_own - keep_own
        more_other = count_other - keep_other
        start_copies(lists, 0, 1, keep_own, more_own, own_in, rest, 0, sem)
        start_copies(lists, 1, 1, keep_other, more_other, other_in, rest, more_own, sem)
        take_arrived(arrived, lam, low_rows, lo)
        sums[...] = acc_rim[...]
        run_copied(lists, (0, 0), (keep_own, keep_other), lo, kept, sums, MANY)
        finish_copies(more_own + more_other, own_in, rest, sem)
        run_copied(
            lists, (keep_own, keep_other), (more_own, more_other), lo, rest, sums, FEW
        )
        out[...] = sums[...].astype(BF16)

    def main_body(
        lists, bus, left, low_rows, lam, lo, hi, acc, icar, own, other,
        hot, hot_next, head0, place, place_next, label_next, decay, inflow,
        lam_low, acc_rim, sent, kept, icar_out, lam_out, hi_out,
        icar_next, lo_base, lam_next, hi_next, sems,
    ):
        keep_own = jnp.minimum(count_of(lists, 0, 1), KEEP)
        keep_other = jnp.minimum(count_of(lists, 1, 1), KEEP - keep_own)
        for b in range(blocks):
            row = low_rows[b] if b < low else lam[b]
            icar_next[b] = decay[b : b + 1, :] * icar[b] + inflow[b : b + 1, :] * row
        icar_copy = pltpu.make_async_copy(icar_next, icar_out, sems.at[0])
        icar_copy.start()
        lam_next[...] = acc[...]
        run(lists, [((0, 3), lo, own, lam_next), ((1, 3), lo, other, lam_next)], MANY)
        upper = pl.ds(low, blocks - low)
        lam_copy = pltpu.make_async_copy(lam_next.at[upper], lam_out, sems.at[1])
        lam_copy.start()
        for b in range(low):
            lam_low[b] = lam_next[b]
            lo_base[b] = lam_next[b].astype(BF16)
        for b in range(low, blocks):
            hi_next[b - low] = lam_next[b].astype(BF16)
        hi_next[blocks - low] = jnp.zeros((cases, nodes), BF16)
        hi_copy = pltpu.make_async_copy(hi_next, hi_out, sems.at[2])
        hi_copy.start()
        acc_rim[...] = jnp.zeros(acc_rim.shape, F32)
        run(lists, [((0, 0), hi_next, own, acc_rim), ((1, 0), hi_next, other, acc_rim)], FEW)
        head_next = jnp.dot(left[0], hot_next[0], preferred_element_type=F32)
        for b in range(1, low):
            head_next += jnp.dot(left[b], hot_next[b], preferred_element_type=F32)
        width = (nodes - cases, heads)
        label = jnp.broadcast_to((bus[...] + 1).astype(F32), width).astype(BF16)
        pairs = [
            (place, head0[...], head_values(lo, hi, hot)),
            (place, head_values(lo_base, hi_next, hot), label),
            (place_next, head_next.astype(BF16), label_next[...]),
        ]
        for i, (where, first_half, second_half) in enumerate(pairs):
            part = lax.dot_general(
                where[...],
                jnp.concatenate([first_half, second_half], axis=0),
                (((1,), (1,)), ((), ())),
                preferred_element_type=F32,
            )
            sent[:, i] = part.astype(BF16).reshape(network, slots, nodes)

        def keep_own_block(i, carry):
            kept[i] = own[word_of(lists, 0, 1, i) & 255]
            return carry

        def keep_other_block(i, carry):
            kept[keep_own + i] = other[word_of(lists, 1, 1, i) & 255]
            return carry

        lax.fori_loop(0, keep_own, keep_own_block, 0)
        lax.fori_loop(0, keep_other, keep_other_block, 0)
        icar_copy.wait()
        lam_copy.wait()
        hi_copy.wait()

    tiles = [(own, VM), (other, VM)]
    rim_type = array((rim, cases, nodes), BF16)
    low_type = array(half, F32)
    sums = pltpu.VMEM((rim, cases, nodes), F32)
    assert STEPS == 3
    hi = hi_next
    leaving, low_rows, lo = kernel(
        with_lists(rim_body),
        (rim_type, low_type, array(padded, BF16)),
        listed + [(arriving, VM), (lam, VM), (acc_rim, VM)] + tiles,
        scratch=[sums],
    )
    arriving = lax.ppermute(leaving, "blk", onward)
    lam_low, acc_rim, sent, kept, icar, lam_high, hi_next = kernel(
        with_lists(main_body),
        (
            low_type,
            array((rim, cases, nodes), F32),
            array((network, 3, slots, nodes), BF16),
            array((KEEP, nodes, nodes), BF16),
            hbm_array(state, F32),
            hbm_array((blocks - low, cases, nodes), F32),
            hbm_array(padded, BF16),
        ),
        listed
        + [(distribution_entry_substation.reshape(1, heads), VM), (leaving, VM)]
        + [(low_rows, VM), (lam, VM), (lo, VM), (hi, VM), (acc, VM), (icar, VM)]
        + tiles
        + [(hot, VM), (hot_next, VM), (head0, VM), (place, VM), (place_next, VM), (label_next, VM)]
        + [(decay, VM), (inflow, VM)],
        scratch=[
            pltpu.VMEM(state, F32),
            pltpu.VMEM(half, BF16),
            pltpu.VMEM(state, F32),
            pltpu.VMEM(padded, BF16),
            pltpu.SemaphoreType.DMA((3,)),
        ],
        out_specs=(VM,) * 4 + (HB,) * 3,
    )
    received = lax.all_to_all(
        sent.reshape(network, 3 * slots, nodes),
        ("sec", "blk"),
        split_axis=0,
        concat_axis=0,
        tiled=True,
    )
    received = received.reshape(rows_sent, nodes)
    stored_in = [(derivative_tiles, HB), (other_kept, HB)]
    fetched_shape = (2 * stored, nodes, nodes)
    leaving, low_rows, lo = kernel(
        with_lists(rim_last_body),
        (rim_type, low_type, array(padded, BF16)),
        listed + [(arriving, VM), (lam_low, VM), (acc_rim, VM), (kept, VM)] + stored_in,
        scratch=[sums, pltpu.VMEM(fetched_shape, BF16), pltpu.SemaphoreType.DMA],
    )
    arriving = lax.ppermute(leaving, "blk", onward[:-1])

    def main_last_body(
        lists, low_rows, lam_high, lo, hi, decay, inflow, outflow, own, other, icar,
        lam_out, low_next, icar_out, lam_next, icar_next, sems,
    ):
        for b in range(blocks):
            row = low_rows[b] if b < low else lam_high[b - low]
            before = icar[b]
            lam_next[b] = outflow[b : b + 1, :] * before
            icar_next[b] = decay[b : b + 1, :] * before + inflow[b : b + 1, :] * row
        icar_copy = pltpu.make_async_copy(icar_next, icar_out, sems.at[0])
        icar_copy.start()
        run(lists, [((0, 2), hi, own, lam_next), ((1, 2), hi, other, lam_next)], MANY)
        run(lists, [((0, 3), lo, own, lam_next), ((1, 3), lo, other, lam_next)], MANY)
        upper = pl.ds(low, blocks - low)
        lam_copy = pltpu.make_async_copy(lam_next.at[upper], lam_out.at[upper], sems.at[1])
        lam_copy.start()
        low_next[...] = lam_next[:low]
        icar_copy.wait()
        lam_copy.wait()

    lam, low_next, icar = kernel(
        with_lists(main_last_body),
        (hbm_array(state, F32), low_type, hbm_array(state, F32)),
        listed
        + [(low_rows, VM), (lam_high, VM), (lo, VM), (hi_next, VM)]
        + [(decay, VM), (inflow, VM), (outflow, VM)]
        + [(derivative_tiles, VM), (other_kept, VM), (icar, VM)],
        scratch=[
            pltpu.VMEM(state, F32),
            pltpu.VMEM(state, F32),
            pltpu.SemaphoreType.DMA((2,)),
        ],
        out_specs=(HB, VM, HB),
    )

    def trans_body(received, product, matrix, out):
        dims = (((0,), (0,)), ((), ()))
        if slots % 16 == 0:
            parts = received[...].reshape(network, 3, slots, nodes)
            part = [parts[:, i].reshape(network * slots, nodes) for i in range(3)]
            column = lax.broadcasted_iota(jnp.int32, (network * slots, buses), 1)

            def hot_of(rows):
                label = rows[:, cases : cases + 1].astype(F32).astype(jnp.int32) - 1
                return jnp.where(label == column, 1.0, 0.0).astype(BF16)

            hot = hot_of(part[1])
            first = lax.dot_general(part[0], hot, dims, preferred_element_type=F32)
            last = lax.dot_general(part[1], hot, dims, preferred_element_type=F32)
            last += lax.dot_general(part[2], hot_of(part[2]), dims, preferred_element_type=F32)
        else:
            got = received[...].astype(F32)
            row = lax.broadcasted_iota(jnp.int32, (rows_sent, buses), 0)
            place = lax.rem(row, 3 * slots)
            column = lax.broadcasted_iota(jnp.int32, (rows_sent, buses), 1)
            label = got[:, cases : cases + 1].astype(jnp.int32) - 1
            hot = jnp.where(jnp.logical_and(label == column, place >= slots), 1.0, 0.0)
            own_hot = jnp.where(place < 2 * slots, hot, 0.0)
            hot_a = pltpu.roll(own_hot, rows_sent - slots, 0).astype(BF16)
            first = lax.dot_general(received[...], hot_a, dims, preferred_element_type=F32)
            last = lax.dot_general(
                received[...], hot.astype(BF16), dims, preferred_element_type=F32
            )
        value = product[...] + first[:cases]
        for inj in (first[cases:], last[:cases]):
            value = jnp.dot(value.astype(BF16), matrix[...], preferred_element_type=F32) + inj
        out[...] = value

    (trans,) = kernel(
        trans_body,
        (array(highvoltage_costate.shape, F32),),
        [(received, VM), (product, VM), (highvoltage_derivative_matrix, VM)],
    )

    def last_body(arrived, low_next, lam_in, lam_out, rows, sems):
        del lam_in
        keep = lax.axis_index("blk") > 0
        copies = []
        part = low // 4
        for i in range(4):
            for b in range(i * part, (i + 1) * part):
                rows[b] = low_next[b] + jnp.where(keep, arrived[b].astype(F32), 0.0)
            here = pl.ds(i * part, part)
            copies.append(pltpu.make_async_copy(rows.at[here], lam_out.at[here], sems.at[i]))
            copies[-1].start()
        for copy in copies:
            copy.wait()

    (lam,) = kernel(
        last_body,
        (array(state, F32),),
        [(arriving, VM), (low_next, VM), (lam, HB)],
        scratch=[pltpu.VMEM(half, F32), pltpu.SemaphoreType.DMA((4,))],
        out_specs=(HB,),
        aliases={2: 0},
    )
    return (lam, icar, trans)


def solution(mesh):
    placed = (
        P(("sec", "blk"), "case", None),
        P(("sec", "blk"), "case", None),
        P("case", ("sec", "blk")),
        P(("sec", "blk", "case"), None, None),
        P(("sec", "blk", "case")),
        P(("sec", "blk", "case")),
        P(("sec", "blk"), None),
        P(("sec", "blk"), None),
        P(("sec", "blk"), None),
        P(("sec", "blk")),
        P(("sec", "blk"), None),
        P(("sec", "blk")),
        P(("sec", "blk"), None),
    )

    return jax.shard_map(
        local,
        mesh=mesh,
        in_specs=placed,
        out_specs=(
            P(("sec", "blk"), "case", None),
            P(("sec", "blk"), "case", None),
            P("case", ("sec", "blk")),
        ),
        check_vma=False,
    )
```
